32 devices in a mesh: seq: 4 (over x, core), fsdp: 8 (over z, y).
Axes of the slice: x: 2, y: 2, z: 4, core: 2. Of those that a mesh axis runs over, the one named last changes fastest.
Arguments:
- hidden: float32 [8, 512, 768], P('fsdp', 'seq'), may hold values from -6 to 6
- cotangent: float32 [8, 512, 768], P('fsdp', 'seq'), may hold values from -6 to 6
- segments: int32 [8, 512], P('fsdp'), may hold values from 0 to 2, never falling along the last dimension, each value on 1 to 256 neighbouring positions
- in_weight: bfloat16 [2, 768, 3352], P(None, 'fsdp'), may hold values from -0.21875 to 0.21875
- out_weight: bfloat16 [2, 1536, 768], P(None, 'fsdp'), may hold values from -0.15625 to 0.15625
- conv_weight: bfloat16 [2, 4, 1792], P(None, None, 'fsdp'), may hold values from -3 to 3
- conv_bias: bfloat16 [2, 1792], P(None, 'fsdp'), may hold values from -0.5 to 0.5
- norm_gain: bfloat16 [2, 768], P(None, 'fsdp'), may hold values from 0.099609375 to 1.8984375
- gate_gain: bfloat16 [2, 1536], P(None, 'fsdp'), may hold values from 0.099609375 to 1.8984375
- a_log: float32 [2, 24], replicated, may hold values from -3 to 2.5
- dt_bias: float32 [2, 24], replicated, may hold values from -5 to -1
- d_skip: float32 [2, 24], replicated, may hold values from 0.5 to 2
Outputs:
- hidden_out: float32 [8, 512, 768], P('fsdp', 'seq')
- input_grad: float32 [8, 512, 768], P('fsdp', 'seq')
- grad_in_weight: float32 [2, 768, 3352], P(None, 'fsdp')
- grad_out_weight: float32 [2, 1536, 768], P(None, 'fsdp')
- grad_conv_weight: float32 [2, 4, 1792], P(None, None, 'fsdp')
- grad_conv_bias: float32 [2, 1792], P(None, 'fsdp')
- grad_norm_gain: float32 [2, 768], P(None, 'fsdp')
- grad_gate_gain: float32 [2, 1536], P(None, 'fsdp')
- grad_a_log: float32 [2, 24], replicated
- grad_dt_bias: float32 [2, 24], replicated
- grad_d_skip: float32 [2, 24], replicated
The draws below stay inside these ranges and needn't reach their ends.
Inputs may be any that keep to these rules, and one draw needn't show every extreme that they name: `segments`: in each sequence the ids never fall and start at 0; each id covers 1 to 256 positions, one exactly 256.
All inputs are finite; a program needn't handle non-finite values.
Results may differ from the reference program's by a relative error of at most 0.015.
Values may be sent and summed in bfloat16 or wider, within the bound.
A program may use at most 192 MiB of HBM per device.

```python
import math
from functools import partial
import jax
import jax.numpy as jnp
import numpy as np
from jax import lax

D = 768
HEADS = 24
NSTATE = 128
KCONV = 4
SPAN = 256
LAYERS = 2
E = 1536
CONVDIM = 1792
PROJ = 3352
LEN = 512
SEQS = 8


def level_of(rng, extent, cuts, smallest, high):
    factor_of = 1.0
    for dim, shards_of in cuts:
        draws = jax.random.uniform(jax.random.fold_in(jax.random.fold_in(rng, 6), dim), (shards_of,), jnp.float32, smallest / len(cuts), high / len(cuts))
        factor_of = factor_of * jnp.repeat(jnp.exp(draws), extent[dim] // shards_of).reshape((-1,) + (1,) * (len(extent) - 1 - dim))
    return factor_of


def length_profile(amount, total, most, skew):
    loads = [(1 << 20) // math.isqrt(grade ** skew) + 1 for grade in range(2, amount + 1)]
    surplus, holding = total - most - (amount - 1), [1] * (amount - 1)
    while surplus > 0:
        movable = [i for i in range(amount - 1) if holding[i] < most]
        whole, left = sum([loads[i] for i in movable]), surplus
        for i in movable:
            extra = min(most - holding[i], max(1, left * loads[i] // whole), surplus)
            holding[i] = holding[i] + extra
            surplus = surplus - extra
    return np.array([most] + holding)


def ragged_sizes(stream_key, count, total, reach, slope):
    if count == 2:
        one = jax.random.randint(stream_key, (), max(1, total - reach), min(reach, total - 1) + 1)
        return jnp.stack([one, total - one])
    lengths = jnp.asarray(length_profile(count, total, reach, slope), jnp.int32)
    pairs = (count - 1) // 2
    donor, receiver = lengths[1:1 + 2 * pairs:2], lengths[2:2 + 2 * pairs:2]
    margin = jnp.minimum(donor - 1, reach - receiver)
    passed = jax.random.randint(jax.random.fold_in(stream_key, 1), (pairs,), 0, 1 << 20) % (margin + 1)
    lengths = lengths.at[1:1 + 2 * pairs:2].set(donor - passed).at[2:2 + 2 * pairs:2].set(receiver + passed)
    return lengths[jax.random.permutation(jax.random.fold_in(stream_key, 2), count)]


def scatter_about(rng, shape, deviation, reach, shards=(), kind=jnp.bfloat16):
    result = jax.random.normal(rng, shape, jnp.float32) * deviation
    if len(shards) > 0:
        result = level_of(rng, shape, shards, -0.22, 0.18) * result
    return jnp.clip(result, min=-reach, max=reach).astype(kind)


def setup_inputs(seed: int = 0) -> dict:
    streams_of = jax.random.split(jax.random.key(seed), 13)
    hidden = scatter_about(streams_of[0], (SEQS, LEN, D), 1.0, 6.0, ((0, 8), (1, 4)), jnp.float32)
    cotangent = scatter_about(streams_of[1], (SEQS, LEN, D), 1.0, 6.0, ((0, 8), (1, 4)), jnp.float32)
    segments = jax.vmap(lambda own: jnp.searchsorted(jnp.cumsum(ragged_sizes(own, 3, LEN, LEN // 2, 2)), jnp.arange(LEN), side="right"))(jax.random.split(streams_of[2], SEQS)).reshape((SEQS, LEN)).astype(jnp.int32)
    in_weight = scatter_about(streams_of[3], (LAYERS, D, PROJ), D ** -0.5, 0.21875, ((1, 8),))
    out_weight = scatter_about(streams_of[4], (LAYERS, E, D), E ** -0.5, 0.15625, ((1, 8),))
    conv_weight = scatter_about(streams_of[5], (LAYERS, KCONV, CONVDIM), KCONV ** -0.5, 3.0, ((2, 8),))
    conv_bias = jnp.clip(jax.random.uniform(streams_of[6], (LAYERS, CONVDIM), jnp.float32, -0.5, 0.5) * level_of(streams_of[6], (LAYERS, CONVDIM), ((1, 8),), -0.4, 0.0), -0.5, 0.5).astype(jnp.bfloat16)
    norm_gain = jnp.clip(1.0 + 0.18 * jax.random.normal(streams_of[7], (LAYERS, D), jnp.float32), 0.099609375, 1.8984375).astype(jnp.bfloat16)
    gate_gain = jnp.clip(1.0 + 0.18 * jax.random.normal(streams_of[8], (LAYERS, E), jnp.float32), 0.099609375, 1.8984375).astype(jnp.bfloat16)
    a_log = jnp.clip(jax.random.uniform(streams_of[9], (LAYERS, HEADS), jnp.float32, -3.0, 2.5), -3.0, 2.5)
    dt_bias = jnp.clip(jax.random.uniform(streams_of[10], (LAYERS, HEADS), jnp.float32, -5.0, -1.0), -5.0, -1.0)
    d_skip = jnp.clip(jax.random.uniform(streams_of[11], (LAYERS, HEADS), jnp.float32, 0.5, 2.0), 0.5, 2.0)
    return {"hidden": hidden, "cotangent": cotangent, "segments": segments, "in_weight": in_weight, "out_weight": out_weight, "conv_weight": conv_weight, "conv_bias": conv_bias, "norm_gain": norm_gain, "gate_gain": gate_gain, "a_log": a_log, "dt_bias": dt_bias, "d_skip": d_skip}


EPS = 1e-05
PRECISE = lax.Precision.HIGHEST

def rms_norm(values, gain_vec):
    return values * lax.rsqrt(lax.optimization_barrier(jnp.mean(values * values, axis=-1, keepdims=True)) + EPS) * gain_vec

def gate_part(y_val, z_val, gain_vec):
    return rms_norm(y_val * jax.nn.silu(z_val), gain_vec)

def rounded(values):
    return lax.optimization_barrier(values.astype(jnp.bfloat16)).astype(jnp.float32)

def conv_silu(joined, conv_w, conv_b, segment):
    tap_count = conv_w.shape[0]
    length = joined.shape[0]
    padded = jnp.pad(joined, ((tap_count - 1, 0), (0, 0)))
    seg_pad = jnp.concatenate([jnp.full((tap_count - 1,), -1, dtype=jnp.int32), segment.astype(jnp.int32)])
    summed = jnp.zeros_like(joined) + conv_b[None, :]
    for offset in range(tap_count):
        same_doc = (seg_pad[offset:offset + length] == segment.astype(jnp.int32))[:, None]
        summed = summed + jnp.where(same_doc, padded[offset:offset + length] * conv_w[offset][None, :], 0.0)
    return jax.nn.silu(summed)

def ssd_mixer(x_in, bc_in, dt_in, conv_w, conv_b, a_log_h, dt_bias_h, d_skip_h, segment):
    head_count = dt_in.shape[1]
    inner_width = x_in.shape[1]
    headdim = inner_width // head_count
    nstate = bc_in.shape[1] // 2
    length = x_in.shape[0]
    blocks = length // SPAN
    active = conv_silu(jnp.concatenate([x_in, bc_in], axis=1), conv_w, conv_b, segment)
    x_act = active[:, :inner_width]
    b_act = active[:, inner_width:inner_width + nstate]
    c_act = active[:, inner_width + nstate:]
    delta = jax.nn.softplus(dt_in + dt_bias_h[None, :])
    log_decay = -jnp.exp(a_log_h)[None, :] * delta
    x_scaled = x_act.reshape(length, head_count, headdim) * delta[:, :, None]
    pieces_all = (x_scaled.reshape(blocks, SPAN, head_count, headdim), b_act.reshape(blocks, SPAN, nstate), c_act.reshape(blocks, SPAN, nstate), log_decay.reshape(blocks, SPAN, head_count), segment.astype(jnp.int32).reshape(blocks, SPAN))
    causal = jnp.arange(SPAN)[:, None] >= jnp.arange(SPAN)[None, :]

    def one_block(carried, pieces):
        carry_state, last_seg = carried
        x_block, b_block, c_block, decay_block, seg_block = pieces
        cumulated = jnp.cumsum(decay_block, axis=0).T
        kept_mask = (causal & (seg_block[:, None] == seg_block[None, :]))[None]
        log_gap = cumulated[:, :, None] - cumulated[:, None, :]
        weights = jnp.where(kept_mask, jnp.exp(jnp.where(kept_mask, log_gap, 0.0)), 0.0)
        inner_prod = jnp.einsum('in,jn->ij', c_block, b_block, precision=PRECISE)
        scores = weights * inner_prod[None]
        intra = jnp.einsum('hij,jhp->ihp', scores, x_block, precision=PRECISE)
        carry_in = jnp.where((seg_block == last_seg)[None, :], jnp.exp(cumulated), 0.0)
        inter = jnp.einsum('in,hpn->ihp', c_block, carry_state, precision=PRECISE) * carry_in.T[:, :, None]
        end_seg = seg_block[SPAN - 1]
        end_log = cumulated[:, SPAN - 1]
        tail_decay = jnp.where((seg_block == end_seg)[None, :], jnp.exp(end_log[:, None] - cumulated), 0.0)
        keep_old = jnp.where(end_seg == last_seg, jnp.exp(end_log), 0.0)
        x_tail = x_block * tail_decay.T[:, :, None]
        new_state = carry_state * keep_old[:, None, None] + jnp.einsum('jhp,jn->hpn', x_tail, b_block, precision=PRECISE)
        return ((new_state, end_seg), intra + inter)
    start = (jnp.zeros((head_count, headdim, nstate), jnp.float32), jnp.array(-1, dtype=jnp.int32))
    discard, outputs = lax.scan(one_block, start, pieces_all)
    return outputs.reshape(length, inner_width) + x_act * jnp.repeat(d_skip_h, headdim)[None, :]

def reference(hidden, cotangent, segments, in_weight, out_weight, conv_weight, conv_bias, norm_gain, gate_gain, a_log, dt_bias, d_skip):

    def per_sequence(grads, items):
        hidden_seq, cot_seq, seg_row = items
        saved = []
        current = hidden_seq
        mixer_fn = partial(ssd_mixer, segment=seg_row)
        for layer_idx in range(LAYERS):
            gain_one = norm_gain[layer_idx].astype(jnp.float32)
            normed_in = rms_norm(current, gain_one).astype(jnp.bfloat16)
            projected = jnp.dot(normed_in, in_weight[layer_idx], preferred_element_type=jnp.float32)
            gate_z = projected[:, :E]
            primals = (rounded(projected[:, E:2 * E]), rounded(projected[:, 2 * E:2 * E + 2 * NSTATE]), rounded(projected[:, 2 * E + 2 * NSTATE:]), conv_weight[layer_idx].astype(jnp.float32), conv_bias[layer_idx].astype(jnp.float32), a_log[layer_idx], dt_bias[layer_idx], d_skip[layer_idx])
            y_val = rounded(mixer_fn(*primals))
            gate_one = gate_gain[layer_idx].astype(jnp.float32)
            gated = gate_part(y_val, gate_z, gate_one).astype(jnp.bfloat16)
            saved.append((current, normed_in, gate_z, y_val, primals, gated, gain_one, gate_one))
            current = current + jnp.dot(gated, out_weight[layer_idx], preferred_element_type=jnp.float32)
        grad_now = cot_seq
        grad_list = list(grads)
        for layer_idx in reversed(range(LAYERS)):
            prior, normed_in, gate_z, y_val, primals, gated, gain_one, gate_one = saved[layer_idx]
            grad_b = grad_now.astype(jnp.bfloat16)
            grad_out_w = jnp.dot(gated.T, grad_b, preferred_element_type=jnp.float32)
            d_gated = jnp.dot(grad_b, out_weight[layer_idx].T, preferred_element_type=jnp.float32)
            discard, gate_back = jax.vjp(gate_part, y_val, gate_z, gate_one)
            d_y, d_gate_z, grad_gate = gate_back(d_gated)
            discard, mixer_back = jax.vjp(mixer_fn, *primals)
            d_x, d_bc, d_dt, grad_cw, grad_cb, grad_alog, grad_dtb, grad_dsk = mixer_back(rounded(d_y))
            d_proj = jnp.concatenate([d_gate_z, d_x, d_bc, d_dt], axis=1).astype(jnp.bfloat16)
            grad_in_w = jnp.dot(normed_in.T, d_proj, preferred_element_type=jnp.float32)
            d_normed = jnp.dot(d_proj, in_weight[layer_idx].T, preferred_element_type=jnp.float32)
            discard, norm_back = jax.vjp(rms_norm, prior, gain_one)
            d_hidden, grad_norm = norm_back(d_normed)
            grad_now = grad_now + d_hidden
            terms = (grad_in_w, grad_out_w, grad_cw, grad_cb, grad_norm, grad_gate, grad_alog, grad_dtb, grad_dsk)
            grad_list = [accum.at[layer_idx].add(term) for accum, term in zip(grad_list, terms)]
        return (tuple(grad_list), (current, grad_now))
    start = (jnp.zeros((LAYERS, D, PROJ), jnp.float32), jnp.zeros((LAYERS, E, D), jnp.float32), jnp.zeros((LAYERS, KCONV, CONVDIM), jnp.float32), jnp.zeros((LAYERS, CONVDIM), jnp.float32), jnp.zeros((LAYERS, D), jnp.float32), jnp.zeros((LAYERS, E), jnp.float32), jnp.zeros((LAYERS, HEADS), jnp.float32), jnp.zeros((LAYERS, HEADS), jnp.float32), jnp.zeros((LAYERS, HEADS), jnp.float32))
    grads, results = lax.scan(per_sequence, start, (hidden, cotangent, segments))
    hidden_out, input_grad = results
    return (hidden_out, input_grad, grads[0], grads[1], grads[2], grads[3], grads[4], grads[5], grads[6], grads[7], grads[8])
```

```python
from functools import partial

import jax
import jax.numpy as jnp
from jax import lax
from jax.experimental import pallas as pl
from jax.experimental.pallas import tpu as pltpu
from jax.sharding import PartitionSpec as P

HEADDIM = 64
SPAN = 256
EPS = 1e-05
HIGH = lax.Precision.HIGHEST
BF = jnp.bfloat16
F32 = jnp.float32
MESH = pl.DeviceIdType.MESH
NEGATIVE = -1e30
LANES = 128
VMEM_LIMIT = 56 * 1024 * 1024


def factor(n):
    b = 1
    while (2 * b) * (2 * b) <= n:
        b *= 2
    return n // b, b


def peers_of(axis, n):
    a_n, b_n = factor(n)
    s, f = lax.axis_index("seq"), lax.axis_index("fsdp")
    i = s if axis == "seq" else f
    a, b = i // b_n, i % b_n

    def dev(k):
        return (k, f) if axis == "seq" else (s, k)

    out = []
    for da in range(1, a_n):
        out.append(dev(lax.rem(a + da, a_n) * b_n + b))
    for db in range(1, b_n):
        out.append(dev(a * b_n + lax.rem(b + db, b_n)))
    return out


def barrier(groups, extra=None):
    sem = pltpu.get_barrier_semaphore()
    devices = [d for axis, n in groups for d in peers_of(axis, n)]
    for d in devices:
        pl.semaphore_signal(sem, inc=1, device_id=d, device_id_type=MESH)
    if extra is None:
        pl.semaphore_wait(sem, len(devices))
        return
    source, moved = extra

    @pl.when(moved)
    def _():
        pl.semaphore_signal(sem, inc=1, device_id=source, device_id_type=MESH)

    pl.semaphore_wait(sem, len(devices) + moved.astype(jnp.int32))


class Gather:
    def __init__(self, axis, n, ref, sems):
        self.n = n
        self.a_n, self.b_n = factor(n)
        s, f = lax.axis_index("seq"), lax.axis_index("fsdp")
        i = s if axis == "seq" else f
        self.a, self.b = i // self.b_n, i % self.b_n
        self.dev = (lambda k: (k, f)) if axis == "seq" else (lambda k: (s, k))
        self.ref = ref
        self.send, self.recv = sems

    @staticmethod
    def scratch(n):
        a_n, b_n = factor(n)
        count = a_n * b_n
        return [pltpu.SemaphoreType.DMA((count,)), pltpu.SemaphoreType.DMA((count,))]

    def _first(self, da, sender):
        a = self.a if sender else lax.rem(self.a + self.a_n - da, self.a_n)
        block = a * self.b_n + self.b
        return pltpu.make_async_remote_copy(
            src_ref=self.ref.at[block],
            dst_ref=self.ref.at[block],
            send_sem=self.send.at[da * self.b_n],
            recv_sem=self.recv.at[da * self.b_n],
            device_id=self.dev(lax.rem(self.a + da, self.a_n) * self.b_n + self.b),
            device_id_type=MESH,
        )

    def _second(self, da, db, sender):
        a = lax.rem(self.a + self.a_n - da, self.a_n)
        b = self.b if sender else lax.rem(self.b + self.b_n - db, self.b_n)
        block = a * self.b_n + b
        return pltpu.make_async_remote_copy(
            src_ref=self.ref.at[block],
            dst_ref=self.ref.at[block],
            send_sem=self.send.at[da * self.b_n + db],
            recv_sem=self.recv.at[da * self.b_n + db],
            device_id=self.dev(self.a * self.b_n + lax.rem(self.b + db, self.b_n)),
            device_id_type=MESH,
        )

    def start(self):
        for da in range(1, self.a_n):
            self._first(da, True).start()
        for db in range(1, self.b_n):
            self._second(0, db, True).start()

    def forward(self, da):
        self._first(da, False).wait_recv()
        for db in range(1, self.b_n):
            self._second(da, db, True).start()

    def forwards(self):
        for da in range(1, self.a_n):
            self.forward(da)

    def finish(self):
        for da in range(self.a_n):
            for db in range(1, self.b_n):
                self._second(da, db, False).wait_recv()
        for da in range(1, self.a_n):
            self._first(da, True).wait_send()
        for da in range(self.a_n):
            for db in range(1, self.b_n):
                self._second(da, db, True).wait_send()


class Scatter:
    def __init__(self, axis, n, ref, scratch):
        self.a_n, self.b_n = factor(n)
        s, f = lax.axis_index("seq"), lax.axis_index("fsdp")
        i = s if axis == "seq" else f
        self.a, self.b = i // self.b_n, i % self.b_n
        self.dev = (lambda k: (k, f)) if axis == "seq" else (lambda k: (s, k))
        self.ref = ref
        self.row_in, self.mid, self.col_in, self.send, self.recv, self.send2, self.recv2 = scratch

    @staticmethod
    def scratch(n, shape, dtype=BF):
        a_n, b_n = factor(n)
        sem = pltpu.SemaphoreType.DMA
        return [
            pltpu.VMEM((a_n, b_n - 1) + shape, dtype),
            pltpu.VMEM((a_n,) + shape, dtype),
            pltpu.VMEM((a_n - 1,) + shape, dtype),
            sem((a_n, b_n - 1)),
            sem((a_n, b_n - 1)),
            sem((a_n,)),
            sem((a_n,)),
        ]

    def _row(self, da, db):
        a = lax.rem(self.a + da, self.a_n)
        b = lax.rem(self.b + db, self.b_n)
        return pltpu.make_async_remote_copy(
            src_ref=self.ref.at[a * self.b_n + b],
            dst_ref=self.row_in.at[da, db - 1],
            send_sem=self.send.at[da, db - 1],
            recv_sem=self.recv.at[da, db - 1],
            device_id=self.dev(self.a * self.b_n + b),
            device_id_type=MESH,
        )

    def _col(self, da):
        a = lax.rem(self.a + da, self.a_n)
        return pltpu.make_async_remote_copy(
            src_ref=self.mid.at[da],
            dst_ref=self.col_in.at[da - 1],
            send_sem=self.send2.at[da],
            recv_sem=self.recv2.at[da],
            device_id=self.dev(a * self.b_n + self.b),
            device_id_type=MESH,
        )

    def start(self):
        for da in list(range(1, self.a_n)) + [0]:
            for db in range(1, self.b_n):
                self._row(da, db).start()

    def _sum(self, da):
        a = lax.rem(self.a + da, self.a_n)
        for db in range(1, self.b_n):
            self._row(da, db).wait_recv()
        total = self.ref[a * self.b_n + self.b].astype(F32)
        for db in range(1, self.b_n):
            total = total + self.row_in[da, db - 1].astype(F32)
        return total

    def middle(self):
        for da in range(1, self.a_n):
            self.mid[da] = self._sum(da).astype(self.mid.dtype)
            self._col(da).start()

    def finish(self):
        total = self._sum(0)
        for da in range(1, self.a_n):
            self._col(da).wait_recv()
            total = total + self.col_in[da - 1].astype(F32)
        for da in range(self.a_n):
            for db in range(1, self.b_n):
                self._row(da, db).wait_send()
        for da in range(1, self.a_n):
            self._col(da).wait_send()
        return total


N_SCATTER = 7


def comm_call(kernel, name, collective_id, outs, scratch, args, any_space=False):
    space = pl.ANY if any_space else pltpu.VMEM
    spec = pl.BlockSpec(memory_space=space)
    return pl.pallas_call(
        kernel,
        name=name,
        out_shape=outs,
        in_specs=[spec] * len(args),
        out_specs=[spec] * len(outs),
        scratch_shapes=scratch,
        compiler_params=pltpu.CompilerParams(
            collective_id=collective_id, has_side_effects=True, vmem_limit_bytes=VMEM_LIMIT
        ),
    )(*args)


def local_call(kernel, name, outs, args):
    spec = pl.BlockSpec(memory_space=pltpu.VMEM)
    return pl.pallas_call(
        kernel,
        name=name,
        out_shape=outs,
        in_specs=[spec] * len(args),
        out_specs=[spec] * len(outs),
        compiler_params=pltpu.CompilerParams(vmem_limit_bytes=VMEM_LIMIT),
    )(*args)


def sds(shape, dtype):
    return jax.ShapeDtypeStruct(shape, dtype)


def weights_kernel(S, F, layers, *refs):
    small, win, wout, cot = refs[:4]
    small_all, win_all, wout_all, cot_all = refs[4:8]
    rest = list(refs[8:])
    copies, perm_send, perm_recv = rest[:3]
    sems = rest[3:]
    s, f = lax.axis_index("seq"), lax.axis_index("fsdp")
    flat = f * S + s
    target = (flat // F, flat % F)
    own = s * F + f
    source = (own % S, own // S)
    moved = flat != own
    barrier([("fsdp", F), ("seq", S)], (source, moved))

    gathers = []

    def gather(axis, n, ref):
        k = 2 * len(gathers)
        gathers.append(Gather(axis, n, ref, (sems[k], sems[k + 1])))
        return gathers[-1]

    perm = pltpu.make_async_remote_copy(
        src_ref=wout.at[s],
        dst_ref=wout_all.at[flat % F],
        send_sem=perm_send,
        recv_sem=perm_recv,
        device_id=target,
        device_id_type=MESH,
    )
    stay = pltpu.make_async_copy(wout.at[s], wout_all.at[f], copies.at[2 + layers])

    @pl.when(moved)
    def _():
        perm.start()

    @pl.when(jnp.logical_not(moved))
    def _():
        stay.start()

    locals_ = [
        pltpu.make_async_copy(small, small_all.at[f], copies.at[0]),
        pltpu.make_async_copy(cot, cot_all.at[s], copies.at[1]),
    ]
    for l in range(layers):
        locals_.append(pltpu.make_async_copy(win.at[l], win_all.at[l, f], copies.at[2 + l]))
    for c in locals_:
        c.start()
    g_small = gather("fsdp", F, small_all)
    g_cot = gather("seq", S, cot_all)
    g_in = [gather("fsdp", F, win_all.at[l]) for l in range(layers)]
    g_out = gather("fsdp", F, wout_all)
    locals_[0].wait()
    g_small.start()
    locals_[2].wait()
    g_in[0].start()
    locals_[1].wait()
    g_cot.start()

    @pl.when(moved)
    def _():
        perm.wait_recv()

    @pl.when(jnp.logical_not(moved))
    def _():
        stay.wait()

    g_out.start()
    for l in range(1, layers):
        locals_[2 + l].wait()
        g_in[l].start()
    order = [g_small, g_in[0], g_cot, g_out] + g_in[1:]
    for g in order:
        g.forwards()
    for g in order:
        g.finish()

    @pl.when(moved)
    def _():
        perm.wait_send()


def gather_weights(S, F, small, win, wout, cot):
    layers = win.shape[0]
    scratch = [
        pltpu.SemaphoreType.DMA((layers + 3,)),
        pltpu.SemaphoreType.DMA,
        pltpu.SemaphoreType.DMA,
    ]
    scratch += Gather.scratch(F) + Gather.scratch(S)
    for _ in range(layers + 1):
        scratch += Gather.scratch(F)
    outs = [
        sds((F,) + small.shape, small.dtype),
        sds((layers, F) + win.shape[1:], win.dtype),
        sds((F,) + wout.shape[1:], wout.dtype),
        sds((S,) + cot.shape, cot.dtype),
    ]
    return comm_call(
        partial(weights_kernel, S, F, layers), "weights", 0, outs, scratch,
        (small, win, wout, cot), any_space=True,
    )


def as_row(col):
    t = col.shape[0]
    return jnp.broadcast_to(col, (t, LANES)).T[:8]


def as_col(row):
    t = row.shape[1]
    return jnp.broadcast_to(row, (LANES, t)).T[:, :1]


def norm_of(u, gain):
    return u * lax.rsqrt(jnp.mean(u * u, axis=-1, keepdims=True) + EPS) * gain


def start_kernel(S, u_ref, gain_ref, out_ref, *sems):
    barrier([("seq", S)])
    s = lax.axis_index("seq")
    out_ref[s] = norm_of(u_ref[...], gain_ref[...]).astype(BF)
    g = Gather("seq", S, out_ref, sems)
    g.start()
    g.forwards()
    g.finish()


def turn_kernel(S, inner, last, *refs):
    part, sq, current, aux = refs[:4]
    new_ref, delta_ref, inv_ref, gat_ref = refs[4:8]
    rest = list(refs[8:])
    sq_all = rest[0]
    sems_sq, sems_out = rest[1:3], rest[3:5]
    sc = Scatter("seq", S, part, rest[5 : 5 + N_SCATTER])
    barrier([("seq", S)])
    s = lax.axis_index("seq")
    sc.start()
    sq_all[s] = sq[...]
    g_sq = Gather("seq", S, sq_all, sems_sq)
    g_sq.start()
    sc.middle()
    g_sq.forwards()
    g_sq.finish()
    inv_ref[...] = lax.rsqrt(jnp.sum(sq_all[...], axis=0) / inner + EPS)
    inv = as_col(inv_ref[s][:1])
    rows = sc.finish()
    delta = rows * inv
    u = current[...] + delta
    new_ref[...] = u
    delta_ref[...] = delta
    if last:
        dots = jnp.sum(aux[...].astype(F32) * delta, axis=1, keepdims=True)
        gat_ref[s] = as_row(dots)
    else:
        gat_ref[s] = norm_of(u, aux[...]).astype(BF)
    g = Gather("seq", S, gat_ref, sems_out)
    g.start()
    g.forwards()
    g.finish()


def turn(S, inner, last, cid, part, sq, current, aux):
    tokens, width = current.shape
    outs = [
        sds(current.shape, F32),
        sds(current.shape, F32),
        sds((S, 8, tokens), F32),
        sds((S, 8, tokens), F32) if last else sds((S, tokens, width), BF),
    ]
    scratch = [pltpu.VMEM((S,) + sq.shape, F32)]
    scratch += Gather.scratch(S) + Gather.scratch(S)
    scratch += Scatter.scratch(S, (tokens, width))
    return comm_call(
        partial(turn_kernel, S, inner, last), f"turn{cid}", cid, outs, scratch,
        (part, sq, current, aux),
    )


def back_turn_kernel(S, first, *refs):
    dpart, dbc, prior, gain, g_ref = refs[:5]
    refs = list(refs[5:])
    delta_ref = None if first else refs.pop(0)
    new_ref, dbc_ref, gn_ref = refs[:3]
    refs = refs[3:]
    if not first:
        gb_ref, dots_ref = refs[:2]
        refs = refs[2:]
    sc = Scatter("seq", S, dpart, refs[:N_SCATTER])
    sb = Scatter("seq", S, dbc, refs[N_SCATTER : 2 * N_SCATTER])
    sems = refs[2 * N_SCATTER :]
    barrier([("seq", S)])
    s = lax.axis_index("seq")
    sc.start()
    sb.start()
    u = prior[...]
    n = lax.rsqrt(jnp.mean(u * u, axis=-1, keepdims=True) + EPS)
    xhat = u * n
    sc.middle()
    sb.middle()
    dn = sc.finish()
    gn_ref[...] = jnp.broadcast_to(jnp.sum(dn * xhat, axis=0, keepdims=True), gn_ref.shape)
    t = dn * gain[...]
    new = g_ref[...] + n * (t - xhat * jnp.mean(t * xhat, axis=-1, keepdims=True))
    new_ref[...] = new
    if not first:
        gb = new.astype(BF)
        gb_ref[s] = gb
        dots_ref[s] = as_row(jnp.sum(gb.astype(F32) * delta_ref[...], axis=1, keepdims=True))
        gs = [Gather("seq", S, gb_ref, sems[:2]), Gather("seq", S, dots_ref, sems[2:])]
        for g in gs:
            g.start()
        for g in gs:
            g.forwards()
    dbc_ref[...] = sb.finish().astype(BF)
    if not first:
        for g in gs:
            g.finish()


def back_turn(S, first, cid, dpart, dbc, prior, gain, g, delta):
    tokens, width = prior.shape
    outs = [sds(prior.shape, F32), sds(dbc.shape[1:], BF), sds((8, width), F32)]
    scratch = Scatter.scratch(S, (tokens, width)) + Scatter.scratch(S, dbc.shape[1:])
    args = [dpart, dbc, prior, gain, g]
    if not first:
        outs += [sds((S, tokens, width), BF), sds((S, 8, tokens), F32)]
        scratch += Gather.scratch(S) + Gather.scratch(S)
        args.append(delta)
    return comm_call(
        partial(back_turn_kernel, S, first), f"back_turn{cid}", cid, outs, scratch, args
    )


def grads_kernel(S, F, layers, *refs):
    n_in = 3 * layers + 1
    jobs = refs[: 3 * layers]
    small = refs[3 * layers]
    refs = list(refs[n_in:])
    outs = refs[: 3 * layers]
    small_out = refs[3 * layers]
    refs = refs[n_in:]
    scat = []
    for j in range(3 * layers):
        scat.append(Scatter("fsdp", F, jobs[j], refs[:N_SCATTER]))
        refs = refs[N_SCATTER:]
    out_mid = refs[:layers]
    refs = refs[layers:]
    perm_send, perm_recv = refs[:2]
    refs = refs[2:]
    sm_row, sm_mid, sm_col, sm_s1, sm_r1, sm_s2, sm_r2 = refs[:7]
    refs = refs[7:]
    gathers = []
    for j in range(3 * layers):
        gathers.append(Gather("seq", S, outs[j], (refs[2 * j], refs[2 * j + 1])))
    g_small = Gather("seq", S, small_out, (refs[6 * layers], refs[6 * layers + 1]))

    s, f = lax.axis_index("seq"), lax.axis_index("fsdp")
    a_n, b_n = factor(F)
    a, b = f // b_n, f % b_n
    flat = f * S + s
    own = s * F + f
    target = (own % S, own // S)
    source = (flat // F, flat % F)
    moved = flat != own
    barrier([("fsdp", F), ("seq", S)], (source, moved))

    def row(db):
        return pltpu.make_async_remote_copy(
            src_ref=small,
            dst_ref=sm_row.at[db],
            send_sem=sm_s1.at[db],
            recv_sem=sm_r1.at[db],
            device_id=(s, a * b_n + lax.rem(b + db, b_n)),
            device_id_type=MESH,
        )

    def col(da):
        return pltpu.make_async_remote_copy(
            src_ref=sm_mid,
            dst_ref=sm_col.at[a],
            send_sem=sm_s2.at[da],
            recv_sem=sm_r2.at[da],
            device_id=(s, lax.rem(a + da, a_n) * b_n + b),
            device_id_type=MESH,
        )

    order = []
    for l in reversed(range(layers)):
        order += [3 * l + 2, 3 * l, 3 * l + 1]
    for db in range(1, b_n):
        row(db).start()
    for j in order:
        scat[j].start()
    sm_row[0] = small[...]
    for db in range(1, b_n):
        row(db).wait_recv()
    total = None
    for k in range(b_n):
        term = sm_row[lax.rem(b + b_n - k, b_n)]
        total = term if total is None else total + term
    sm_mid[...] = total
    for da in range(1, a_n):
        col(da).start()
    for j in order:
        scat[j].middle()
    sm_col[a] = sm_mid[...]
    for da in range(1, a_n):
        col(da).wait_recv()
    small_out[s] = jnp.sum(sm_col[...], axis=0)
    g_small.start()

    perms = []
    for l in range(layers):
        perms.append(
            pltpu.make_async_remote_copy(
                src_ref=out_mid[l],
                dst_ref=outs[3 * l + 2].at[own % S],
                send_sem=perm_send.at[l],
                recv_sem=perm_recv.at[l],
                device_id=target,
                device_id_type=MESH,
            )
        )
    for j in order:
        l, kind = j // 3, j % 3
        value = scat[j].finish().astype(BF)
        if kind == 2:
            out_mid[l][...] = value

            @pl.when(moved)
            def _():
                perms[l].start()

            @pl.when(jnp.logical_not(moved))
            def _():
                outs[3 * l + 2][s] = value
        else:
            outs[j][s] = value
            gathers[j].start()
    for l in reversed(range(layers)):

        @pl.when(moved)
        def _():
            perms[l].wait()

        gathers[3 * l + 2].start()
    for j in order:
        gathers[j].forwards()
    g_small.forwards()
    for j in order:
        gathers[j].finish()
    g_small.finish()
    for db in range(1, b_n):
        row(db).wait_send()
    for da in range(1, a_n):
        col(da).wait_send()


def reduce_grads(S, F, jobs, small):
    layers = len(jobs) // 3
    a_n, b_n = factor(F)
    sem = pltpu.SemaphoreType.DMA
    outs = [sds((S,) + j.shape[1:], BF) for j in jobs] + [sds((S,) + small.shape, F32)]
    scratch = []
    for j in jobs:
        scratch += Scatter.scratch(F, j.shape[1:])
    scratch += [pltpu.VMEM(jobs[2].shape[1:], BF) for _ in range(layers)]
    scratch += [sem((layers,)), sem((layers,))]
    scratch += [
        pltpu.VMEM((b_n,) + small.shape, F32),
        pltpu.VMEM(small.shape, F32),
        pltpu.VMEM((a_n,) + small.shape, F32),
        sem((b_n,)), sem((b_n,)), sem((a_n,)), sem((a_n,)),
    ]
    for _ in range(len(jobs) + 1):
        scratch += Gather.scratch(S)
    return comm_call(
        partial(grads_kernel, S, F, layers), "grads", 7, outs, scratch, tuple(jobs) + (small,)
    )


def bdot(x, y, dims=((1,), (0,))):
    return lax.dot_general(
        x.astype(BF), y.astype(BF), (dims, ((), ())), preferred_element_type=F32
    )


def hdot(x, y, dims=((1,), (0,))):
    return lax.dot_general(x, y, (dims, ((), ())), precision=HIGH, preferred_element_type=F32)


NT = ((1,), (1,))
TN = ((0,), (0,))


def span(i):
    return slice(i * SPAN, (i + 1) * SPAN)


def limits(segc, segr):
    blocks = segc.shape[0] // SPAN
    rows = lax.broadcasted_iota(jnp.int32, (SPAN, SPAN), 0)
    cols = lax.broadcasted_iota(jnp.int32, (SPAN, SPAN), 1)
    out = {}
    for i in range(blocks):
        for j in range(i + 1):
            kept = segc[span(i)] == segr[:, span(j)]
            if i == j:
                kept = kept & (rows >= cols)
            out[i, j] = jnp.where(kept, 0.0, NEGATIVE)
    return out


def head_map(inner):
    rows = lax.broadcasted_iota(jnp.int32, (inner, LANES), 0)
    cols = lax.broadcasted_iota(jnp.int32, (inner, LANES), 1)
    return ((rows // HEADDIM) == cols).astype(F32)


def shifts(v, cm):
    return [pltpu.roll(v, d, 0) * cm[:, d - 1 : d] for d in range(1, 4)]


def conv_pre(v, moved, par):
    pre = par[4:5] + par[3:4] * v
    for d in range(1, 4):
        pre = pre + par[3 - d : 4 - d] * moved[d - 1]
    return pre


def sigmoid(x):
    return 1.0 / (1.0 + jnp.exp(-x))


def softplus(x):
    return jnp.maximum(x, 0.0) + jnp.log1p(jnp.exp(-jnp.abs(x)))


def decay_of(dt, hp):
    u = dt + hp[1:2]
    delta = softplus(u)
    return u, delta, -jnp.exp(hp[0:1]) * delta


def cumulate(lim, decay):
    blocks = decay.shape[0] // SPAN
    out = []
    for i in range(blocks):
        total = None
        for j in range(i + 1):
            term = hdot((lim[i, j] == 0.0).astype(F32), decay[span(j)])
            total = term if total is None else total + term
        out.append(total)
    return out


def halves(pair):
    lane = lax.broadcasted_iota(jnp.int32, pair.shape, 1)
    low = lane < HEADDIM
    return jnp.where(low, pair, 0.0).astype(BF), jnp.where(low, 0.0, pair).astype(BF)


def forward_kernel(
    nrm, win, wout, par_ref, hp_ref, segc_ref, segr_ref, cm_ref,
    part_ref, sq_ref, z_ref, v_ref, dt_ref, y_ref, sc_ref,
):
    inner = wout.shape[0]
    length = nrm.shape[0]
    blocks = length // SPAN
    conv = v_ref.shape[1]
    x = nrm[...]
    z_ref[...] = jnp.dot(x, win[:, :inner], preferred_element_type=F32)
    v_ref[...] = jnp.dot(x, win[:, inner : inner + conv], preferred_element_type=F32).astype(BF)
    dt = jnp.dot(x, win[:, inner + conv :], preferred_element_type=F32).astype(BF).astype(F32)
    dt_ref[...] = dt
    par, hp = par_ref[...], hp_ref[...]
    lim = limits(segc_ref[...], segr_ref[...])
    v = v_ref[...].astype(F32)
    pre = conv_pre(v, shifts(v, cm_ref[...]), par)
    act = pre * sigmoid(pre)
    x_act = act[:, :inner]
    nstate = (conv - inner) // 2
    b_act = act[:, inner : inner + nstate].astype(BF)
    c_act = act[:, inner + nstate :].astype(BF)
    u, delta, decay = decay_of(dt, hp)
    cum = cumulate(lim, decay)
    cum_t = [c.T for c in cum]
    hm = head_map(inner)
    xs = x_act * hdot(delta, hm, NT)
    cb = {k: bdot(c_act[span(k[0])], b_act[span(k[1])], NT) for k in lim}
    for q in range(inner // LANES):
        ql = slice(q * LANES, (q + 1) * LANES)
        pair = halves(xs[:, ql])
        for i in range(blocks):
            total = par[6:7, ql] * x_act[span(i), ql]
            for j in range(i + 1):
                for e in range(2):
                    h = 2 * q + e
                    w = jnp.exp(jnp.minimum(cum[i][:, h : h + 1] - cum_t[j][h : h + 1], lim[i, j]))
                    total = total + bdot(w * cb[i, j], pair[e][span(j)])
            y_ref[span(i), ql] = total.astype(BF)
    z = z_ref[...]
    prod = y_ref[...].astype(F32) * (z * sigmoid(z))
    square = jnp.sum(prod * prod, axis=1, keepdims=True)
    tokens = sq_ref.shape[2]
    for k in range(sq_ref.shape[0]):
        sq_ref[k] = as_row(square[k * tokens : (k + 1) * tokens])
    sc_ref[...] = (prod * par[5:6, :inner]).astype(BF)
    part_ref[...] = jnp.dot(sc_ref[...], wout[...], preferred_element_type=F32).astype(BF)


def backward_kernel(
    total_inner, nrm, win, wout, par_ref, hp_ref, segc_ref, segr_ref, cm_ref,
    z_ref, v_ref, dt_ref, y_ref, sc_ref, gb_ref, inv_ref, dots_ref,
    gin_ref, gout_ref, dpart_ref, dbc_ref, ddt_ref, small_ref, dproj,
):
    inner = wout.shape[0]
    length = nrm.shape[0]
    blocks = length // SPAN
    conv = v_ref.shape[1]
    nstate = (conv - inner) // 2
    par, hp = par_ref[...], hp_ref[...]
    gb = gb_ref[...]
    inv = jnp.concatenate([as_col(inv_ref[k][:1]) for k in range(inv_ref.shape[0])], axis=0)
    dots = jnp.concatenate([as_col(dots_ref[k][:1]) for k in range(dots_ref.shape[0])], axis=0)
    small_ref[...] = jnp.zeros_like(small_ref)

    scaled_in = lax.dot_general(gb, wout[...], (NT, ((), ())), preferred_element_type=F32) * inv
    z = z_ref[...]
    y = y_ref[...].astype(F32)
    sig = sigmoid(z)
    silu = z * sig
    prod = y * silu
    small_ref[5:6, :inner] = jnp.sum(scaled_in * prod, axis=0, keepdims=True)
    d_prod = scaled_in * par[5:6, :inner] - prod * (inv * inv * dots * (1.0 / total_inner))
    dy = d_prod * silu
    dy = dy.astype(BF).astype(F32)
    dproj[:, :inner] = (d_prod * y * (sig * (1.0 + z * (1.0 - sig)))).astype(BF)
    grad_scaled = (gb.astype(F32) * inv).astype(BF)
    gout_ref[...] = lax.dot_general(
        sc_ref[...], grad_scaled, (TN, ((), ())), preferred_element_type=F32
    ).astype(BF)

    lim = limits(segc_ref[...], segr_ref[...])
    cm = cm_ref[...]
    v = v_ref[...].astype(F32)
    moved = shifts(v, cm)
    pre = conv_pre(v, moved, par)
    csig = sigmoid(pre)
    act = pre * csig
    x_act = act[:, :inner]
    b_act = act[:, inner : inner + nstate].astype(BF)
    c_act = act[:, inner + nstate :].astype(BF)
    u, delta, decay = decay_of(dt_ref[...], hp)
    cum = cumulate(lim, decay)
    cum_t = [c.T for c in cum]
    hm = head_map(inner)
    delta_bc = hdot(delta, hm, NT)
    xs = x_act * delta_bc
    cb = {k: bdot(c_act[span(k[0])], b_act[span(k[1])], NT) for k in lim}

    lane = lax.broadcasted_iota(jnp.int32, (SPAN, LANES), 1)
    sub = lax.broadcasted_iota(jnp.int32, (LANES, SPAN), 0)
    dcb = {k: jnp.zeros((SPAN, SPAN), F32) for k in lim}
    drow = [jnp.zeros((SPAN, LANES), F32) for _ in range(blocks)]
    dcol = [jnp.zeros((LANES, SPAN), F32) for _ in range(blocks)]
    dxs = []
    for q in range(inner // LANES):
        ql = slice(q * LANES, (q + 1) * LANES)
        pair = xs[:, ql].astype(BF)
        dyp = halves(dy[:, ql])
        dxq = [jnp.zeros((SPAN, LANES), F32) for _ in range(blocks)]
        for i in range(blocks):
            for j in range(i + 1):
                for e in range(2):
                    h = 2 * q + e
                    w = jnp.exp(jnp.minimum(cum[i][:, h : h + 1] - cum_t[j][h : h + 1], lim[i, j]))
                    p = w * cb[i, j]
                    dp = bdot(dyp[e][span(i)], pair[span(j)], NT)
                    dxq[j] = dxq[j] + bdot(p, dyp[e][span(i)], TN)
                    dcb[i, j] = dcb[i, j] + dp * w
                    g = dp * p
                    drow[i] = drow[i] + jnp.where(lane == h, jnp.sum(g, axis=1, keepdims=True), 0.0)
                    dcol[j] = dcol[j] + jnp.where(sub == h, jnp.sum(g, axis=0, keepdims=True), 0.0)
        dxs.append(jnp.concatenate(dxq, axis=0))
    dxs = jnp.concatenate(dxs, axis=1)
    db, dc = [], []
    for k in range(blocks):
        db.append(sum(bdot(dcb[i, k], c_act[span(i)], TN) for i in range(k, blocks)))
        dc.append(sum(bdot(dcb[k, j], b_act[span(j)]) for j in range(k + 1)))
    dcum_t = [drow[k].T - dcol[k] for k in range(blocks)]
    ddecay = []
    for j in range(blocks):
        total = None
        for i in range(j, blocks):
            term = hdot(dcum_t[i], (lim[i, j] == 0.0).astype(F32))
            total = term if total is None else total + term
        ddecay.append(total.T)
    ddecay = jnp.concatenate(ddecay, axis=0)
    ddelta = hdot(dxs * x_act, hm) - jnp.exp(hp[0:1]) * ddecay
    ddt = ddelta * sigmoid(u)
    small_ref[6:7, :LANES] = jnp.sum(ddecay * decay, axis=0, keepdims=True)
    small_ref[6:7, LANES : 2 * LANES] = jnp.sum(ddt, axis=0, keepdims=True)
    skip = jnp.broadcast_to(jnp.sum(dy * x_act, axis=0, keepdims=True), (8, inner))
    small_ref[6:7, 2 * LANES : 3 * LANES] = hdot(skip, hm)[:1]
    dx_act = dxs * delta_bc + dy * par[6:7, :inner]
    dact = jnp.concatenate(
        [dx_act, jnp.concatenate(db, axis=0), jnp.concatenate(dc, axis=0)], axis=1
    )

    dpre = dact * (csig * (1.0 + pre * (1.0 - csig)))
    small_ref[4:5, :conv] = jnp.sum(dpre, axis=0, keepdims=True)
    small_ref[3:4, :conv] = jnp.sum(dpre * v, axis=0, keepdims=True)
    dv = par[3:4] * dpre
    for d in range(1, 4):
        small_ref[3 - d : 4 - d, :conv] = jnp.sum(dpre * moved[d - 1], axis=0, keepdims=True)
        back = dpre * cm[:, d - 1 : d] * par[3 - d : 4 - d]
        dv = dv + pltpu.roll(back, length - d, 0)
    heads = inner // HEADDIM
    real = lax.broadcasted_iota(jnp.int32, (length, LANES), 1) < heads
    ddt = jnp.where(real, ddt, 0.0)
    dproj[:, inner : inner + conv] = dv.astype(BF)
    dproj[:, inner + conv :] = ddt.astype(BF)
    dbc_ref[...] = dv[:, inner:].T.astype(BF)
    ddt_ref[...] = ddt.T[: ddt_ref.shape[0]].astype(BF)
    gin_ref[...] = lax.dot_general(
        nrm[...], dproj[:, : 2 * inner], (TN, ((), ())), preferred_element_type=F32
    ).astype(BF)
    dpart_ref[...] = lax.dot_general(
        dproj[...], win[...], (NT, ((), ())), preferred_element_type=F32
    ).astype(BF)


def body(
    hidden, cotangent, segments, in_weight, out_weight, conv_weight, conv_bias,
    norm_gain, gate_gain, a_log, dt_bias, d_skip,
):
    seq_idx = lax.axis_index("seq")
    S = lax.axis_size("seq")
    F = lax.axis_size("fsdp")
    current = hidden[0]
    tokens, width = current.shape
    segment = segments[0]
    length = segment.shape[0]
    layers, taps, conv_part = conv_weight.shape
    width_part = norm_gain.shape[1]
    inner_part = gate_gain.shape[1]
    heads = a_log.shape[1]
    inner = inner_part * F
    convdim = conv_part * F
    bc = convdim - inner
    hl, il, bl = heads // S, inner // S, bc // S
    dt_base = 2 * inner + bc

    def mine(arr, size, axis, base=0):
        return lax.dynamic_slice_in_dim(arr, base + seq_idx * size, size, axis)

    win = jnp.concatenate(
        [
            mine(in_weight, il, 2),
            mine(in_weight, il, 2, inner),
            in_weight[:, :, 2 * inner : dt_base],
            mine(in_weight, hl, 2, dt_base),
            jnp.zeros((layers, in_weight.shape[1], LANES - hl), BF),
        ],
        axis=2,
    )
    small_width = -(-max(conv_part, width_part, inner_part) // LANES) * LANES

    def padded(arr):
        arr = arr.reshape(-1, arr.shape[-1])
        return jnp.pad(arr, ((0, 0), (0, small_width - arr.shape[1])))

    small = jnp.concatenate(
        [padded(conv_weight), padded(conv_bias), padded(norm_gain), padded(gate_gain)], axis=0
    )
    small = jnp.pad(small, ((0, -small.shape[0] % 16), (0, 0)))
    piece = inner_part // S
    wout_in = out_weight.reshape(layers, S, piece, width).transpose(1, 0, 2, 3)
    cot = cotangent[0].astype(BF)
    small_all, win_all, wout_all, gb_all = gather_weights(S, F, small, win, wout_in, cot)
    win_loc = win_all.reshape(layers, width, -1)
    wout_loc = wout_all.transpose(1, 0, 2, 3).reshape(layers, il, width)

    def unpack(start, rows, part):
        got = small_all[:, start : start + rows, :part].astype(F32)
        return got.transpose(1, 0, 2).reshape(rows, F * part)

    conv_full = unpack(0, layers * taps, conv_part).reshape(layers, taps, convdim)
    bias_full = unpack(layers * taps, layers, conv_part)[:, None]
    norm_full = unpack(layers * (taps + 1), layers, width_part)
    gate_full = unpack(layers * (taps + 2), layers, inner_part)
    five = jnp.concatenate([conv_full, bias_full], axis=1)
    five = jnp.concatenate([mine(five, il, 2), five[:, :, inner:]], axis=2)
    skip = jnp.repeat(mine(d_skip, hl, 1), HEADDIM, axis=1)
    rows = jnp.stack([mine(gate_full, il, 1), skip, jnp.zeros_like(skip)], axis=1)
    par = jnp.concatenate([five, jnp.pad(rows, ((0, 0), (0, 0), (0, bc)))], axis=1)
    hp = jnp.stack([mine(a_log, hl, 1), mine(dt_bias, hl, 1)], axis=1)
    hp = jnp.pad(hp, ((0, 0), (0, 6), (0, LANES - hl)))

    segc, segr = segment[:, None], segment[None, :]
    cm = jnp.stack(
        [
            jnp.concatenate([jnp.zeros((d,), bool), segment[d:] == segment[:-d]])
            for d in range(1, taps)
        ],
        axis=1,
    ).astype(F32)
    cm = jnp.pad(cm, ((0, 0), (0, 8 - cm.shape[1])))

    nrm_all = comm_call(
        partial(start_kernel, S), "start", 1, [sds((S, tokens, width), BF)],
        Gather.scratch(S), (current, norm_full[:1]),
    )[0]

    conv_loc = il + bc
    saved = []
    for l in range(layers):
        last = l == layers - 1
        shared = (win_loc[l], wout_loc[l], par[l], hp[l], segc, segr, cm)
        nrm = nrm_all.reshape(length, width)
        part, sq, z, v, dt, y, scaled = local_call(
            forward_kernel,
            f"forward{l}",
            [
                sds((length, width), BF),
                sds((S, 8, tokens), F32),
                sds((length, il), F32),
                sds((length, conv_loc), BF),
                sds((length, LANES), F32),
                sds((length, il), BF),
                sds((length, il), BF),
            ],
            (nrm,) + shared,
        )
        new, delta, inv, got = turn(
            S, inner, last, 2 + l, part.reshape(S, tokens, width), sq, current,
            cot if last else norm_full[l + 1 : l + 2],
        )
        saved.append((nrm, shared, (z, v, dt, y, scaled), current, delta, inv))
        current = new
        nrm_all = got
    dots_all = got

    grad = cotangent[0]
    jobs = [None] * (3 * layers)
    smalls = [None] * layers
    norms = [None] * layers
    for l in reversed(range(layers)):
        nrm, shared, kept, prior, delta, inv = saved[l]
        gin, gout, dpart, dbc, ddt, small_l = pl.pallas_call(
            partial(backward_kernel, inner),
            name=f"backward{l}",
            out_shape=[
                sds((width, 2 * il), BF),
                sds((il, width), BF),
                sds((length, width), BF),
                sds((bc, length), BF),
                sds((LANES - bl, length), BF),
                sds((8, width), F32),
            ],
            in_specs=[pl.BlockSpec(memory_space=pltpu.VMEM)] * 16,
            out_specs=[pl.BlockSpec(memory_space=pltpu.VMEM)] * 6,
            scratch_shapes=[pltpu.VMEM((length, il + conv_loc + LANES), BF)],
            compiler_params=pltpu.CompilerParams(vmem_limit_bytes=VMEM_LIMIT),
        )(nrm, *shared, *kept, gb_all.reshape(length, width), inv, dots_all)
        got = back_turn(
            S, l == 0, 4 + l, dpart.reshape(S, tokens, width), dbc.reshape(S, bl, length),
            prior, norm_full[l : l + 1], grad, saved[l - 1][4] if l > 0 else None,
        )
        grad, dbc_own, norms[l] = got[:3]
        if l > 0:
            gb_all, dots_all = got[3:]
        tail = lax.dot_general(
            nrm, jnp.concatenate([dbc_own, ddt], axis=0), (((0,), (1,)), ((), ())),
            preferred_element_type=F32,
        ).astype(BF)
        jobs[3 * l] = gin.reshape(F, width // F, 2 * il)
        jobs[3 * l + 1] = tail.reshape(F, width // F, LANES)
        jobs[3 * l + 2] = gout.reshape(F, il // F, width)
        smalls[l] = small_l

    small = jnp.concatenate([x for l in range(layers) for x in (smalls[l], norms[l])], axis=0)
    got = reduce_grads(S, F, jobs, small)
    sums = got[-1].reshape(S, layers, 16, width)

    in_out, out_out = [], []
    for l in range(layers):
        zx, tail, out = got[3 * l : 3 * l + 3]
        cols = [zx[s, :, :il] for s in range(S)] + [zx[s, :, il:] for s in range(S)]
        cols += [tail[s, :, :bl] for s in range(S)] + [tail[s, :, bl : bl + hl] for s in range(S)]
        in_out.append(jnp.concatenate(cols, axis=1).astype(F32))
        out_out.append(out.reshape(-1, width).astype(F32))

    def own(arr, part):
        return lax.dynamic_slice_in_dim(arr, lax.axis_index("fsdp") * part, part, arr.ndim - 1)

    def lined(arr):
        return jnp.concatenate([arr[s] for s in range(S)], axis=-1)

    five_sum = sums[:, :, : taps + 1]
    five_all = jnp.concatenate(
        [lined(five_sum[..., :il]), jnp.sum(five_sum[..., il:conv_loc], axis=0)], axis=-1
    )
    five_own = own(five_all, conv_part)
    gate_own = own(lined(sums[:, :, 5, :il]), inner_part)
    norm_own = own(jnp.sum(sums[:, :, 8], axis=0), width_part)
    per_head = [lined(sums[:, :, 6, k * LANES : k * LANES + hl]) for k in range(3)]
    return (
        current[None],
        grad[None],
        jnp.stack(in_out),
        jnp.stack(out_out),
        five_own[:, :taps],
        five_own[:, taps],
        norm_own,
        gate_own,
        *per_head,
    )


def solution(mesh):
    token = P("fsdp", "seq", None)
    rows = P(None, "fsdp", None)
    split = P(None, "fsdp")
    taps = P(None, None, "fsdp")
    return jax.shard_map(
        body,
        mesh=mesh,
        in_specs=(token, token, P("fsdp", None), rows, rows, taps, split, split, split, P(), P(), P()),
        out_specs=(token, token, rows, rows, taps, split, split, split, P(), P(), P()),
        check_vma=False,
    )
```

```python
from functools import partial

import jax
import jax.numpy as jnp
from jax import lax
from jax.experimental import pallas as pl
from jax.experimental.pallas import tpu as pltpu
from jax.sharding import PartitionSpec as P

HEADDIM = 64
SPAN = 256
EPS = 1e-05
HIGH = lax.Precision.HIGHEST
BF = jnp.bfloat16
F32 = jnp.float32
MESH = pl.DeviceIdType.MESH
NEGATIVE = -1e30
LANES = 128
VMEM_LIMIT = 60 * 1024 * 1024


def factor(n):
    b = 1
    while (2 * b) * (2 * b) <= n:
        b *= 2
    return n // b, b


def peers_of(axis, n):
    a_n, b_n = factor(n)
    s, f = lax.axis_index("seq"), lax.axis_index("fsdp")
    i = s if axis == "seq" else f
    a, b = i // b_n, i % b_n

    def dev(k):
        return (k, f) if axis == "seq" else (s, k)

    out = []
    for da in range(1, a_n):
        out.append(dev(lax.rem(a + da, a_n) * b_n + b))
    for db in range(1, b_n):
        out.append(dev(a * b_n + lax.rem(b + db, b_n)))
    return out


def barrier(groups, extra=None):
    sem = pltpu.get_barrier_semaphore()
    devices = [d for axis, n in groups for d in peers_of(axis, n)]
    for d in devices:
        pl.semaphore_signal(sem, inc=1, device_id=d, device_id_type=MESH)
    if extra is None:
        pl.semaphore_wait(sem, len(devices))
        return
    source, moved = extra

    @pl.when(moved)
    def _():
        pl.semaphore_signal(sem, inc=1, device_id=source, device_id_type=MESH)

    pl.semaphore_wait(sem, len(devices) + moved.astype(jnp.int32))


class Gather:
    def __init__(self, axis, n, ref, sems):
        self.n = n
        self.a_n, self.b_n = factor(n)
        s, f = lax.axis_index("seq"), lax.axis_index("fsdp")
        i = s if axis == "seq" else f
        self.a, self.b = i // self.b_n, i % self.b_n
        self.dev = (lambda k: (k, f)) if axis == "seq" else (lambda k: (s, k))
        self.ref = ref
        self.send, self.recv = sems

    @staticmethod
    def scratch(n):
        a_n, b_n = factor(n)
        count = a_n * b_n
        return [pltpu.SemaphoreType.DMA((count,)), pltpu.SemaphoreType.DMA((count,))]

    def _first(self, da, sender):
        a = self.a if sender else lax.rem(self.a + self.a_n - da, self.a_n)
        block = a * self.b_n + self.b
        return pltpu.make_async_remote_copy(
            src_ref=self.ref.at[block],
            dst_ref=self.ref.at[block],
            send_sem=self.send.at[da * self.b_n],
            recv_sem=self.recv.at[da * self.b_n],
            device_id=self.dev(lax.rem(self.a + da, self.a_n) * self.b_n + self.b),
            device_id_type=MESH,
        )

    def _second(self, da, db, sender):
        a = lax.rem(self.a + self.a_n - da, self.a_n)
        b = self.b if sender else lax.rem(self.b + self.b_n - db, self.b_n)
        block = a * self.b_n + b
        return pltpu.make_async_remote_copy(
            src_ref=self.ref.at[block],
            dst_ref=self.ref.at[block],
            send_sem=self.send.at[da * self.b_n + db],
            recv_sem=self.recv.at[da * self.b_n + db],
            device_id=self.dev(self.a * self.b_n + lax.rem(self.b + db, self.b_n)),
            device_id_type=MESH,
        )

    def start_columns(self):
        for da in range(1, self.a_n):
            self._first(da, True).start()

    def start_rows(self):
        for db in range(1, self.b_n):
            self._second(0, db, True).start()

    def start(self):
        self.start_columns()
        self.start_rows()

    def forward(self, da):
        self._first(da, False).wait_recv()
        for db in range(1, self.b_n):
            self._second(da, db, True).start()

    def forwards(self):
        for da in range(1, self.a_n):
            self.forward(da)

    def finish(self):
        for da in range(self.a_n):
            for db in range(1, self.b_n):
                self._second(da, db, False).wait_recv()
        for da in range(1, self.a_n):
            self._first(da, True).wait_send()
        for da in range(self.a_n):
            for db in range(1, self.b_n):
                self._second(da, db, True).wait_send()


class Scatter:
    def __init__(self, axis, n, ref, scratch):
        self.a_n, self.b_n = factor(n)
        s, f = lax.axis_index("seq"), lax.axis_index("fsdp")
        i = s if axis == "seq" else f
        self.a, self.b = i // self.b_n, i % self.b_n
        self.dev = (lambda k: (k, f)) if axis == "seq" else (lambda k: (s, k))
        self.ref = ref
        self.row_in, self.mid, self.col_in, self.send, self.recv, self.send2, self.recv2 = scratch

    @staticmethod
    def scratch(n, shape, dtype=BF):
        a_n, b_n = factor(n)
        sem = pltpu.SemaphoreType.DMA
        return [
            pltpu.VMEM((a_n, b_n - 1) + shape, dtype),
            pltpu.VMEM((a_n,) + shape, dtype),
            pltpu.VMEM((a_n - 1,) + shape, dtype),
            sem((a_n, b_n - 1)),
            sem((a_n, b_n - 1)),
            sem((a_n,)),
            sem((a_n,)),
        ]

    def _row(self, da, db):
        a = lax.rem(self.a + da, self.a_n)
        b = lax.rem(self.b + db, self.b_n)
        return pltpu.make_async_remote_copy(
            src_ref=self.ref.at[a * self.b_n + b],
            dst_ref=self.row_in.at[da, db - 1],
            send_sem=self.send.at[da, db - 1],
            recv_sem=self.recv.at[da, db - 1],
            device_id=self.dev(self.a * self.b_n + b),
            device_id_type=MESH,
        )

    def _col(self, da):
        a = lax.rem(self.a + da, self.a_n)
        return pltpu.make_async_remote_copy(
            src_ref=self.mid.at[da],
            dst_ref=self.col_in.at[da - 1],
            send_sem=self.send2.at[da],
            recv_sem=self.recv2.at[da],
            device_id=self.dev(a * self.b_n + self.b),
            device_id_type=MESH,
        )

    def start(self):
        for da in list(range(1, self.a_n)) + [0]:
            for db in range(1, self.b_n):
                self._row(da, db).start()

    def _sum(self, da):
        a = lax.rem(self.a + da, self.a_n)
        for db in range(1, self.b_n):
            self._row(da, db).wait_recv()
        total = self.ref[a * self.b_n + self.b].astype(F32)
        for db in range(1, self.b_n):
            total = total + self.row_in[da, db - 1].astype(F32)
        return total

    def middle(self):
        for da in range(1, self.a_n):
            self.mid[da] = self._sum(da).astype(self.mid.dtype)
            self._col(da).start()

    def finish(self):
        total = self._sum(0)
        for da in range(1, self.a_n):
            self._col(da).wait_recv()
            total = total + self.col_in[da - 1].astype(F32)
        for da in range(self.a_n):
            for db in range(1, self.b_n):
                self._row(da, db).wait_send()
        for da in range(1, self.a_n):
            self._col(da).wait_send()
        return total


N_SCATTER = 7


def comm_call(kernel, name, collective_id, outs, scratch, args, any_space=False):
    space = pl.ANY if any_space else pltpu.VMEM
    spec = pl.BlockSpec(memory_space=space)
    return pl.pallas_call(
        kernel,
        name=name,
        out_shape=outs,
        in_specs=[spec] * len(args),
        out_specs=[spec] * len(outs),
        scratch_shapes=scratch,
        compiler_params=pltpu.CompilerParams(
            collective_id=collective_id, has_side_effects=True, vmem_limit_bytes=VMEM_LIMIT
        ),
    )(*args)


def local_call(kernel, name, outs, args):
    spec = pl.BlockSpec(memory_space=pltpu.VMEM)
    return pl.pallas_call(
        kernel,
        name=name,
        out_shape=outs,
        in_specs=[spec] * len(args),
        out_specs=[spec] * len(outs),
        compiler_params=pltpu.CompilerParams(vmem_limit_bytes=VMEM_LIMIT),
    )(*args)


def sds(shape, dtype):
    return jax.ShapeDtypeStruct(shape, dtype)


def as_row(col):
    t = col.shape[0]
    return jnp.broadcast_to(col, (t, LANES)).T[:8]


def as_col(row):
    t = row.shape[1]
    return jnp.broadcast_to(row, (LANES, t)).T[:, :1]


def norm_of(u, gain):
    return u * lax.rsqrt(jnp.mean(u * u, axis=-1, keepdims=True) + EPS) * gain


def bdot(x, y, dims=((1,), (0,))):
    return lax.dot_general(
        x.astype(BF), y.astype(BF), (dims, ((), ())), preferred_element_type=F32
    )


def hdot(x, y, dims=((1,), (0,))):
    return lax.dot_general(x, y, (dims, ((), ())), precision=HIGH, preferred_element_type=F32)


NT = ((1,), (1,))
TN = ((0,), (0,))


def span(i):
    return slice(i * SPAN, (i + 1) * SPAN)


def limits(segc, segr):
    blocks = segc.shape[0] // SPAN
    rows = lax.broadcasted_iota(jnp.int32, (SPAN, SPAN), 0)
    cols = lax.broadcasted_iota(jnp.int32, (SPAN, SPAN), 1)
    out = {}
    for i in range(blocks):
        for j in range(i + 1):
            kept = segc[span(i)] == segr[:, span(j)]
            if i == j:
                kept = kept & (rows >= cols)
            out[i, j] = jnp.where(kept, 0.0, NEGATIVE)
    return out


def head_map(inner):
    rows = lax.broadcasted_iota(jnp.int32, (inner, LANES), 0)
    cols = lax.broadcasted_iota(jnp.int32, (inner, LANES), 1)
    return ((rows // HEADDIM) == cols).astype(F32)


def shifts(v, cm):
    return [pltpu.roll(v, d, 0) * cm[:, d - 1 : d] for d in range(1, 4)]


def conv_pre(v, moved, par):
    pre = par[4:5] + par[3:4] * v
    for d in range(1, 4):
        pre = pre + par[3 - d : 4 - d] * moved[d - 1]
    return pre


def sigmoid(x):
    return 1.0 / (1.0 + jnp.exp(-x))


def softplus(x):
    return jnp.maximum(x, 0.0) + jnp.log1p(jnp.exp(-jnp.abs(x)))


def decay_of(dt, hp):
    u = dt + hp[1:2]
    delta = softplus(u)
    return u, delta, -jnp.exp(hp[0:1]) * delta


def cumulate(lim, decay):
    blocks = decay.shape[0] // SPAN
    out = []
    for i in range(blocks):
        total = None
        for j in range(i + 1):
            term = hdot((lim[i, j] == 0.0).astype(F32), decay[span(j)])
            total = term if total is None else total + term
        out.append(total)
    return out


def halves(pair):
    lane = lax.broadcasted_iota(jnp.int32, pair.shape, 1)
    low = lane < HEADDIM
    return jnp.where(low, pair, 0.0).astype(BF), jnp.where(low, 0.0, pair).astype(BF)


class Take:
    def __init__(self, refs):
        self.refs = list(refs)

    def __call__(self, n=None):
        if n is None:
            return self.refs.pop(0)
        got, self.refs = self.refs[:n], self.refs[n:]
        return got


def flat(ref):
    f, rows, cols = ref.shape
    if rows % 16 == 0:
        return ref[...].reshape(f * rows, cols)
    return jnp.concatenate([ref[k].astype(F32) for k in range(f)], axis=0).astype(ref.dtype)


def put(ref, value):
    rows = ref.shape[1]
    for k in range(ref.shape[0]):
        ref[k] = value[k * rows : (k + 1) * rows].astype(ref.dtype)


def seg_parts(segr_ref):
    row = segr_ref[...].astype(F32)
    length = row.shape[1]
    wide = jnp.broadcast_to(row, (LANES, length)).T
    pos = lax.broadcasted_iota(jnp.int32, (length, LANES), 0)
    cm = []
    for d in range(1, 4):
        same = (pltpu.roll(wide, d, 0) == wide) & (pos >= d)
        cm.append(same.astype(F32)[:, :1])
    return wide[:, :1], row, jnp.concatenate(cm, axis=1)


def mix_forward(l, seg, nrm, win, wout, par, hp, out, hooks):
    part_ref, sq_ref, z_ref, v_ref, dt_ref, y_ref, sc_ref = out
    segc, segr, cm = seg
    inner = z_ref.shape[1]
    length, conv = v_ref.shape
    blocks = length // SPAN
    x = flat(nrm)
    w = flat(win)
    z_ref[...] = jnp.dot(x, w[:, :inner], preferred_element_type=F32)
    v_ref[...] = jnp.dot(x, w[:, inner : inner + conv], preferred_element_type=F32).astype(BF)
    dt = jnp.dot(x, w[:, inner + conv :], preferred_element_type=F32).astype(BF).astype(F32)
    dt_ref[...] = dt
    hooks("projected")
    lim = limits(segc, segr)
    v = v_ref[...].astype(F32)
    pre = conv_pre(v, shifts(v, cm), par)
    act = pre * sigmoid(pre)
    x_act = act[:, :inner]
    nstate = (conv - inner) // 2
    b_act = act[:, inner : inner + nstate].astype(BF)
    c_act = act[:, inner + nstate :].astype(BF)
    u, delta, decay = decay_of(dt, hp)
    cum = cumulate(lim, decay)
    cum_t = [c.T for c in cum]
    hm = head_map(inner)
    xs = x_act * hdot(delta, hm, NT)
    cb = {k: bdot(c_act[span(k[0])], b_act[span(k[1])], NT) for k in lim}
    for q in range(inner // LANES):
        ql = slice(q * LANES, (q + 1) * LANES)
        pair = halves(xs[:, ql])
        for i in range(blocks):
            total = par[6:7, ql] * x_act[span(i), ql]
            for j in range(i + 1):
                for e in range(2):
                    h = 2 * q + e
                    g = jnp.exp(jnp.minimum(cum[i][:, h : h + 1] - cum_t[j][h : h + 1], lim[i, j]))
                    total = total + bdot(g * cb[i, j], pair[e][span(j)])
            y_ref[span(i), ql] = total.astype(BF)
    hooks("mixed")
    z = z_ref[...]
    prod = y_ref[...].astype(F32) * (z * sigmoid(z))
    square = jnp.sum(prod * prod, axis=1, keepdims=True)
    tokens = sq_ref.shape[1]
    for k in range(sq_ref.shape[0] // 8):
        sq_ref[8 * k : 8 * k + 8] = as_row(square[k * tokens : (k + 1) * tokens])
    sc_ref[...] = (prod * par[5:6, :inner]).astype(BF)
    hooks("gated")
    put(part_ref, jnp.dot(sc_ref[...], flat(wout), preferred_element_type=F32))


def forward_kernel(S, F, L, heads, *refs):
    take = Take(refs)
    hidden, cot, segr_ref, win_raw, wout_raw, cw, cb, ng, gg, hp_ref = take(10)
    hidden_out, gb_all, gains, par_ref, dots_all = take(5)
    per = [dict(zip(FORWARD_OUTS, take(len(FORWARD_OUTS)))) for _ in range(L)]
    small_all, full = take(2)
    parts, sq_all = take(L), take(L)
    scs = [take(N_SCATTER) for _ in range(L)]

    def sems():
        return take(2)

    s, f = lax.axis_index("seq"), lax.axis_index("fsdp")
    g_small = Gather("fsdp", F, small_all, sems())
    g_cot = Gather("seq", S, gb_all, sems())
    g_dots = Gather("seq", S, dots_all, sems())
    g_in = [Gather("fsdp", F, per[l]["win"], sems()) for l in range(L)]
    g_out = [Gather("fsdp", F, per[l]["wout"], sems()) for l in range(L)]
    g_nrm = [Gather("seq", S, per[l]["nrm"], sems()) for l in range(L)]
    g_sq = [Gather("seq", S, sq_all[l], sems()) for l in range(L)]
    perm_send, perm_recv, perm_stay = take(3)

    flat_id = f * S + s
    own = s * F + f
    target = (flat_id // F, flat_id % F)
    source = (own % S, own // S)
    moved = flat_id != own
    barrier([("fsdp", F), ("seq", S)], (source, moved))

    taps, conv_part = cw.shape[1:]
    width_part, inner_part = ng.shape[1], gg.shape[1]
    inner, convdim = inner_part * F, conv_part * F
    il, hl = inner // S, heads // S
    bc = convdim - inner
    dt_base = 2 * inner + bc

    wide = small_all.shape[2]

    def lanes(x):
        x = x.astype(F32)
        if x.shape[1] == wide:
            return x
        return jnp.concatenate([x, jnp.zeros((x.shape[0], wide - x.shape[1]), F32)], axis=1)

    rows = [lanes(cw[l]) for l in range(L)] + [lanes(cb[...]), lanes(ng[...]), lanes(gg[...])]
    count = L * (taps + 3)
    rows.append(jnp.zeros((small_all.shape[1] - count, wide), F32))
    small_all[f] = jnp.concatenate(rows, axis=0).astype(BF)
    g_small.start()

    def block(l):
        raw = win_raw[l]
        tail = raw[:, dt_base:].astype(F32)
        tail = jnp.concatenate(
            [tail, jnp.zeros((tail.shape[0], LANES - tail.shape[1]), F32)], axis=1
        )
        tail = pltpu.roll(tail, lax.rem(LANES - s * hl, LANES), 1)
        lane = lax.broadcasted_iota(jnp.int32, tail.shape, 1)
        tail = jnp.where(lane < hl, tail, 0.0).astype(BF)
        start = pl.multiple_of(s * il, LANES)
        dst = per[l]["win"]
        dst[f, :, :il] = win_raw[l, :, pl.ds(start, il)]
        dst[f, :, il : 2 * il] = win_raw[l, :, pl.ds(pl.multiple_of(inner + start, LANES), il)]
        dst[f, :, 2 * il : 2 * il + bc] = raw[:, 2 * inner : dt_base]
        dst[f, :, 2 * il + bc :] = tail

    block(0)
    g_in[0].start()

    def perm(l):
        return pltpu.make_async_remote_copy(
            src_ref=wout_raw.at[l, s],
            dst_ref=per[l]["wout"].at[flat_id % F],
            send_sem=perm_send.at[l],
            recv_sem=perm_recv.at[l],
            device_id=target,
            device_id_type=MESH,
        )

    def stay(l):
        return pltpu.make_async_copy(
            wout_raw.at[l, s], per[l]["wout"].at[f], perm_stay.at[l]
        )

    def perm_start(l):
        @pl.when(moved)
        def _():
            perm(l).start()

        @pl.when(jnp.logical_not(moved))
        def _():
            stay(l).start()

    def perm_wait(l):
        @pl.when(moved)
        def _():
            perm(l).wait()

        @pl.when(jnp.logical_not(moved))
        def _():
            stay(l).wait()

    for l in range(L):
        perm_start(l)
    for l in range(1, L):
        block(l)
    gb_all[s] = cot[...].astype(BF)
    seg = seg_parts(segr_ref)

    g_small.forwards()
    g_small.finish()
    got = [small_all[k].astype(F32) for k in range(F)]

    def joined(lo, hi, part):
        return jnp.concatenate([x[lo:hi, :part] for x in got], axis=1)

    full[: L * (taps + 1)] = joined(0, L * (taps + 1), conv_part)
    lo = L * (taps + 1)
    full[lo + L : lo + 2 * L, :inner] = joined(lo + L, lo + 2 * L, inner_part)
    gains[...] = jnp.zeros_like(gains)
    gains[:L] = joined(lo, lo + L, width_part)
    part_in = pl.ds(pl.multiple_of(s * il, LANES), il)
    hm = head_map(il)
    for l in range(L):
        par_ref[l] = jnp.zeros_like(par_ref[l])
        par_ref[l, :taps, :il] = full[l * taps : (l + 1) * taps, part_in]
        par_ref[l, :taps, il:] = full[l * taps : (l + 1) * taps, inner:convdim]
        r = L * taps + l
        par_ref[l, 4:5, :il] = full[r : r + 1, part_in]
        par_ref[l, 4:5, il:] = full[r : r + 1, inner:convdim]
        r = lo + L + l
        par_ref[l, 5:6, :il] = full[r : r + 1, part_in]
        par_ref[l, 6:7, :il] = hdot(hp_ref[l], hm, NT)[2:3]

    per[0]["nrm"][s] = norm_of(hidden[...], gains[:1]).astype(BF)
    g_nrm[0].start()
    g_in[0].forwards()
    perm_wait(0)
    g_out[0].start()
    for l in range(1, L):
        g_in[l].start_columns()
    g_nrm[0].forwards()
    g_cot.start()
    g_nrm[0].finish()
    g_in[0].finish()

    for l in range(L):
        last = l == L - 1
        if l > 0:
            g_in[l].finish()

        def hooks(stage, l=l, last=last):
            if stage == "projected":
                g_out[l].forwards()
                if l == 0:
                    g_cot.forwards()
            if stage == "mixed" and not last:
                g_in[l + 1].start_rows()
                g_in[l + 1].forwards()
                perm_wait(l + 1)
                g_out[l + 1].start()
            if stage == "gated":
                g_out[l].finish()

        o = per[l]
        mix_forward(
            l, seg, o["nrm"], o["win"], o["wout"], par_ref[l], hp_ref[l],
            (parts[l], sq_all[l].at[s], o["z"], o["v"], o["dt"], o["y"], o["sc"]), hooks,
        )
        sc = Scatter("seq", S, parts[l], scs[l])
        sc.start()
        g_sq[l].start()
        current = hidden if l == 0 else per[l - 1]["new"]
        sc.middle()
        g_sq[l].forwards()
        g_sq[l].finish()
        tokens = hidden.shape[0]
        o["inv"][...] = lax.rsqrt(jnp.sum(sq_all[l][...], axis=0) * (1.0 / inner) + EPS)
        inv = as_col(o["inv"][pl.ds(pl.multiple_of(8 * s, 8), 8)][:1])
        delta = sc.finish() * inv
        u = current[...] + delta
        o["delta"][...] = delta
        o["new"][...] = u
        if last:
            hidden_out[...] = u
            dots = jnp.sum(gb_all[s].astype(F32) * delta, axis=1, keepdims=True)
            dots_all[s] = as_row(dots)
            g = g_dots
        else:
            per[l + 1]["nrm"][s] = norm_of(u, gains[l + 1 : l + 2]).astype(BF)
            g = g_nrm[l + 1]
        g.start()
        if l == 0:
            g_cot.finish()
        g.forwards()
        g.finish()


FORWARD_OUTS = ("win", "wout", "nrm", "z", "v", "dt", "y", "sc", "new", "delta", "inv")


def forward(S, F, heads, hidden, cot, segr, win_raw, wout_raw, cw, cb, ng, gg, hp):
    tokens, width = hidden.shape
    length = segr.shape[1]
    L, taps, conv_part = cw.shape
    inner, convdim = gg.shape[1] * F, conv_part * F
    il, bc = inner // S, convdim - inner
    conv = il + bc
    sem = pltpu.SemaphoreType.DMA
    rows = -(-(L * (taps + 3)) // 16) * 16
    wide = -(-max(conv_part, ng.shape[1], gg.shape[1]) // LANES) * LANES
    outs = [
        sds((tokens, width), F32),
        sds((S, tokens, width), BF),
        sds((8, width), F32),
        sds((L, 8, conv), F32),
        sds((S, 8, tokens), F32),
    ]
    for _ in range(L):
        outs += [
            sds((F, win_raw.shape[1], 2 * il + bc + LANES), BF),
            sds((F,) + wout_raw.shape[2:], BF),
            sds((S, tokens, width), BF),
            sds((length, il), F32),
            sds((length, conv), BF),
            sds((length, LANES), F32),
            sds((length, il), BF),
            sds((length, il), BF),
            sds((tokens, width), F32),
            sds((tokens, width), F32),
            sds((S * 8, tokens), F32),
        ]
    scratch = [pltpu.VMEM((F, rows, wide), BF), pltpu.VMEM((rows, convdim), F32)]
    scratch += [pltpu.VMEM((S, tokens, width), BF) for _ in range(L)]
    scratch += [pltpu.VMEM((S, S * 8, tokens), F32) for _ in range(L)]
    for _ in range(L):
        scratch += Scatter.scratch(S, (tokens, width))
    for n in [F, S, S] + [F] * (2 * L) + [S] * (2 * L):
        scratch += Gather.scratch(n)
    scratch += [sem((L,)), sem((L,)), sem((L,))]
    return comm_call(
        partial(forward_kernel, S, F, L, heads), "forward", 0, outs, scratch,
        (hidden, cot, segr, win_raw, wout_raw, cw, cb, ng, gg, hp),
    )


def mix_backward(total_inner, seg, nrm, win, wout, par, hp, kept, gb, inv, dots, out, hooks):
    z_ref, v_ref, dt_ref, y_ref, sc_ref = kept
    zx_ref, gout_ref, dpart_ref, dbc_ref, ddt_ref, small_ref, dproj = out
    segc, segr, cm = seg
    inner = z_ref.shape[1]
    length, conv = v_ref.shape
    blocks = length // SPAN
    nstate = (conv - inner) // 2

    scaled_in = lax.dot_general(gb, wout[...], (NT, ((), ())), preferred_element_type=F32) * inv
    z = z_ref[...]
    y = y_ref[...].astype(F32)
    sig = sigmoid(z)
    silu = z * sig
    prod = y * silu
    small_ref[5:6, :inner] = jnp.sum(scaled_in * prod, axis=0, keepdims=True)
    d_prod = scaled_in * par[5:6, :inner] - prod * (inv * inv * dots * (1.0 / total_inner))
    dy = d_prod * silu
    dy = dy.astype(BF).astype(F32)
    dproj[:, :inner] = (d_prod * y * (sig * (1.0 + z * (1.0 - sig)))).astype(BF)
    grad_scaled = (gb.astype(F32) * inv).astype(BF)
    put(
        gout_ref,
        lax.dot_general(sc_ref[...], grad_scaled, (TN, ((), ())), preferred_element_type=F32),
    )
    hooks("gout")

    lim = limits(segc, segr)
    v = v_ref[...].astype(F32)
    moved = shifts(v, cm)
    pre = conv_pre(v, moved, par)
    csig = sigmoid(pre)
    act = pre * csig
    x_act = act[:, :inner]
    b_act = act[:, inner : inner + nstate].astype(BF)
    c_act = act[:, inner + nstate :].astype(BF)
    u, delta, decay = decay_of(dt_ref[...], hp)
    cum = cumulate(lim, decay)
    cum_t = [c.T for c in cum]
    hm = head_map(inner)
    delta_bc = hdot(delta, hm, NT)
    xs = x_act * delta_bc
    cb = {k: bdot(c_act[span(k[0])], b_act[span(k[1])], NT) for k in lim}

    lane = lax.broadcasted_iota(jnp.int32, (SPAN, LANES), 1)
    sub = lax.broadcasted_iota(jnp.int32, (LANES, SPAN), 0)
    dcb = {k: jnp.zeros((SPAN, SPAN), F32) for k in lim}
    drow = [jnp.zeros((SPAN, LANES), F32) for _ in range(blocks)]
    dcol = [jnp.zeros((LANES, SPAN), F32) for _ in range(blocks)]
    dxs = []
    for q in range(inner // LANES):
        ql = slice(q * LANES, (q + 1) * LANES)
        pair = xs[:, ql].astype(BF)
        dyp = halves(dy[:, ql])
        dxq = [jnp.zeros((SPAN, LANES), F32) for _ in range(blocks)]
        for i in range(blocks):
            for j in range(i + 1):
                for e in range(2):
                    h = 2 * q + e
                    w = jnp.exp(jnp.minimum(cum[i][:, h : h + 1] - cum_t[j][h : h + 1], lim[i, j]))
                    p = w * cb[i, j]
                    dp = bdot(dyp[e][span(i)], pair[span(j)], NT)
                    dxq[j] = dxq[j] + bdot(p, dyp[e][span(i)], TN)
                    dcb[i, j] = dcb[i, j] + dp * w
                    g = dp * p
                    drow[i] = drow[i] + jnp.where(lane == h, jnp.sum(g, axis=1, keepdims=True), 0.0)
                    dcol[j] = dcol[j] + jnp.where(sub == h, jnp.sum(g, axis=0, keepdims=True), 0.0)
        dxs.append(jnp.concatenate(dxq, axis=0))
        hooks(f"pair{q}")
    dxs = jnp.concatenate(dxs, axis=1)
    db, dc = [], []
    for k in range(blocks):
        db.append(sum(bdot(dcb[i, k], c_act[span(i)], TN) for i in range(k, blocks)))
        dc.append(sum(bdot(dcb[k, j], b_act[span(j)]) for j in range(k + 1)))
    dcum_t = [drow[k].T - dcol[k] for k in range(blocks)]
    ddecay = []
    for j in range(blocks):
        total = None
        for i in range(j, blocks):
            term = hdot(dcum_t[i], (lim[i, j] == 0.0).astype(F32))
            total = term if total is None else total + term
        ddecay.append(total.T)
    ddecay = jnp.concatenate(ddecay, axis=0)
    ddelta = hdot(dxs * x_act, hm) - jnp.exp(hp[0:1]) * ddecay
    ddt = ddelta * sigmoid(u)
    small_ref[6:7, :LANES] = jnp.sum(ddecay * decay, axis=0, keepdims=True)
    small_ref[6:7, LANES : 2 * LANES] = jnp.sum(ddt, axis=0, keepdims=True)
    skip = jnp.broadcast_to(jnp.sum(dy * x_act, axis=0, keepdims=True), (8, inner))
    small_ref[6:7, 2 * LANES : 3 * LANES] = hdot(skip, hm)[:1]
    dx_act = dxs * delta_bc + dy * par[6:7, :inner]
    dact = jnp.concatenate(
        [dx_act, jnp.concatenate(db, axis=0), jnp.concatenate(dc, axis=0)], axis=1
    )

    dpre = dact * (csig * (1.0 + pre * (1.0 - csig)))
    small_ref[4:5, :conv] = jnp.sum(dpre, axis=0, keepdims=True)
    small_ref[3:4, :conv] = jnp.sum(dpre * v, axis=0, keepdims=True)
    dv = par[3:4] * dpre
    for d in range(1, 4):
        small_ref[3 - d : 4 - d, :conv] = jnp.sum(dpre * moved[d - 1], axis=0, keepdims=True)
        back = dpre * cm[:, d - 1 : d] * par[3 - d : 4 - d]
        dv = dv + pltpu.roll(back, length - d, 0)
    heads = inner // HEADDIM
    real = lax.broadcasted_iota(jnp.int32, (length, LANES), 1) < heads
    ddt = jnp.where(real, ddt, 0.0)
    dproj[:, inner : inner + conv] = dv.astype(BF)
    dproj[:, inner + conv :] = ddt.astype(BF)
    put(dbc_ref, dv[:, inner:].T)
    ddt_ref[...] = ddt.T[: ddt_ref.shape[0]].astype(BF)
    put(
        dpart_ref,
        lax.dot_general(dproj[...], win[...], (NT, ((), ())), preferred_element_type=F32),
    )
    hooks("dpart")
    put(
        zx_ref,
        lax.dot_general(
            nrm[...], dproj[:, : 2 * inner], (TN, ((), ())), preferred_element_type=F32
        ),
    )
    hooks("gin")


BACKWARD_INS = ("nrm", "win", "wout", "z", "v", "dt", "y", "sc", "inv", "prior")


def backward_kernel(S, F, L, total_inner, *refs):
    take = Take(refs)
    cot, segr_ref, gb_last, dots_last, gains, par_ref, hp_ref = take(7)
    ins = [dict(zip(BACKWARD_INS, take(len(BACKWARD_INS)))) for _ in range(L)]
    deltas = take(L)
    input_grad, small_out = take(2)
    outs = [take(3) for _ in range(L)]
    jobs = [take(3) for _ in range(L)]
    dparts, dbcs, ddts = take(L), take(L), take(L)
    gbs, dotss = take(L - 1), take(L - 1)
    dproj, small, out_mid = take(), take(), take(L)
    scat = [[Scatter("fsdp", F, jobs[l][k], take(N_SCATTER)) for k in range(3)] for l in range(L)]
    sc = [Scatter("seq", S, dparts[l], take(N_SCATTER)) for l in range(L)]
    sb = [Scatter("seq", S, dbcs[l], take(N_SCATTER)) for l in range(L)]
    g_gb = [Gather("seq", S, gbs[l], take(2)) for l in range(L - 1)]
    g_dots = [Gather("seq", S, dotss[l], take(2)) for l in range(L - 1)]
    g_job = [[Gather("seq", S, outs[l][k], take(2)) for k in range(3)] for l in range(L)]
    g_small = Gather("seq", S, small_out, take(2))
    perm_send, perm_recv = take(2)
    sm_row, sm_mid, sm_col, sm_s1, sm_r1, sm_s2, sm_r2 = take(7)

    s, f = lax.axis_index("seq"), lax.axis_index("fsdp")
    a_n, b_n = factor(F)
    a, b = f // b_n, f % b_n
    flat_id = f * S + s
    own = s * F + f
    target = (own % S, own // S)
    source = (flat_id // F, flat_id % F)
    moved = flat_id != own
    barrier([("fsdp", F), ("seq", S)], (source, moved))

    def perm(l):
        return pltpu.make_async_remote_copy(
            src_ref=out_mid[l],
            dst_ref=outs[l][2].at[own % S],
            send_sem=perm_send.at[l],
            recv_sem=perm_recv.at[l],
            device_id=target,
            device_id_type=MESH,
        )

    def row(db):
        return pltpu.make_async_remote_copy(
            src_ref=small,
            dst_ref=sm_row.at[db],
            send_sem=sm_s1.at[db],
            recv_sem=sm_r1.at[db],
            device_id=(s, a * b_n + lax.rem(b + db, b_n)),
            device_id_type=MESH,
        )

    def col(da, sender=True):
        at = a if sender else lax.rem(a + a_n - da, a_n)
        return pltpu.make_async_remote_copy(
            src_ref=sm_mid,
            dst_ref=sm_col.at[at],
            send_sem=sm_s2.at[da],
            recv_sem=sm_r2.at[da],
            device_id=(s, lax.rem(a + da, a_n) * b_n + b),
            device_id_type=MESH,
        )

    def out_done(l):
        value = scat[l][2].finish().astype(BF)
        out_mid[l][...] = value

        @pl.when(moved)
        def _():
            perm(l).start()

        @pl.when(jnp.logical_not(moved))
        def _():
            outs[l][2][s] = value

    def out_gather(l):
        @pl.when(moved)
        def _():
            perm(l).wait()

        g_job[l][2].start()

    def job_done(l, k):
        outs[l][k][s] = scat[l][k].finish().astype(BF)
        g_job[l][k].start()

    seg = seg_parts(segr_ref)
    small[...] = jnp.zeros_like(small)
    pairs = ins[0]["z"].shape[1] // LANES

    for l in reversed(range(L)):
        x = ins[l]
        base = 16 * l
        if l == L - 1:
            gb_ref, dots_ref = gb_last, dots_last
        else:
            gb_ref, dots_ref = gbs[l], dotss[l]

        def hooks(stage, l=l):
            if stage == "gout":
                scat[l][2].start()
                if l < L - 1:
                    out_done(l + 1)
                    scat[l + 1][0].middle()
                    scat[l + 1][1].middle()
            if stage == f"pair{pairs - 1}":
                scat[l][2].middle()
                if l < L - 1:
                    out_gather(l + 1)
            if stage == "dpart":
                sb[l].start()
                sc[l].start()
            if stage == "gin":
                scat[l][0].start()

        inv = jnp.concatenate([as_col(x["inv"][8 * k : 8 * k + 1]) for k in range(S)], axis=0)
        dots = jnp.concatenate([as_col(dots_ref[k][:1]) for k in range(S)], axis=0)
        mix_backward(
            total_inner, seg, x["nrm"], x["win"], x["wout"], par_ref[l], hp_ref[l],
            (x["z"], x["v"], x["dt"], x["y"], x["sc"]), flat(gb_ref), inv, dots,
            (jobs[l][0], jobs[l][2], dparts[l], dbcs[l], ddts[l], small.at[base : base + 8], dproj),
            hooks,
        )
        sb[l].middle()
        sc[l].middle()
        u = x["prior"][...]
        n = lax.rsqrt(jnp.mean(u * u, axis=-1, keepdims=True) + EPS)
        xhat = u * n
        tail = jnp.concatenate([sb[l].finish().astype(BF), ddts[l][...]], axis=0)
        put(
            jobs[l][1],
            lax.dot_general(
                x["nrm"][...], tail, (((0,), (1,)), ((), ())), preferred_element_type=F32
            ),
        )
        scat[l][1].start()
        dn = sc[l].finish()
        small[base + 8 : base + 9] = jnp.sum(dn * xhat, axis=0, keepdims=True)
        t = dn * gains[l : l + 1]
        g_ref = cot if l == L - 1 else input_grad
        new = g_ref[...] + n * (t - xhat * jnp.mean(t * xhat, axis=-1, keepdims=True))
        input_grad[...] = new
        if l > 0:
            gb = new.astype(BF)
            gbs[l - 1][s] = gb
            dotss[l - 1][s] = as_row(
                jnp.sum(gb.astype(F32) * deltas[l - 1][...], axis=1, keepdims=True)
            )
            for g in (g_gb[l - 1], g_dots[l - 1]):
                g.start()
            for g in (g_gb[l - 1], g_dots[l - 1]):
                g.forwards()
            for g in (g_gb[l - 1], g_dots[l - 1]):
                g.finish()

    for db in range(1, b_n):
        row(db).start()
    for l in range(1, L):
        job_done(l, 0)
        job_done(l, 1)
    scat[0][0].middle()
    scat[0][1].middle()
    sm_row[0] = small[...]
    for db in range(1, b_n):
        row(db).wait_recv()
    total = None
    for k in range(b_n):
        term = sm_row[lax.rem(b + b_n - k, b_n)]
        total = term if total is None else total + term
    sm_mid[...] = total
    for da in range(1, a_n):
        col(da).start()
    out_done(0)
    for l in range(1, L):
        for g in g_job[l]:
            g.forwards()
    out_gather(0)
    sm_col[a] = sm_mid[...]
    for da in range(1, a_n):
        col(da, False).wait_recv()
    small_out[s] = jnp.sum(sm_col[...], axis=0)
    g_small.start()
    job_done(0, 0)
    job_done(0, 1)
    g_job[0][2].forwards()
    g_small.forwards()
    g_job[0][0].forwards()
    g_job[0][1].forwards()
    for l in range(L):
        for g in g_job[l]:
            g.finish()
    g_small.finish()
    for db in range(1, b_n):
        row(db).wait_send()
    for da in range(1, a_n):
        col(da).wait_send()


def backward(S, F, total_inner, cot, segr, gb_last, dots_last, gains, par, hp, layers, deltas):
    L = len(layers)
    tokens, width = cot.shape
    length, il = layers[0]["z"].shape
    conv = layers[0]["v"].shape[1]
    bc = conv - il
    bl = bc // S
    a_n, b_n = factor(F)
    sem = pltpu.SemaphoreType.DMA
    shapes = [(width // F, 2 * il), (width // F, LANES), (il // F, width)]
    outs = [sds((tokens, width), F32), sds((S, 16 * L, width), F32)]
    for _ in range(L):
        outs += [sds((S,) + shape, BF) for shape in shapes]
    scratch = []
    for _ in range(L):
        scratch += [pltpu.VMEM((F,) + shape, BF) for shape in shapes]
    scratch += [pltpu.VMEM((S, tokens, width), BF) for _ in range(L)]
    scratch += [pltpu.VMEM((S, bl, length), BF) for _ in range(L)]
    scratch += [pltpu.VMEM((LANES - bl, length), BF) for _ in range(L)]
    scratch += [pltpu.VMEM((S, tokens, width), BF) for _ in range(L - 1)]
    scratch += [pltpu.VMEM((S, 8, tokens), F32) for _ in range(L - 1)]
    scratch += [pltpu.VMEM((length, il + conv + LANES), BF), pltpu.VMEM((16 * L, width), F32)]
    scratch += [pltpu.VMEM(shapes[2], BF) for _ in range(L)]
    for _ in range(L):
        for shape in shapes:
            scratch += Scatter.scratch(F, shape)
    for _ in range(L):
        scratch += Scatter.scratch(S, (tokens, width))
    for _ in range(L):
        scratch += Scatter.scratch(S, (bl, length))
    for _ in range(2 * (L - 1) + 3 * L + 1):
        scratch += Gather.scratch(S)
    scratch += [sem((L,)), sem((L,))]
    scratch += [
        pltpu.VMEM((b_n, 16 * L, width), F32),
        pltpu.VMEM((16 * L, width), F32),
        pltpu.VMEM((a_n, 16 * L, width), F32),
        sem((b_n,)), sem((b_n,)), sem((a_n,)), sem((a_n,)),
    ]
    args = [cot, segr, gb_last, dots_last, gains, par, hp]
    for x in layers:
        args += [x[k] for k in BACKWARD_INS]
    args += deltas
    return comm_call(
        partial(backward_kernel, S, F, L, total_inner), "backward", 1, outs, scratch, args
    )


def finish_kernel(S, F, L, heads, *refs):
    take = Take(refs)
    sums = take()
    jobs = [take(3) for _ in range(L)]
    gin, gout, gcw, gcb, gng, ggg, gal, gdb, gds = take(9)
    f = lax.axis_index("fsdp")
    taps, conv_part = gcw.shape[1:]
    width_part, inner_part = gng.shape[1], ggg.shape[1]
    inner, convdim = inner_part * F, conv_part * F
    il, hl = inner // S, heads // S
    bc = convdim - inner
    bl = bc // S

    def own(x, part):
        n = x.shape[1]
        return pltpu.roll(x, lax.rem(n - f * part, n), 1)[:, :part]

    for l in range(L):
        zx, tail, out = jobs[l]
        for s in range(S):
            gin[l, :, s * il : (s + 1) * il] = zx[s, :, :il].astype(F32)
            gin[l, :, inner + s * il : inner + (s + 1) * il] = zx[s, :, il:].astype(F32)
        tails = [tail[s].astype(F32) for s in range(S)]
        gin[l, :, 2 * inner : 2 * inner + bc] = jnp.concatenate([t[:, :bl] for t in tails], axis=1)
        gin[l, :, 2 * inner + bc :] = jnp.concatenate([t[:, bl : bl + hl] for t in tails], axis=1)
        rows = out.shape[1]
        for s in range(S):
            gout[l, s * rows : (s + 1) * rows] = out[s].astype(F32)
        base = 16 * l
        low = [sums[s, base : base + 8] for s in range(S)]
        xs = jnp.concatenate([t[:, :il] for t in low], axis=1)
        both = sum(t[:, il : il + bc] for t in low)
        five = own(jnp.concatenate([xs, both], axis=1), conv_part)
        gcw[l] = five[:taps]
        gcb[l : l + 1] = five[taps : taps + 1]
        ggg[l : l + 1] = own(xs, inner_part)[5:6]
        gng[l : l + 1] = own(sum(sums[s, base + 8 : base + 16] for s in range(S)), width_part)[:1]
        for k, ref in enumerate((gal, gdb, gds)):
            ref[l : l + 1] = jnp.concatenate(
                [t[6:7, k * LANES : k * LANES + hl] for t in low], axis=1
            )


def body(
    hidden, cotangent, segments, in_weight, out_weight, conv_weight, conv_bias,
    norm_gain, gate_gain, a_log, dt_bias, d_skip,
):
    seq_idx = lax.axis_index("seq")
    S = lax.axis_size("seq")
    F = lax.axis_size("fsdp")
    tokens, width = hidden.shape[1:]
    L = in_weight.shape[0]
    heads = a_log.shape[1]
    hl = heads // S
    inner = gate_gain.shape[1] * F
    length = segments.shape[1]

    hp = lax.dynamic_slice_in_dim(jnp.stack([a_log, dt_bias, d_skip], axis=1), seq_idx * hl, hl, 2)
    hp = jnp.pad(hp, ((0, 0), (0, 5), (0, LANES - hl)))
    wout_raw = out_weight.reshape(L, S, out_weight.shape[1] // S, width)
    hid, cot = hidden[0], cotangent[0]
    got = forward(
        S, F, heads, hid, cot, segments, in_weight, wout_raw,
        conv_weight, conv_bias, norm_gain, gate_gain, hp,
    )
    hidden_out, gb_all, gains, par, dots_all = got[:5]
    layers = []
    for l in range(L):
        n = len(FORWARD_OUTS)
        layers.append(dict(zip(FORWARD_OUTS, got[5 + l * n : 5 + (l + 1) * n])))
    deltas = [x["delta"] for x in layers]
    for l, x in enumerate(layers):
        x["prior"] = hid if l == 0 else layers[l - 1]["new"]
        x["nrm"] = x["nrm"].reshape(length, width)
        x["win"] = x["win"].reshape(width, -1)
        x["wout"] = x["wout"].reshape(-1, width)
    got = backward(S, F, inner, cot, segments, gb_all, dots_all, gains, par, hp, layers, deltas)
    outs = [
        sds(in_weight.shape, F32),
        sds(out_weight.shape, F32),
        sds(conv_weight.shape, F32),
        sds(conv_bias.shape, F32),
        sds(norm_gain.shape, F32),
        sds(gate_gain.shape, F32),
    ] + [sds(a_log.shape, F32)] * 3
    final = local_call(partial(finish_kernel, S, F, L, heads), "finish", outs, got[1:])
    return (hidden_out[None], got[0][None], *final)


def solution(mesh):
    token = P("fsdp", "seq", None)
    rows = P(None, "fsdp", None)
    split = P(None, "fsdp")
    taps = P(None, None, "fsdp")
    return jax.shard_map(
        body,
        mesh=mesh,
        in_specs=(
            token, token, P("fsdp", None), rows, rows, taps, split, split, split, P(), P(), P(),
        ),
        out_specs=(token, token, rows, rows, taps, split, split, split, P(), P(), P()),
        check_vma=False,
    )
```

```python
from functools import partial

import jax
import jax.numpy as jnp
from jax import lax
from jax.experimental import pallas as pl
from jax.experimental.pallas import tpu as pltpu
from jax.sharding import PartitionSpec as P

HEADDIM = 64
SPAN = 256
EPS = 1e-05
HIGH = lax.Precision.HIGHEST
BF = jnp.bfloat16
F32 = jnp.float32
MESH = pl.DeviceIdType.MESH
NEGATIVE = -1e30
LANES = 128
VMEM_LIMIT = 60 * 1024 * 1024


def factor(n):
    b = 1
    while (2 * b) * (2 * b) <= n:
        b *= 2
    return n // b, b


def peers_of(axis, n):
    a_n, b_n = factor(n)
    s, f = lax.axis_index("seq"), lax.axis_index("fsdp")
    i = s if axis == "seq" else f
    a, b = i // b_n, i % b_n

    def dev(k):
        return (k, f) if axis == "seq" else (s, k)

    out = []
    for da in range(1, a_n):
        out.append(dev(lax.rem(a + da, a_n) * b_n + b))
    for db in range(1, b_n):
        out.append(dev(a * b_n + lax.rem(b + db, b_n)))
    return out


def barrier(groups, extra=None):
    sem = pltpu.get_barrier_semaphore()
    devices = [d for axis, n in groups for d in peers_of(axis, n)]
    for d in devices:
        pl.semaphore_signal(sem, inc=1, device_id=d, device_id_type=MESH)
    if extra is None:
        pl.semaphore_wait(sem, len(devices))
        return
    source, moved = extra

    @pl.when(moved)
    def _():
        pl.semaphore_signal(sem, inc=1, device_id=source, device_id_type=MESH)

    pl.semaphore_wait(sem, len(devices) + moved.astype(jnp.int32))


class Gather:
    def __init__(self, axis, n, ref, sems):
        self.n = n
        self.a_n, self.b_n = factor(n)
        s, f = lax.axis_index("seq"), lax.axis_index("fsdp")
        i = s if axis == "seq" else f
        self.a, self.b = i // self.b_n, i % self.b_n
        self.dev = (lambda k: (k, f)) if axis == "seq" else (lambda k: (s, k))
        self.ref = ref
        self.send, self.recv = sems

    @staticmethod
    def scratch(n):
        a_n, b_n = factor(n)
        count = a_n * b_n
        return [pltpu.SemaphoreType.DMA((count,)), pltpu.SemaphoreType.DMA((count,))]

    def _first(self, da, sender):
        a = self.a if sender else lax.rem(self.a + self.a_n - da, self.a_n)
        block = a * self.b_n + self.b
        return pltpu.make_async_remote_copy(
            src_ref=self.ref.at[block],
            dst_ref=self.ref.at[block],
            send_sem=self.send.at[da * self.b_n],
            recv_sem=self.recv.at[da * self.b_n],
            device_id=self.dev(lax.rem(self.a + da, self.a_n) * self.b_n + self.b),
            device_id_type=MESH,
        )

    def _second(self, da, db, sender):
        a = lax.rem(self.a + self.a_n - da, self.a_n)
        b = self.b if sender else lax.rem(self.b + self.b_n - db, self.b_n)
        block = a * self.b_n + b
        return pltpu.make_async_remote_copy(
            src_ref=self.ref.at[block],
            dst_ref=self.ref.at[block],
            send_sem=self.send.at[da * self.b_n + db],
            recv_sem=self.recv.at[da * self.b_n + db],
            device_id=self.dev(self.a * self.b_n + lax.rem(self.b + db, self.b_n)),
            device_id_type=MESH,
        )

    def start_columns(self):
        for da in range(1, self.a_n):
            self._first(da, True).start()

    def start_rows(self):
        for db in range(1, self.b_n):
            self._second(0, db, True).start()

    def start(self):
        self.start_columns()
        self.start_rows()

    def forward(self, da):
        self._first(da, False).wait_recv()
        for db in range(1, self.b_n):
            self._second(da, db, True).start()

    def forwards(self):
        for da in range(1, self.a_n):
            self.forward(da)

    def finish(self):
        for da in range(self.a_n):
            for db in range(1, self.b_n):
                self._second(da, db, False).wait_recv()
        for da in range(1, self.a_n):
            self._first(da, True).wait_send()
        for da in range(self.a_n):
            for db in range(1, self.b_n):
                self._second(da, db, True).wait_send()


class Line(Gather):
    @staticmethod
    def scratch(n):
        a_n, b_n = factor(n)
        count = 2 * a_n + a_n * b_n
        return [pltpu.SemaphoreType.DMA((count,)), pltpu.SemaphoreType.DMA((count,))]

    def _copy(self, block, k, device):
        return pltpu.make_async_remote_copy(
            src_ref=self.ref.at[block],
            dst_ref=self.ref.at[block],
            send_sem=self.send.at[k],
            recv_sem=self.recv.at[k],
            device_id=self.dev(device),
            device_id_type=MESH,
        )

    def _step(self, way, k):
        to = self.a + way
        slot = k if way > 0 else self.a_n + k
        return self._copy((to - way * k) * self.b_n + self.b, slot, to * self.b_n + self.b)

    def _row(self, a, db, sender):
        b = self.b if sender else lax.rem(self.b + self.b_n - db, self.b_n)
        slot = 2 * self.a_n + a * self.b_n + db
        device = self.a * self.b_n + lax.rem(self.b + db, self.b_n)
        return self._copy(a * self.b_n + b, slot, device)

    def _may(self, way, k):
        if way > 0:
            return (self.a + 1 < self.a_n) & (self.a + 1 >= k)
        return (self.a >= 1) & (self.a - 1 + k < self.a_n)

    def start_columns(self):
        for way in (1, -1):

            @pl.when(self._may(way, 1))
            def _():
                self._step(way, 1).start()

    def start_rows(self):
        for db in range(1, self.b_n):
            self._row(self.a, db, True).start()

    def forward(self, k):
        for way in (1, -1):
            block = self.a - way * k
            here = (block >= 0) & (block < self.a_n)

            @pl.when(here)
            def _():
                slot = k if way > 0 else self.a_n + k
                sender = (self.a - way) * self.b_n + self.b
                self._copy(block * self.b_n + self.b, slot, sender).wait_recv()
                if k + 1 < self.a_n:

                    @pl.when(self._may(way, k + 1))
                    def _():
                        self._step(way, k + 1).start()

                for db in range(1, self.b_n):
                    self._row(block, db, True).start()

    def finish(self):
        for a in range(self.a_n):
            for db in range(1, self.b_n):
                self._row(a, db, False).wait_recv()
        for k in range(1, self.a_n):
            for way in (1, -1):

                @pl.when(self._may(way, k))
                def _():
                    self._step(way, k).wait_send()

        for a in range(self.a_n):
            for db in range(1, self.b_n):
                self._row(a, db, True).wait_send()


class Scatter:
    def __init__(self, axis, n, ref, scratch):
        self.a_n, self.b_n = factor(n)
        s, f = lax.axis_index("seq"), lax.axis_index("fsdp")
        i = s if axis == "seq" else f
        self.a, self.b = i // self.b_n, i % self.b_n
        self.dev = (lambda k: (k, f)) if axis == "seq" else (lambda k: (s, k))
        self.ref = ref
        self.row_in, self.mid, self.col_in, self.send, self.recv, self.send2, self.recv2 = scratch

    @staticmethod
    def scratch(n, shape, dtype=BF):
        a_n, b_n = factor(n)
        sem = pltpu.SemaphoreType.DMA
        return [
            pltpu.VMEM((a_n, b_n - 1) + shape, dtype),
            pltpu.VMEM((a_n,) + shape, dtype),
            pltpu.VMEM((a_n - 1,) + shape, dtype),
            sem((a_n, b_n - 1)),
            sem((a_n, b_n - 1)),
            sem((a_n,)),
            sem((a_n,)),
        ]

    def _row(self, da, db):
        a = lax.rem(self.a + da, self.a_n)
        b = lax.rem(self.b + db, self.b_n)
        return pltpu.make_async_remote_copy(
            src_ref=self.ref.at[a * self.b_n + b],
            dst_ref=self.row_in.at[da, db - 1],
            send_sem=self.send.at[da, db - 1],
            recv_sem=self.recv.at[da, db - 1],
            device_id=self.dev(self.a * self.b_n + b),
            device_id_type=MESH,
        )

    def _col(self, da):
        a = lax.rem(self.a + da, self.a_n)
        return pltpu.make_async_remote_copy(
            src_ref=self.mid.at[da],
            dst_ref=self.col_in.at[da - 1],
            send_sem=self.send2.at[da],
            recv_sem=self.recv2.at[da],
            device_id=self.dev(a * self.b_n + self.b),
            device_id_type=MESH,
        )

    def start(self):
        for da in list(range(1, self.a_n)) + [0]:
            for db in range(1, self.b_n):
                self._row(da, db).start()

    def _sum(self, da):
        a = lax.rem(self.a + da, self.a_n)
        for db in range(1, self.b_n):
            self._row(da, db).wait_recv()
        total = self.ref[a * self.b_n + self.b].astype(F32)
        for db in range(1, self.b_n):
            total = total + self.row_in[da, db - 1].astype(F32)
        return total

    def middle(self):
        for da in range(1, self.a_n):
            self.mid[da] = self._sum(da).astype(self.mid.dtype)
            self._col(da).start()

    def finish(self):
        total = self._sum(0)
        for da in range(1, self.a_n):
            self._col(da).wait_recv()
            total = total + self.col_in[da - 1].astype(F32)
        for da in range(self.a_n):
            for db in range(1, self.b_n):
                self._row(da, db).wait_send()
        for da in range(1, self.a_n):
            self._col(da).wait_send()
        return total


N_SCATTER = 7


def comm_call(kernel, name, collective_id, outs, scratch, args, in_spaces=None, out_spaces=None):
    def specs(spaces, n):
        spaces = spaces or [pltpu.VMEM] * n
        return [pl.BlockSpec(memory_space=x) for x in spaces]

    return pl.pallas_call(
        kernel,
        name=name,
        out_shape=outs,
        in_specs=specs(in_spaces, len(args)),
        out_specs=specs(out_spaces, len(outs)),
        scratch_shapes=scratch,
        compiler_params=pltpu.CompilerParams(
            collective_id=collective_id, has_side_effects=True, vmem_limit_bytes=VMEM_LIMIT
        ),
    )(*args)


def local_call(kernel, name, outs, args):
    spec = pl.BlockSpec(memory_space=pltpu.VMEM)
    return pl.pallas_call(
        kernel,
        name=name,
        out_shape=outs,
        in_specs=[spec] * len(args),
        out_specs=[spec] * len(outs),
        compiler_params=pltpu.CompilerParams(vmem_limit_bytes=VMEM_LIMIT),
    )(*args)


def sds(shape, dtype):
    return jax.ShapeDtypeStruct(shape, dtype)


def as_row(col):
    t = col.shape[0]
    return jnp.broadcast_to(col, (t, LANES)).T[:8]


def as_col(row):
    t = row.shape[1]
    return jnp.broadcast_to(row, (LANES, t)).T[:, :1]


def norm_of(u, gain):
    return u * lax.rsqrt(jnp.mean(u * u, axis=-1, keepdims=True) + EPS) * gain


def bdot(x, y, dims=((1,), (0,))):
    return lax.dot_general(
        x.astype(BF), y.astype(BF), (dims, ((), ())), preferred_element_type=F32
    )


def hdot(x, y, dims=((1,), (0,))):
    return lax.dot_general(x, y, (dims, ((), ())), precision=HIGH, preferred_element_type=F32)


NT = ((1,), (1,))
TN = ((0,), (0,))


def span(i):
    return slice(i * SPAN, (i + 1) * SPAN)


def limits(segc, segr):
    blocks = segc.shape[0] // SPAN
    rows = lax.broadcasted_iota(jnp.int32, (SPAN, SPAN), 0)
    cols = lax.broadcasted_iota(jnp.int32, (SPAN, SPAN), 1)
    out = {}
    for i in range(blocks):
        for j in range(i + 1):
            kept = segc[span(i)] == segr[:, span(j)]
            if i == j:
                kept = kept & (rows >= cols)
            out[i, j] = jnp.where(kept, 0.0, NEGATIVE)
    return out


def head_map(inner):
    rows = lax.broadcasted_iota(jnp.int32, (inner, LANES), 0)
    cols = lax.broadcasted_iota(jnp.int32, (inner, LANES), 1)
    return ((rows // HEADDIM) == cols).astype(F32)


def shifts(v, cm):
    return [pltpu.roll(v, d, 0) * cm[:, d - 1 : d] for d in range(1, 4)]


def conv_pre(v, moved, par):
    pre = par[4:5] + par[3:4] * v
    for d in range(1, 4):
        pre = pre + par[3 - d : 4 - d] * moved[d - 1]
    return pre


def sigmoid(x):
    return 1.0 / (1.0 + jnp.exp(-x))


def softplus(x):
    return jnp.maximum(x, 0.0) + jnp.log1p(jnp.exp(-jnp.abs(x)))


def decay_of(dt, hp):
    u = dt + hp[1:2]
    delta = softplus(u)
    return u, delta, -jnp.exp(hp[0:1]) * delta


def cumulate(lim, decay):
    blocks = decay.shape[0] // SPAN
    out = []
    for i in range(blocks):
        total = None
        for j in range(i + 1):
            term = hdot((lim[i, j] == 0.0).astype(F32), decay[span(j)])
            total = term if total is None else total + term
        out.append(total)
    return out


def halves(pair):
    lane = lax.broadcasted_iota(jnp.int32, pair.shape, 1)
    low = lane < HEADDIM
    return jnp.where(low, pair, 0.0).astype(BF), jnp.where(low, 0.0, pair).astype(BF)


class Take:
    def __init__(self, refs):
        self.refs = list(refs)

    def __call__(self, n=None):
        if n is None:
            return self.refs.pop(0)
        got, self.refs = self.refs[:n], self.refs[n:]
        return got


def flat(ref):
    f, rows, cols = ref.shape
    if rows % 16 == 0:
        return ref[...].reshape(f * rows, cols)
    return jnp.concatenate([ref[k].astype(F32) for k in range(f)], axis=0).astype(ref.dtype)


def put(ref, value):
    rows = ref.shape[1]
    for k in range(ref.shape[0]):
        ref[k] = value[k * rows : (k + 1) * rows].astype(ref.dtype)


def seg_parts(segr_ref):
    row = segr_ref[...].astype(F32)
    length = row.shape[1]
    wide = jnp.broadcast_to(row, (LANES, length)).T
    pos = lax.broadcasted_iota(jnp.int32, (length, LANES), 0)
    cm = []
    for d in range(1, 4):
        same = (pltpu.roll(wide, d, 0) == wide) & (pos >= d)
        cm.append(same.astype(F32)[:, :1])
    return wide[:, :1], row, jnp.concatenate(cm, axis=1)


def mix_forward(seg, nrm, win, wsh, wout, par, hp, out, hooks):
    part_ref, sq_ref, z_ref, v_ref, dt_ref, y_ref, sc_ref = out
    segc, segr, cm = seg
    inner = z_ref.shape[1]
    length, conv = v_ref.shape
    blocks = length // SPAN
    x = flat(nrm)
    w = flat(win)
    z_ref[...] = jnp.dot(x, w[:, :inner], preferred_element_type=F32)
    v_ref[:, :inner] = jnp.dot(x, w[:, inner:], preferred_element_type=F32).astype(BF)
    hooks("projected")
    shared = jnp.dot(x, wsh[...], preferred_element_type=F32)
    v_ref[:, inner:] = shared[:, : conv - inner].astype(BF)
    dt = shared[:, conv - inner :].astype(BF).astype(F32)
    dt_ref[...] = dt
    lim = limits(segc, segr)
    v = v_ref[...].astype(F32)
    pre = conv_pre(v, shifts(v, cm), par)
    act = pre * sigmoid(pre)
    x_act = act[:, :inner]
    nstate = (conv - inner) // 2
    b_act = act[:, inner : inner + nstate].astype(BF)
    c_act = act[:, inner + nstate :].astype(BF)
    u, delta, decay = decay_of(dt, hp)
    cum = cumulate(lim, decay)
    cum_t = [c.T for c in cum]
    hm = head_map(inner)
    xs = x_act * hdot(delta, hm, NT)
    cb = {k: bdot(c_act[span(k[0])], b_act[span(k[1])], NT) for k in lim}
    for q in range(inner // LANES):
        ql = slice(q * LANES, (q + 1) * LANES)
        pair = halves(xs[:, ql])
        for i in range(blocks):
            total = par[6:7, ql] * x_act[span(i), ql]
            for j in range(i + 1):
                for e in range(2):
                    h = 2 * q + e
                    g = jnp.exp(jnp.minimum(cum[i][:, h : h + 1] - cum_t[j][h : h + 1], lim[i, j]))
                    total = total + bdot(g * cb[i, j], pair[e][span(j)])
            y_ref[span(i), ql] = total.astype(BF)
    hooks("mixed")
    z = z_ref[...]
    prod = y_ref[...].astype(F32) * (z * sigmoid(z))
    square = jnp.sum(prod * prod, axis=1, keepdims=True)
    tokens = sq_ref.shape[1]
    for k in range(sq_ref.shape[0] // 8):
        sq_ref[8 * k : 8 * k + 8] = as_row(square[k * tokens : (k + 1) * tokens])
    sc_ref[...] = (prod * par[5:6, :inner]).astype(BF)
    hooks("gated")
    put(part_ref, jnp.dot(sc_ref[...], flat(wout), preferred_element_type=F32))


def forward_kernel(S, F, L, heads, *refs):
    take = Take(refs)
    hidden, cot, segr_ref, win_raw, wout_raw, cw, cb, ng, gg, hp_ref = take(10)
    hidden_out, gb_all, gains, par_ref, dots_all = take(5)
    per = [dict(zip(KEPT, take(len(KEPT)))) for _ in range(L)]
    stored = [take(len(STORED)) for _ in range(L)]
    small_all, full = take(2)
    parts, sq_all = take(L), take(L)
    scs = [take(N_SCATTER) for _ in range(L)]
    shared, shared32 = take(L), take()
    stores = []
    for l in range(L):
        for k, ref in zip(STORED, take(len(STORED))):
            per[l][k] = ref
        sem = take()
        stores.append(
            [
                pltpu.make_async_copy(per[l][k], stored[l][i], sem.at[i])
                for i, k in enumerate(STORED)
            ]
        )

    def sems():
        return take(2)

    s, f = lax.axis_index("seq"), lax.axis_index("fsdp")
    g_small = Gather("fsdp", F, small_all, sems())
    g_cot = Gather("seq", S, gb_all, sems())
    g_dots = Gather("seq", S, dots_all, sems())
    g_in = [
        (Line if l == 0 else Gather)("fsdp", F, per[l]["win"], sems()) for l in range(L)
    ]
    g_out = [Gather("fsdp", F, per[l]["wout"], sems()) for l in range(L)]
    g_nrm = [Gather("seq", S, per[l]["nrm"], sems()) for l in range(L)]
    g_sq = [Gather("seq", S, sq_all[l], sems()) for l in range(L)]
    g_part = [Gather("fsdp", F, shared[l].at[s], sems()) for l in range(L)]
    g_shared = [Gather("seq", S, shared[l], sems()) for l in range(L)]
    perm_send, perm_recv, perm_stay = take(3)

    flat_id = f * S + s
    own = s * F + f
    target = (flat_id // F, flat_id % F)
    source = (own % S, own // S)
    moved = flat_id != own
    barrier([("fsdp", F), ("seq", S)], (source, moved))

    taps, conv_part = cw.shape[1:]
    width_part, inner_part = ng.shape[1], gg.shape[1]
    inner, convdim = inner_part * F, conv_part * F
    il, hl = inner // S, heads // S
    bc = convdim - inner

    def perm(l):
        return pltpu.make_async_remote_copy(
            src_ref=wout_raw.at[l, s],
            dst_ref=per[l]["wout"].at[flat_id % F],
            send_sem=perm_send.at[l],
            recv_sem=perm_recv.at[l],
            device_id=target,
            device_id_type=MESH,
        )

    def stay(l):
        return pltpu.make_async_copy(
            wout_raw.at[l, s], per[l]["wout"].at[f], perm_stay.at[l]
        )

    def perm_start(l):
        @pl.when(moved)
        def _():
            perm(l).start()

        @pl.when(jnp.logical_not(moved))
        def _():
            stay(l).start()

    def perm_wait(l):
        @pl.when(moved)
        def _():
            perm(l).wait()

        @pl.when(jnp.logical_not(moved))
        def _():
            stay(l).wait()

    for l in range(L):
        perm_start(l)
    wide = small_all.shape[2]

    def lanes(x):
        x = x.astype(F32)
        if x.shape[1] == wide:
            return x
        return jnp.concatenate([x, jnp.zeros((x.shape[0], wide - x.shape[1]), F32)], axis=1)

    rows = [lanes(cw[l]) for l in range(L)] + [lanes(cb[...]), lanes(ng[...]), lanes(gg[...])]
    count = L * (taps + 3)
    rows.append(jnp.zeros((small_all.shape[1] - count, wide), F32))
    small_all[f] = jnp.concatenate(rows, axis=0).astype(BF)
    g_small.start()

    block_rows = win_raw.shape[1]
    part_rows = block_rows // S
    high, breadth = shared[0].shape[2:]

    def block(l):
        start = pl.multiple_of(s * il, LANES)
        dst = per[l]["win"]
        dst[f, :, :il] = win_raw[l, :, pl.ds(start, il)]
        dst[f, :, il:] = win_raw[l, :, pl.ds(pl.multiple_of(inner + start, LANES), il)]

    def part(l):
        tail = win_raw[l, :, 2 * inner :].astype(F32)
        tail = jnp.concatenate(
            [tail, jnp.zeros((block_rows, breadth - tail.shape[1]), F32)], axis=1
        )
        for q in range(S):
            rows = tail[q * part_rows : (q + 1) * part_rows]
            if high > part_rows:
                rows = jnp.concatenate([rows, jnp.zeros((high - part_rows, breadth), F32)], axis=0)

            @pl.when(s == q)
            def _():
                shared[l][q, f] = rows.astype(BF)

    def assemble(l):
        for k in range(F):
            for q in range(S):
                row = k * block_rows + q * part_rows
                shared32[row : row + part_rows] = shared[l][q, k].astype(F32)[:part_rows]
        out = per[l]["wsh"]
        out[:, :bc] = shared32[:, :bc].astype(BF)
        tail = pltpu.roll(shared32[:, bc:], lax.rem(LANES - s * hl, LANES), 1)
        lane = lax.broadcasted_iota(jnp.int32, tail.shape, 1)
        out[:, bc:] = jnp.where(lane < hl, tail, 0.0).astype(BF)

    part(0)
    g_part[0].start()
    block(0)
    g_in[0].start()
    for l in range(1, L):
        part(l)
        g_part[l].start()
        block(l)
    gb_all[s] = cot[...].astype(BF)
    seg = seg_parts(segr_ref)

    g_small.forwards()
    g_part[0].forwards()
    g_small.finish()
    got = [small_all[k].astype(F32) for k in range(F)]

    def joined(lo, hi, part):
        return jnp.concatenate([x[lo:hi, :part] for x in got], axis=1)

    full[: L * (taps + 1)] = joined(0, L * (taps + 1), conv_part)
    lo = L * (taps + 1)
    full[lo + L : lo + 2 * L, :inner] = joined(lo + L, lo + 2 * L, inner_part)
    gains[...] = jnp.zeros_like(gains)
    gains[:L] = joined(lo, lo + L, width_part)
    part_in = pl.ds(pl.multiple_of(s * il, LANES), il)
    hm = head_map(il)
    for l in range(L):
        par_ref[l] = jnp.zeros_like(par_ref[l])
        par_ref[l, :taps, :il] = full[l * taps : (l + 1) * taps, part_in]
        par_ref[l, :taps, il:] = full[l * taps : (l + 1) * taps, inner:convdim]
        r = L * taps + l
        par_ref[l, 4:5, :il] = full[r : r + 1, part_in]
        par_ref[l, 4:5, il:] = full[r : r + 1, inner:convdim]
        r = lo + L + l
        par_ref[l, 5:6, :il] = full[r : r + 1, part_in]
        par_ref[l, 6:7, :il] = hdot(hp_ref[l], hm, NT)[2:3]

    per[0]["nrm"][s] = norm_of(hidden[...], gains[:1]).astype(BF)
    g_nrm[0].start()
    g_part[0].finish()
    g_shared[0].start()
    for l in range(1, L):
        g_part[l].forwards()
    g_in[0].forwards()
    perm_wait(0)
    g_out[0].start()
    for l in range(1, L):
        g_in[l].start()
        perm_wait(l)
        g_out[l].start()
    g_nrm[0].forwards()
    g_shared[0].forwards()
    for l in range(1, L):
        g_part[l].finish()
        g_shared[l].start()
    g_cot.start()
    g_nrm[0].finish()
    g_shared[0].finish()
    assemble(0)
    g_in[0].finish()

    for l in range(L):
        last = l == L - 1

        def hooks(stage, l=l, last=last):
            if stage == "projected" and l == 0:
                for k in range(1, L):
                    g_shared[k].forwards()
                g_cot.forwards()
                g_out[0].forwards()
            if stage == "mixed" and not last:
                g_in[l + 1].forward(1)
            if stage == "gated":
                g_out[l].finish()

        o = per[l]
        mix_forward(
            seg, o["nrm"], o["win"], o["wsh"], o["wout"], par_ref[l], hp_ref[l],
            (parts[l], sq_all[l].at[s], o["z"], o["v"], o["dt"], o["y"], o["sc"]), hooks,
        )
        sc = Scatter("seq", S, parts[l], scs[l])
        sc.start()
        g_sq[l].start()
        if not last:
            g_in[l + 1].forward(2)
        current = hidden if l == 0 else per[l - 1]["new"]
        sc.middle()
        g_sq[l].forwards()
        g_sq[l].finish()
        if not last:
            for da in range(3, factor(F)[0]):
                g_in[l + 1].forward(da)
        tokens = hidden.shape[0]
        o["inv"][...] = lax.rsqrt(jnp.sum(sq_all[l][...], axis=0) * (1.0 / inner) + EPS)
        inv = as_col(o["inv"][pl.ds(pl.multiple_of(8 * s, 8), 8)][:1])
        delta = sc.finish() * inv
        u = current[...] + delta
        o["delta"][...] = delta
        o["new"][...] = u
        if l == 0:
            g_cot.finish()
        if last:
            hidden_out[...] = u
            dots = jnp.sum(gb_all[s].astype(F32) * delta, axis=1, keepdims=True)
            dots_all[s] = as_row(dots)
            g = g_dots
        else:
            per[l + 1]["nrm"][s] = norm_of(u, gains[l + 1 : l + 2]).astype(BF)
            g = g_nrm[l + 1]
        g.start()
        for c in stores[l]:
            c.start()
        if not last:
            g_out[l + 1].forwards()
        g.forwards()
        if not last:
            g_shared[l + 1].finish()
            assemble(l + 1)
        g.finish()
        if not last:
            g_in[l + 1].finish()
    for c in stores[L - 1]:
        c.wait()
    for l in range(L - 1):
        for c in stores[l]:
            c.wait()


KEPT = ("new", "delta", "inv")
STORED = ("win", "wsh", "wout", "nrm", "z", "v", "dt", "y", "sc")
FORWARD_OUTS = KEPT + STORED


def forward(S, F, heads, hidden, cot, segr, win_raw, wout_raw, cw, cb, ng, gg, hp):
    tokens, width = hidden.shape
    length = segr.shape[1]
    L, taps, conv_part = cw.shape
    inner, convdim = gg.shape[1] * F, conv_part * F
    il, bc = inner // S, convdim - inner
    conv = il + bc
    sem = pltpu.SemaphoreType.DMA
    rows = -(-(L * (taps + 3)) // 16) * 16
    wide = -(-max(conv_part, ng.shape[1], gg.shape[1]) // LANES) * LANES
    breadth = bc + LANES
    part_rows = -(-(win_raw.shape[1] // S) // 16) * 16
    outs = [
        sds((tokens, width), F32),
        sds((S, tokens, width), BF),
        sds((8, width), F32),
        sds((L, 8, conv), F32),
        sds((S, 8, tokens), F32),
    ]
    kept = [
        sds((tokens, width), F32),
        sds((tokens, width), F32),
        sds((S * 8, tokens), F32),
    ]
    stored = [
        sds((F, win_raw.shape[1], 2 * il), BF),
        sds((width, breadth), BF),
        sds((F,) + wout_raw.shape[2:], BF),
        sds((S, tokens, width), BF),
        sds((length, il), F32),
        sds((length, conv), BF),
        sds((length, LANES), F32),
        sds((length, il), BF),
        sds((length, il), BF),
    ]
    vmem_outs = len(outs) + L * len(kept)
    outs += kept * L + stored * L
    scratch = [pltpu.VMEM((F, rows, wide), BF), pltpu.VMEM((rows, convdim), F32)]
    scratch += [pltpu.VMEM((S, tokens, width), BF) for _ in range(L)]
    scratch += [pltpu.VMEM((S, S * 8, tokens), F32) for _ in range(L)]
    for _ in range(L):
        scratch += Scatter.scratch(S, (tokens, width))
    scratch += [pltpu.VMEM((S, F, part_rows, breadth), BF) for _ in range(L)]
    scratch += [pltpu.VMEM((width, breadth), F32)]
    for _ in range(L):
        scratch += [pltpu.VMEM(x.shape, x.dtype) for x in stored] + [sem((len(stored),))]
    for n in [F, S, S]:
        scratch += Gather.scratch(n)
    scratch += Line.scratch(F)
    for n in [F] * (2 * L - 1) + [S] * (2 * L) + [F] * L + [S] * L:
        scratch += Gather.scratch(n)
    scratch += [sem((L,)), sem((L,)), sem((L,))]
    got = comm_call(
        partial(forward_kernel, S, F, L, heads), "forward", 0, outs, scratch,
        (hidden, cot, segr, win_raw, wout_raw, cw, cb, ng, gg, hp),
        out_spaces=[pltpu.VMEM] * vmem_outs + [pl.ANY] * (len(outs) - vmem_outs),
    )
    k, n = len(kept), len(stored)
    layers = []
    for l in range(L):
        low, high = 5 + l * k, vmem_outs + l * n
        layers.append(dict(zip(FORWARD_OUTS, got[low : low + k] + got[high : high + n])))
    return got[:5], layers


def mix_backward(total_inner, seg, nrm, win, wsh, wout, par, hp, kept, gb, inv, dots, out, hooks):
    z_ref, v_ref, dt_ref, y_ref, sc_ref = kept
    gz_ref, gx_ref, gout_ref, dpart_ref, dbc_ref, ddt_ref, small_ref, dproj = out
    segc, segr, cm = seg
    inner = z_ref.shape[1]
    length, conv = v_ref.shape
    blocks = length // SPAN
    nstate = (conv - inner) // 2

    scaled_in = lax.dot_general(gb, wout[...], (NT, ((), ())), preferred_element_type=F32) * inv
    z = z_ref[...]
    y = y_ref[...].astype(F32)
    sig = sigmoid(z)
    silu = z * sig
    prod = y * silu
    small_ref[5:6, :inner] = jnp.sum(scaled_in * prod, axis=0, keepdims=True)
    d_prod = scaled_in * par[5:6, :inner] - prod * (inv * inv * dots * (1.0 / total_inner))
    dy = d_prod * silu
    dy = dy.astype(BF).astype(F32)
    dproj[:, :inner] = (d_prod * y * (sig * (1.0 + z * (1.0 - sig)))).astype(BF)
    grad_scaled = (gb.astype(F32) * inv).astype(BF)
    put(
        gout_ref,
        lax.dot_general(sc_ref[...], grad_scaled, (TN, ((), ())), preferred_element_type=F32),
    )
    put(gz_ref, bdot(nrm[...], dproj[:, :inner], TN))
    hooks("gout")

    lim = limits(segc, segr)
    v = v_ref[...].astype(F32)
    moved = shifts(v, cm)
    pre = conv_pre(v, moved, par)
    csig = sigmoid(pre)
    act = pre * csig
    x_act = act[:, :inner]
    b_act = act[:, inner : inner + nstate].astype(BF)
    c_act = act[:, inner + nstate :].astype(BF)
    u, delta, decay = decay_of(dt_ref[...], hp)
    cum = cumulate(lim, decay)
    cum_t = [c.T for c in cum]
    hm = head_map(inner)
    delta_bc = hdot(delta, hm, NT)
    xs = x_act * delta_bc
    cb = {k: bdot(c_act[span(k[0])], b_act[span(k[1])], NT) for k in lim}

    lane = lax.broadcasted_iota(jnp.int32, (SPAN, LANES), 1)
    sub = lax.broadcasted_iota(jnp.int32, (LANES, SPAN), 0)
    dcb = {k: jnp.zeros((SPAN, SPAN), F32) for k in lim}
    drow = [jnp.zeros((SPAN, LANES), F32) for _ in range(blocks)]
    dcol = [jnp.zeros((LANES, SPAN), F32) for _ in range(blocks)]
    dxs = []
    for q in range(inner // LANES):
        ql = slice(q * LANES, (q + 1) * LANES)
        pair = xs[:, ql].astype(BF)
        dyp = halves(dy[:, ql])
        dxq = [jnp.zeros((SPAN, LANES), F32) for _ in range(blocks)]
        for i in range(blocks):
            for j in range(i + 1):
                for e in range(2):
                    h = 2 * q + e
                    w = jnp.exp(jnp.minimum(cum[i][:, h : h + 1] - cum_t[j][h : h + 1], lim[i, j]))
                    p = w * cb[i, j]
                    dp = bdot(dyp[e][span(i)], pair[span(j)], NT)
                    dxq[j] = dxq[j] + bdot(p, dyp[e][span(i)], TN)
                    dcb[i, j] = dcb[i, j] + dp * w
                    g = dp * p
                    drow[i] = drow[i] + jnp.where(lane == h, jnp.sum(g, axis=1, keepdims=True), 0.0)
                    dcol[j] = dcol[j] + jnp.where(sub == h, jnp.sum(g, axis=0, keepdims=True), 0.0)
        dxs.append(jnp.concatenate(dxq, axis=0))
        hooks(f"pair{q}")
    dxs = jnp.concatenate(dxs, axis=1)
    db, dc = [], []
    for k in range(blocks):
        db.append(sum(bdot(dcb[i, k], c_act[span(i)], TN) for i in range(k, blocks)))
        dc.append(sum(bdot(dcb[k, j], b_act[span(j)]) for j in range(k + 1)))
    dcum_t = [drow[k].T - dcol[k] for k in range(blocks)]
    ddecay = []
    for j in range(blocks):
        total = None
        for i in range(j, blocks):
            term = hdot(dcum_t[i], (lim[i, j] == 0.0).astype(F32))
            total = term if total is None else total + term
        ddecay.append(total.T)
    ddecay = jnp.concatenate(ddecay, axis=0)
    ddelta = hdot(dxs * x_act, hm) - jnp.exp(hp[0:1]) * ddecay
    ddt = ddelta * sigmoid(u)
    small_ref[6:7, :LANES] = jnp.sum(ddecay * decay, axis=0, keepdims=True)
    small_ref[6:7, LANES : 2 * LANES] = jnp.sum(ddt, axis=0, keepdims=True)
    skip = jnp.broadcast_to(jnp.sum(dy * x_act, axis=0, keepdims=True), (8, inner))
    small_ref[6:7, 2 * LANES : 3 * LANES] = hdot(skip, hm)[:1]
    dx_act = dxs * delta_bc + dy * par[6:7, :inner]
    dact = jnp.concatenate(
        [dx_act, jnp.concatenate(db, axis=0), jnp.concatenate(dc, axis=0)], axis=1
    )

    dpre = dact * (csig * (1.0 + pre * (1.0 - csig)))
    small_ref[4:5, :conv] = jnp.sum(dpre, axis=0, keepdims=True)
    small_ref[3:4, :conv] = jnp.sum(dpre * v, axis=0, keepdims=True)
    dv = par[3:4] * dpre
    for d in range(1, 4):
        small_ref[3 - d : 4 - d, :conv] = jnp.sum(dpre * moved[d - 1], axis=0, keepdims=True)
        back = dpre * cm[:, d - 1 : d] * par[3 - d : 4 - d]
        dv = dv + pltpu.roll(back, length - d, 0)
    heads = inner // HEADDIM
    real = lax.broadcasted_iota(jnp.int32, (length, LANES), 1) < heads
    ddt = jnp.where(real, ddt, 0.0)
    dproj[:, inner : inner + conv] = dv.astype(BF)
    dproj[:, inner + conv :] = ddt.astype(BF)
    put(dbc_ref, dv[:, inner:].T)
    ddt_ref[...] = ddt.T[: ddt_ref.shape[0]].astype(BF)
    put(
        dpart_ref,
        bdot(dproj[:, : 2 * inner], win[...], NT) + bdot(dproj[:, 2 * inner :], wsh[...], NT),
    )
    hooks("dpart")
    put(gx_ref, bdot(nrm[...], dproj[:, inner : 2 * inner], TN))
    hooks("gin")


BACKWARD_SMALL = ("inv", "prior")
BACKWARD_INS = STORED + BACKWARD_SMALL


def backward_kernel(S, F, L, total_inner, *refs):
    take = Take(refs)
    cot, segr_ref, gb_last, dots_last, gains, par_ref, hp_ref = take(7)
    ins = [dict(zip(BACKWARD_INS, take(len(BACKWARD_INS)))) for _ in range(L)]
    deltas = take(L)
    sources = [x.copy() for x in ins]
    input_grad, small_out = take(2)
    outs = [take(4) for _ in range(L)]
    jobs = [take(4) for _ in range(L)]
    dparts, dbcs, ddts = take(L), take(L), take(L)
    gbs, dotss = take(L - 1), take(L - 1)
    dproj, small, out_mid = take(), take(), take(L)
    scat = [[Scatter("fsdp", F, jobs[l][k], take(N_SCATTER)) for k in range(4)] for l in range(L)]
    sc = [Scatter("seq", S, dparts[l], take(N_SCATTER)) for l in range(L)]
    sb = [Scatter("seq", S, dbcs[l], take(N_SCATTER)) for l in range(L)]
    g_gb = [Gather("seq", S, gbs[l], take(2)) for l in range(L - 1)]
    g_dots = [Gather("seq", S, dotss[l], take(2)) for l in range(L - 1)]
    g_job = [[Gather("seq", S, outs[l][k], take(2)) for k in range(4)] for l in range(L)]
    g_small = Gather("seq", S, small_out, take(2))
    perm_send, perm_recv = take(2)
    sm_row, sm_mid, sm_col, sm_s1, sm_r1, sm_s2, sm_r2 = take(7)
    loads = [[] for _ in range(L)]
    for l in range(L - 1):
        for k, ref in zip(STORED, take(len(STORED))):
            ins[l][k] = ref
        sem = take()
        for i, k in enumerate(STORED):
            loads[l].append(pltpu.make_async_copy(sources[l][k], ins[l][k], sem.at[i]))
    for l in range(L - 1):
        for c in loads[l]:
            c.start()

    s, f = lax.axis_index("seq"), lax.axis_index("fsdp")
    a_n, b_n = factor(F)
    a, b = f // b_n, f % b_n
    flat_id = f * S + s
    own = s * F + f
    target = (own % S, own // S)
    source = (flat_id // F, flat_id % F)
    moved = flat_id != own
    barrier([("fsdp", F), ("seq", S)], (source, moved))

    def perm(l):
        return pltpu.make_async_remote_copy(
            src_ref=out_mid[l],
            dst_ref=outs[l][3].at[own % S],
            send_sem=perm_send.at[l],
            recv_sem=perm_recv.at[l],
            device_id=target,
            device_id_type=MESH,
        )

    def row(db):
        return pltpu.make_async_remote_copy(
            src_ref=small,
            dst_ref=sm_row.at[db],
            send_sem=sm_s1.at[db],
            recv_sem=sm_r1.at[db],
            device_id=(s, a * b_n + lax.rem(b + db, b_n)),
            device_id_type=MESH,
        )

    def col(da, sender=True):
        at = a if sender else lax.rem(a + a_n - da, a_n)
        return pltpu.make_async_remote_copy(
            src_ref=sm_mid,
            dst_ref=sm_col.at[at],
            send_sem=sm_s2.at[da],
            recv_sem=sm_r2.at[da],
            device_id=(s, lax.rem(a + da, a_n) * b_n + b),
            device_id_type=MESH,
        )

    def out_done(l):
        value = scat[l][3].finish().astype(BF)
        out_mid[l][...] = value

        @pl.when(moved)
        def _():
            perm(l).start()

        @pl.when(jnp.logical_not(moved))
        def _():
            outs[l][3][s] = value

    def out_gather(l):
        @pl.when(moved)
        def _():
            perm(l).wait()

        g_job[l][3].start()

    def job_done(l, k):
        outs[l][k][s] = scat[l][k].finish().astype(BF)
        g_job[l][k].start()

    seg = seg_parts(segr_ref)
    small[...] = jnp.zeros_like(small)
    pairs = ins[0]["z"].shape[1] // LANES

    for l in reversed(range(L)):
        x = ins[l]
        base = 16 * l
        if l == L - 1:
            gb_ref, dots_ref = gb_last, dots_last
        else:
            gb_ref, dots_ref = gbs[l], dotss[l]

        def hooks(stage, l=l):
            if stage == "gout":
                scat[l][3].start()
                scat[l][0].start()
                if l < L - 1:
                    out_done(l + 1)
                    scat[l + 1][1].middle()
                    scat[l + 1][2].middle()
            if stage == f"pair{pairs - 1}":
                scat[l][3].middle()
                if l < L - 1:
                    out_gather(l + 1)
                    job_done(l + 1, 0)
            if stage == "dpart":
                sb[l].start()
                sc[l].start()
            if stage == "gin":
                scat[l][1].start()

        for c in loads[l]:
            c.wait()
        inv = jnp.concatenate([as_col(x["inv"][8 * k : 8 * k + 1]) for k in range(S)], axis=0)
        dots = jnp.concatenate([as_col(dots_ref[k][:1]) for k in range(S)], axis=0)
        mix_backward(
            total_inner, seg, x["nrm"], x["win"], x["wsh"], x["wout"], par_ref[l], hp_ref[l],
            (x["z"], x["v"], x["dt"], x["y"], x["sc"]), flat(gb_ref), inv, dots,
            (jobs[l][0], jobs[l][1], jobs[l][3], dparts[l], dbcs[l], ddts[l], small.at[base : base + 8], dproj),
            hooks,
        )
        sb[l].middle()
        sc[l].middle()
        scat[l][0].middle()
        u = x["prior"][...]
        n = lax.rsqrt(jnp.mean(u * u, axis=-1, keepdims=True) + EPS)
        xhat = u * n
        tail = jnp.concatenate([sb[l].finish().astype(BF), ddts[l][...]], axis=0)
        put(
            jobs[l][2],
            lax.dot_general(
                x["nrm"][...], tail, (((0,), (1,)), ((), ())), preferred_element_type=F32
            ),
        )
        scat[l][2].start()
        dn = sc[l].finish()
        small[base + 8 : base + 9] = jnp.sum(dn * xhat, axis=0, keepdims=True)
        t = dn * gains[l : l + 1]
        g_ref = cot if l == L - 1 else input_grad
        new = g_ref[...] + n * (t - xhat * jnp.mean(t * xhat, axis=-1, keepdims=True))
        input_grad[...] = new
        if l > 0:
            gb = new.astype(BF)
            gbs[l - 1][s] = gb
            dotss[l - 1][s] = as_row(
                jnp.sum(gb.astype(F32) * deltas[l - 1][...], axis=1, keepdims=True)
            )
            for g in (g_gb[l - 1], g_dots[l - 1]):
                g.start()
            for g in (g_gb[l - 1], g_dots[l - 1]):
                g.forwards()
            for g in (g_gb[l - 1], g_dots[l - 1]):
                g.finish()

    for db in range(1, b_n):
        row(db).start()
    for l in range(1, L):
        job_done(l, 1)
        job_done(l, 2)
    out_done(0)
    job_done(0, 0)
    scat[0][1].middle()
    scat[0][2].middle()
    sm_row[0] = small[...]
    for db in range(1, b_n):
        row(db).wait_recv()
    total = None
    for k in range(b_n):
        term = sm_row[lax.rem(b + b_n - k, b_n)]
        total = term if total is None else total + term
    sm_mid[...] = total
    for da in range(1, a_n):
        col(da).start()
    for l in range(1, L):
        for g in g_job[l]:
            g.forwards()
    out_gather(0)
    g_job[0][0].forwards()
    job_done(0, 1)
    job_done(0, 2)
    sm_col[a] = sm_mid[...]
    for da in range(1, a_n):
        col(da, False).wait_recv()
    small_out[s] = jnp.sum(sm_col[...], axis=0)
    g_small.start()
    g_job[0][3].forwards()
    g_job[0][1].forwards()
    g_job[0][2].forwards()
    g_small.forwards()
    for l in range(L):
        for g in g_job[l]:
            g.finish()
    g_small.finish()
    for db in range(1, b_n):
        row(db).wait_send()
    for da in range(1, a_n):
        col(da).wait_send()


def backward(S, F, total_inner, cot, segr, gb_last, dots_last, gains, par, hp, layers, deltas):
    L = len(layers)
    tokens, width = cot.shape
    length, il = layers[0]["z"].shape
    conv = layers[0]["v"].shape[1]
    bc = conv - il
    bl = bc // S
    a_n, b_n = factor(F)
    sem = pltpu.SemaphoreType.DMA
    shapes = [(width // F, il)] * 2 + [(width // F, LANES), (il // F, width)]
    outs = [sds((tokens, width), F32), sds((S, 16 * L, width), F32)]
    for _ in range(L):
        outs += [sds((S,) + shape, BF) for shape in shapes]
    scratch = []
    for _ in range(L):
        scratch += [pltpu.VMEM((F,) + shape, BF) for shape in shapes]
    scratch += [pltpu.VMEM((S, tokens, width), BF) for _ in range(L)]
    scratch += [pltpu.VMEM((S, bl, length), BF) for _ in range(L)]
    scratch += [pltpu.VMEM((LANES - bl, length), BF) for _ in range(L)]
    scratch += [pltpu.VMEM((S, tokens, width), BF) for _ in range(L - 1)]
    scratch += [pltpu.VMEM((S, 8, tokens), F32) for _ in range(L - 1)]
    scratch += [pltpu.VMEM((length, il + conv + LANES), BF), pltpu.VMEM((16 * L, width), F32)]
    scratch += [pltpu.VMEM(shapes[3], BF) for _ in range(L)]
    for _ in range(L):
        for shape in shapes:
            scratch += Scatter.scratch(F, shape)
    for _ in range(L):
        scratch += Scatter.scratch(S, (tokens, width))
    for _ in range(L):
        scratch += Scatter.scratch(S, (bl, length))
    for _ in range(2 * (L - 1) + 4 * L + 1):
        scratch += Gather.scratch(S)
    scratch += [sem((L,)), sem((L,))]
    scratch += [
        pltpu.VMEM((b_n, 16 * L, width), F32),
        pltpu.VMEM((16 * L, width), F32),
        pltpu.VMEM((a_n, 16 * L, width), F32),
        sem((b_n,)), sem((b_n,)), sem((a_n,)), sem((a_n,)),
    ]
    for l in range(L - 1):
        scratch += [pltpu.VMEM(layers[l][k].shape, layers[l][k].dtype) for k in STORED]
        scratch += [sem((len(STORED),))]
    args = [cot, segr, gb_last, dots_last, gains, par, hp]
    spaces = [pltpu.VMEM] * len(args)
    for l, x in enumerate(layers):
        args += [x[k] for k in BACKWARD_INS]
        spaces += [pltpu.VMEM if l == L - 1 else pl.ANY] * len(STORED)
        spaces += [pltpu.VMEM] * len(BACKWARD_SMALL)
    args += deltas
    spaces += [pltpu.VMEM] * L
    return comm_call(
        partial(backward_kernel, S, F, L, total_inner), "backward", 1, outs, scratch, args,
        in_spaces=spaces,
    )


def finish_kernel(S, F, L, heads, *refs):
    take = Take(refs)
    sums = take()
    jobs = [take(4) for _ in range(L)]
    gin, gout, gcw, gcb, gng, ggg, gal, gdb, gds = take(9)
    f = lax.axis_index("fsdp")
    taps, conv_part = gcw.shape[1:]
    width_part, inner_part = gng.shape[1], ggg.shape[1]
    inner, convdim = inner_part * F, conv_part * F
    il, hl = inner // S, heads // S
    bc = convdim - inner
    bl = bc // S

    def own(x, part):
        n = x.shape[1]
        return pltpu.roll(x, lax.rem(n - f * part, n), 1)[:, :part]

    for l in range(L):
        gz, gx, tail, out = jobs[l]
        for s in range(S):
            gin[l, :, s * il : (s + 1) * il] = gz[s].astype(F32)
            gin[l, :, inner + s * il : inner + (s + 1) * il] = gx[s].astype(F32)
        tails = [tail[s].astype(F32) for s in range(S)]
        gin[l, :, 2 * inner : 2 * inner + bc] = jnp.concatenate([t[:, :bl] for t in tails], axis=1)
        gin[l, :, 2 * inner + bc :] = jnp.concatenate([t[:, bl : bl + hl] for t in tails], axis=1)
        rows = out.shape[1]
        for s in range(S):
            gout[l, s * rows : (s + 1) * rows] = out[s].astype(F32)
        base = 16 * l
        low = [sums[s, base : base + 8] for s in range(S)]
        xs = jnp.concatenate([t[:, :il] for t in low], axis=1)
        both = sum(t[:, il : il + bc] for t in low)
        five = own(jnp.concatenate([xs, both], axis=1), conv_part)
        gcw[l] = five[:taps]
        gcb[l : l + 1] = five[taps : taps + 1]
        ggg[l : l + 1] = own(xs, inner_part)[5:6]
        gng[l : l + 1] = own(sum(sums[s, base + 8 : base + 16] for s in range(S)), width_part)[:1]
        for k, ref in enumerate((gal, gdb, gds)):
            ref[l : l + 1] = jnp.concatenate(
                [t[6:7, k * LANES : k * LANES + hl] for t in low], axis=1
            )


def body(
    hidden, cotangent, segments, in_weight, out_weight, conv_weight, conv_bias,
    norm_gain, gate_gain, a_log, dt_bias, d_skip,
):
    seq_idx = lax.axis_index("seq")
    S = lax.axis_size("seq")
    F = lax.axis_size("fsdp")
    tokens, width = hidden.shape[1:]
    L = in_weight.shape[0]
    heads = a_log.shape[1]
    hl = heads // S
    inner = gate_gain.shape[1] * F
    length = segments.shape[1]

    hp = lax.dynamic_slice_in_dim(jnp.stack([a_log, dt_bias, d_skip], axis=1), seq_idx * hl, hl, 2)
    hp = jnp.pad(hp, ((0, 0), (0, 5), (0, LANES - hl)))
    wout_raw = out_weight.reshape(L, S, out_weight.shape[1] // S, width)
    hid, cot = hidden[0], cotangent[0]
    got, layers = forward(
        S, F, heads, hid, cot, segments, in_weight, wout_raw,
        conv_weight, conv_bias, norm_gain, gate_gain, hp,
    )
    hidden_out, gb_all, gains, par, dots_all = got
    deltas = [x["delta"] for x in layers]
    for l, x in enumerate(layers):
        x["prior"] = hid if l == 0 else layers[l - 1]["new"]
        x["nrm"] = x["nrm"].reshape(length, width)
        x["win"] = x["win"].reshape(width, -1)
        x["wout"] = x["wout"].reshape(-1, width)
    got = backward(S, F, inner, cot, segments, gb_all, dots_all, gains, par, hp, layers, deltas)
    outs = [
        sds(in_weight.shape, F32),
        sds(out_weight.shape, F32),
        sds(conv_weight.shape, F32),
        sds(conv_bias.shape, F32),
        sds(norm_gain.shape, F32),
        sds(gate_gain.shape, F32),
    ] + [sds(a_log.shape, F32)] * 3
    final = local_call(partial(finish_kernel, S, F, L, heads), "finish", outs, got[1:])
    return (hidden_out[None], got[0][None], *final)


def solution(mesh):
    token = P("fsdp", "seq", None)
    rows = P(None, "fsdp", None)
    split = P(None, "fsdp")
    taps = P(None, None, "fsdp")
    return jax.shard_map(
        body,
        mesh=mesh,
        in_specs=(
            token, token, P("fsdp", None), rows, rows, taps, split, split, split, P(), P(), P(),
        ),
        out_specs=(token, token, rows, rows, taps, split, split, split, P(), P(), P()),
        check_vma=False,
    )
```

```python
from functools import partial

import jax
import jax.numpy as jnp
from jax import lax
from jax.experimental import pallas as pl
from jax.experimental.pallas import tpu as pltpu
from jax.sharding import PartitionSpec as P

HEADDIM = 64
SPAN = 256
EPS = 1e-05
HIGH = lax.Precision.HIGHEST
BF = jnp.bfloat16
F32 = jnp.float32
MESH = pl.DeviceIdType.MESH
NEGATIVE = -1e30
LANES = 128
VMEM_LIMIT = 60 * 1024 * 1024


def factor(n):
    b = 1
    while (2 * b) * (2 * b) <= n:
        b *= 2
    return n // b, b


def peers_of(axis, n):
    a_n, b_n = factor(n)
    s, f = lax.axis_index("seq"), lax.axis_index("fsdp")
    i = s if axis == "seq" else f
    a, b = i // b_n, i % b_n

    def dev(k):
        return (k, f) if axis == "seq" else (s, k)

    out = []
    for da in range(1, a_n):
        out.append(dev(lax.rem(a + da, a_n) * b_n + b))
    for db in range(1, b_n):
        out.append(dev(a * b_n + lax.rem(b + db, b_n)))
    return out


def barrier(groups, extra):
    sem = pltpu.get_barrier_semaphore()
    devices = [d for axis, n in groups for d in peers_of(axis, n)]
    for d in devices:
        pl.semaphore_signal(sem, inc=1, device_id=d, device_id_type=MESH)
    source, moved = extra

    @pl.when(moved)
    def _():
        pl.semaphore_signal(sem, inc=1, device_id=source, device_id_type=MESH)

    return lambda: pl.semaphore_wait(sem, len(devices) + moved.astype(jnp.int32))


class Gather:
    def __init__(self, axis, n, ref, sems):
        self.n = n
        self.a_n, self.b_n = factor(n)
        s, f = lax.axis_index("seq"), lax.axis_index("fsdp")
        i = s if axis == "seq" else f
        self.a, self.b = i // self.b_n, i % self.b_n
        self.dev = (lambda k: (k, f)) if axis == "seq" else (lambda k: (s, k))
        self.ref = ref
        self.send, self.recv = sems

    @staticmethod
    def scratch(n):
        a_n, b_n = factor(n)
        count = a_n * b_n
        return [pltpu.SemaphoreType.DMA((count,)), pltpu.SemaphoreType.DMA((count,))]

    def _first(self, da, sender):
        a = self.a if sender else lax.rem(self.a + self.a_n - da, self.a_n)
        block = a * self.b_n + self.b
        return pltpu.make_async_remote_copy(
            src_ref=self.ref.at[block],
            dst_ref=self.ref.at[block],
            send_sem=self.send.at[da * self.b_n],
            recv_sem=self.recv.at[da * self.b_n],
            device_id=self.dev(lax.rem(self.a + da, self.a_n) * self.b_n + self.b),
            device_id_type=MESH,
        )

    def _second(self, da, db, sender):
        a = lax.rem(self.a + self.a_n - da, self.a_n)
        b = self.b if sender else lax.rem(self.b + self.b_n - db, self.b_n)
        block = a * self.b_n + b
        return pltpu.make_async_remote_copy(
            src_ref=self.ref.at[block],
            dst_ref=self.ref.at[block],
            send_sem=self.send.at[da * self.b_n + db],
            recv_sem=self.recv.at[da * self.b_n + db],
            device_id=self.dev(self.a * self.b_n + lax.rem(self.b + db, self.b_n)),
            device_id_type=MESH,
        )

    def start_columns(self):
        for da in range(1, self.a_n):
            self._first(da, True).start()

    def start_rows(self):
        for db in range(1, self.b_n):
            self._second(0, db, True).start()

    def start(self):
        self.start_columns()
        self.start_rows()

    def forward(self, da):
        self._first(da, False).wait_recv()
        for db in range(1, self.b_n):
            self._second(da, db, True).start()

    def forwards(self):
        for da in range(1, self.a_n):
            self.forward(da)

    def finish(self):
        for da in range(self.a_n):
            for db in range(1, self.b_n):
                self._second(da, db, False).wait_recv()
        for da in range(1, self.a_n):
            self._first(da, True).wait_send()
        for da in range(self.a_n):
            for db in range(1, self.b_n):
                self._second(da, db, True).wait_send()


class Line(Gather):
    @staticmethod
    def scratch(n):
        a_n, b_n = factor(n)
        count = 2 * a_n + a_n * b_n
        return [pltpu.SemaphoreType.DMA((count,)), pltpu.SemaphoreType.DMA((count,))]

    def _copy(self, block, k, device):
        return pltpu.make_async_remote_copy(
            src_ref=self.ref.at[block],
            dst_ref=self.ref.at[block],
            send_sem=self.send.at[k],
            recv_sem=self.recv.at[k],
            device_id=self.dev(device),
            device_id_type=MESH,
        )

    def _step(self, way, k):
        to = self.a + way
        slot = k if way > 0 else self.a_n + k
        return self._copy((to - way * k) * self.b_n + self.b, slot, to * self.b_n + self.b)

    def _row(self, a, db, sender):
        b = self.b if sender else lax.rem(self.b + self.b_n - db, self.b_n)
        slot = 2 * self.a_n + a * self.b_n + db
        device = self.a * self.b_n + lax.rem(self.b + db, self.b_n)
        return self._copy(a * self.b_n + b, slot, device)

    def _may(self, way, k):
        if way > 0:
            return (self.a + 1 < self.a_n) & (self.a + 1 >= k)
        return (self.a >= 1) & (self.a - 1 + k < self.a_n)

    def start_columns(self):
        for way in (1, -1):

            @pl.when(self._may(way, 1))
            def _():
                self._step(way, 1).start()

    def start_rows(self):
        for db in range(1, self.b_n):
            self._row(self.a, db, True).start()

    def forward(self, k):
        for way in (1, -1):
            block = self.a - way * k
            here = (block >= 0) & (block < self.a_n)

            @pl.when(here)
            def _():
                slot = k if way > 0 else self.a_n + k
                sender = (self.a - way) * self.b_n + self.b
                self._copy(block * self.b_n + self.b, slot, sender).wait_recv()
                if k + 1 < self.a_n:

                    @pl.when(self._may(way, k + 1))
                    def _():
                        self._step(way, k + 1).start()

                for db in range(1, self.b_n):
                    self._row(block, db, True).start()

    def finish(self):
        for a in range(self.a_n):
            for db in range(1, self.b_n):
                self._row(a, db, False).wait_recv()
        for k in range(1, self.a_n):
            for way in (1, -1):

                @pl.when(self._may(way, k))
                def _():
                    self._step(way, k).wait_send()

        for a in range(self.a_n):
            for db in range(1, self.b_n):
                self._row(a, db, True).wait_send()


class Scatter:
    def __init__(self, axis, n, ref, scratch):
        self.a_n, self.b_n = factor(n)
        s, f = lax.axis_index("seq"), lax.axis_index("fsdp")
        i = s if axis == "seq" else f
        self.a, self.b = i // self.b_n, i % self.b_n
        self.dev = (lambda k: (k, f)) if axis == "seq" else (lambda k: (s, k))
        self.ref = ref
        self.row_in, self.mid, self.col_in, self.send, self.recv, self.send2, self.recv2 = scratch

    @staticmethod
    def scratch(n, shape, dtype=BF):
        a_n, b_n = factor(n)
        sem = pltpu.SemaphoreType.DMA
        return [
            pltpu.VMEM((a_n, b_n - 1) + shape, dtype),
            pltpu.VMEM((a_n,) + shape, dtype),
            pltpu.VMEM((a_n - 1,) + shape, dtype),
            sem((a_n, b_n - 1)),
            sem((a_n, b_n - 1)),
            sem((a_n,)),
            sem((a_n,)),
        ]

    def _row(self, da, db):
        a = lax.rem(self.a + da, self.a_n)
        b = lax.rem(self.b + db, self.b_n)
        return pltpu.make_async_remote_copy(
            src_ref=self.ref.at[a * self.b_n + b],
            dst_ref=self.row_in.at[da, db - 1],
            send_sem=self.send.at[da, db - 1],
            recv_sem=self.recv.at[da, db - 1],
            device_id=self.dev(self.a * self.b_n + b),
            device_id_type=MESH,
        )

    def _col(self, da):
        a = lax.rem(self.a + da, self.a_n)
        return pltpu.make_async_remote_copy(
            src_ref=self.mid.at[da],
            dst_ref=self.col_in.at[da - 1],
            send_sem=self.send2.at[da],
            recv_sem=self.recv2.at[da],
            device_id=self.dev(a * self.b_n + self.b),
            device_id_type=MESH,
        )

    def start(self):
        for da in list(range(1, self.a_n)) + [0]:
            for db in range(1, self.b_n):
                self._row(da, db).start()

    def _sum(self, da):
        a = lax.rem(self.a + da, self.a_n)
        for db in range(1, self.b_n):
            self._row(da, db).wait_recv()
        total = self.ref[a * self.b_n + self.b].astype(F32)
        for db in range(1, self.b_n):
            total = total + self.row_in[da, db - 1].astype(F32)
        return total

    def middle(self):
        for da in range(1, self.a_n):
            self.mid[da] = self._sum(da).astype(self.mid.dtype)
            self._col(da).start()

    def finish(self):
        total = self._sum(0)
        for da in range(1, self.a_n):
            self._col(da).wait_recv()
            total = total + self.col_in[da - 1].astype(F32)
        for da in range(self.a_n):
            for db in range(1, self.b_n):
                self._row(da, db).wait_send()
        for da in range(1, self.a_n):
            self._col(da).wait_send()
        return total


N_SCATTER = 7


def comm_call(kernel, name, collective_id, outs, scratch, args, in_spaces=None, out_spaces=None):
    def specs(spaces, n):
        spaces = spaces or [pltpu.VMEM] * n
        return [pl.BlockSpec(memory_space=x) for x in spaces]

    return pl.pallas_call(
        kernel,
        name=name,
        out_shape=outs,
        in_specs=specs(in_spaces, len(args)),
        out_specs=specs(out_spaces, len(outs)),
        scratch_shapes=scratch,
        compiler_params=pltpu.CompilerParams(
            collective_id=collective_id, has_side_effects=True, vmem_limit_bytes=VMEM_LIMIT
        ),
    )(*args)


def local_call(kernel, name, outs, args):
    spec = pl.BlockSpec(memory_space=pltpu.VMEM)
    return pl.pallas_call(
        kernel,
        name=name,
        out_shape=outs,
        in_specs=[spec] * len(args),
        out_specs=[spec] * len(outs),
        compiler_params=pltpu.CompilerParams(vmem_limit_bytes=VMEM_LIMIT),
    )(*args)


def sds(shape, dtype):
    return jax.ShapeDtypeStruct(shape, dtype)


def as_row(col):
    t = col.shape[0]
    return jnp.broadcast_to(col, (t, LANES)).T[:8]


def as_col(row):
    t = row.shape[1]
    return jnp.broadcast_to(row, (LANES, t)).T[:, :1]


def norm_of(u, gain):
    return u * lax.rsqrt(jnp.mean(u * u, axis=-1, keepdims=True) + EPS) * gain


def bdot(x, y, dims=((1,), (0,))):
    return lax.dot_general(
        x.astype(BF), y.astype(BF), (dims, ((), ())), preferred_element_type=F32
    )


def hdot(x, y, dims=((1,), (0,))):
    return lax.dot_general(x, y, (dims, ((), ())), precision=HIGH, preferred_element_type=F32)


NT = ((1,), (1,))
TN = ((0,), (0,))


def span(i):
    return slice(i * SPAN, (i + 1) * SPAN)


def limits(segc, segr):
    blocks = segc.shape[0] // SPAN
    rows = lax.broadcasted_iota(jnp.int32, (SPAN, SPAN), 0)
    cols = lax.broadcasted_iota(jnp.int32, (SPAN, SPAN), 1)
    out = {}
    for i in range(blocks):
        for j in range(i + 1):
            kept = segc[span(i)] == segr[:, span(j)]
            if i == j:
                kept = kept & (rows >= cols)
            out[i, j] = jnp.where(kept, 0.0, NEGATIVE)
    return out


def head_map(inner):
    rows = lax.broadcasted_iota(jnp.int32, (inner, LANES), 0)
    cols = lax.broadcasted_iota(jnp.int32, (inner, LANES), 1)
    return ((rows // HEADDIM) == cols).astype(F32)


def shifts(v, cm):
    return [pltpu.roll(v, d, 0) * cm[:, d - 1 : d] for d in range(1, 4)]


def conv_pre(v, moved, par):
    pre = par[4:5] + par[3:4] * v
    for d in range(1, 4):
        pre = pre + par[3 - d : 4 - d] * moved[d - 1]
    return pre


def sigmoid(x):
    return 1.0 / (1.0 + jnp.exp(-x))


def softplus(x):
    return jnp.maximum(x, 0.0) + jnp.log1p(jnp.exp(-jnp.abs(x)))


def decay_of(dt, hp):
    u = dt + hp[1:2]
    delta = softplus(u)
    return u, delta, -jnp.exp(hp[0:1]) * delta


def cumulate(lim, decay):
    blocks = decay.shape[0] // SPAN
    out = []
    for i in range(blocks):
        total = None
        for j in range(i + 1):
            term = hdot((lim[i, j] == 0.0).astype(F32), decay[span(j)])
            total = term if total is None else total + term
        out.append(total)
    return out


def halves(pair):
    lane = lax.broadcasted_iota(jnp.int32, pair.shape, 1)
    low = lane < HEADDIM
    return jnp.where(low, pair, 0.0).astype(BF), jnp.where(low, 0.0, pair).astype(BF)


class Take:
    def __init__(self, refs):
        self.refs = list(refs)

    def __call__(self, n=None):
        if n is None:
            return self.refs.pop(0)
        got, self.refs = self.refs[:n], self.refs[n:]
        return got


def flat(ref):
    f, rows, cols = ref.shape
    if rows % 16 == 0:
        return ref[...].reshape(f * rows, cols)
    return jnp.concatenate([ref[k].astype(F32) for k in range(f)], axis=0).astype(ref.dtype)


def put(ref, value):
    rows = ref.shape[1]
    for k in range(ref.shape[0]):
        ref[k] = value[k * rows : (k + 1) * rows].astype(ref.dtype)


def seg_parts(segr_ref):
    row = segr_ref[...].astype(F32)
    length = row.shape[1]
    wide = jnp.broadcast_to(row, (LANES, length)).T
    pos = lax.broadcasted_iota(jnp.int32, (length, LANES), 0)
    cm = []
    for d in range(1, 4):
        same = (pltpu.roll(wide, d, 0) == wide) & (pos >= d)
        cm.append(same.astype(F32)[:, :1])
    return wide[:, :1], row, jnp.concatenate(cm, axis=1)


def mix_forward(seg, nrm, win, wsh, wout, par, hp, out, hooks):
    part_ref, sq_ref, z_ref, v_ref, dt_ref, y_ref, sc_ref = out
    segc, segr, cm = seg
    inner = z_ref.shape[1]
    length, conv = v_ref.shape
    blocks = length // SPAN
    x = flat(nrm)
    w = flat(win)
    z_ref[...] = jnp.dot(x, w[:, :inner], preferred_element_type=F32)
    v_ref[:, :inner] = jnp.dot(x, w[:, inner:], preferred_element_type=F32).astype(BF)
    hooks("projected")
    shared = jnp.dot(x, wsh[...], preferred_element_type=F32)
    v_ref[:, inner:] = shared[:, : conv - inner].astype(BF)
    dt = shared[:, conv - inner :].astype(BF).astype(F32)
    dt_ref[...] = dt
    lim = limits(segc, segr)
    v = v_ref[...].astype(F32)
    pre = conv_pre(v, shifts(v, cm), par)
    act = pre * sigmoid(pre)
    x_act = act[:, :inner]
    nstate = (conv - inner) // 2
    b_act = act[:, inner : inner + nstate].astype(BF)
    c_act = act[:, inner + nstate :].astype(BF)
    u, delta, decay = decay_of(dt, hp)
    cum = cumulate(lim, decay)
    cum_t = [c.T for c in cum]
    hm = head_map(inner)
    xs = x_act * hdot(delta, hm, NT)
    cb = {k: bdot(c_act[span(k[0])], b_act[span(k[1])], NT) for k in lim}
    for q in range(inner // LANES):
        ql = slice(q * LANES, (q + 1) * LANES)
        pair = halves(xs[:, ql])
        for i in range(blocks):
            total = par[6:7, ql] * x_act[span(i), ql]
            for j in range(i + 1):
                for e in range(2):
                    h = 2 * q + e
                    g = jnp.exp(jnp.minimum(cum[i][:, h : h + 1] - cum_t[j][h : h + 1], lim[i, j]))
                    total = total + bdot(g * cb[i, j], pair[e][span(j)])
            y_ref[span(i), ql] = total.astype(BF)
    hooks("mixed")
    z = z_ref[...]
    prod = y_ref[...].astype(F32) * (z * sigmoid(z))
    square = jnp.sum(prod * prod, axis=1, keepdims=True)
    tokens = sq_ref.shape[1]
    for k in range(sq_ref.shape[0] // 8):
        sq_ref[8 * k : 8 * k + 8] = as_row(square[k * tokens : (k + 1) * tokens])
    sc_ref[...] = (prod * par[5:6, :inner]).astype(BF)
    hooks("gated")
    put(part_ref, jnp.dot(sc_ref[...], flat(wout), preferred_element_type=F32))


def forward_kernel(S, F, L, heads, *refs):
    take = Take(refs)
    hidden, cot, segr_ref, win_raw, wout_raw, cw, cb, ng, gg, hp_ref = take(10)
    hidden_out, gb_all, gains, par_ref, dots_all = take(5)
    per = [dict(zip(KEPT, take(len(KEPT)))) for _ in range(L)]
    stored = [take(len(STORED)) for _ in range(L)]
    small_all, full = take(2)
    parts, sq_all = take(L), take(L)
    scs = [take(N_SCATTER) for _ in range(L)]
    shared, shared32 = take(L), take()
    stores = []
    for l in range(L):
        for k, ref in zip(STORED, take(len(STORED))):
            per[l][k] = ref
        sem = take()
        stores.append(
            [
                pltpu.make_async_copy(per[l][k], stored[l][i], sem.at[i])
                for i, k in enumerate(STORED)
            ]
        )

    def sems():
        return take(2)

    s, f = lax.axis_index("seq"), lax.axis_index("fsdp")
    g_small = Gather("fsdp", F, small_all, sems())
    g_cot = Gather("seq", S, gb_all, sems())
    g_dots = Gather("seq", S, dots_all, sems())
    g_in = [
        (Line if l == 0 else Gather)("fsdp", F, per[l]["win"], sems()) for l in range(L)
    ]
    g_out = [Gather("fsdp", F, per[l]["wout"], sems()) for l in range(L)]
    g_nrm = [Gather("seq", S, per[l]["nrm"], sems()) for l in range(L)]
    g_sq = [Gather("seq", S, sq_all[l], sems()) for l in range(L)]
    g_part = [Gather("fsdp", F, shared[l].at[s], sems()) for l in range(L)]
    g_shared = [Gather("seq", S, shared[l], sems()) for l in range(L)]
    perm_send, perm_recv, perm_stay = take(3)

    flat_id = f * S + s
    own = s * F + f
    target = (flat_id // F, flat_id % F)
    source = (own % S, own // S)
    moved = flat_id != own
    ready = barrier([("fsdp", F), ("seq", S)], (source, moved))

    taps, conv_part = cw.shape[1:]
    width_part, inner_part = ng.shape[1], gg.shape[1]
    inner, convdim = inner_part * F, conv_part * F
    il, hl = inner // S, heads // S
    bc = convdim - inner

    def perm(l):
        return pltpu.make_async_remote_copy(
            src_ref=wout_raw.at[l, s],
            dst_ref=per[l]["wout"].at[flat_id % F],
            send_sem=perm_send.at[l],
            recv_sem=perm_recv.at[l],
            device_id=target,
            device_id_type=MESH,
        )

    def stay(l):
        return pltpu.make_async_copy(
            wout_raw.at[l, s], per[l]["wout"].at[f], perm_stay.at[l]
        )

    def perm_start(l):
        @pl.when(moved)
        def _():
            perm(l).start()

        @pl.when(jnp.logical_not(moved))
        def _():
            stay(l).start()

    def perm_wait(l):
        @pl.when(moved)
        def _():
            perm(l).wait()

        @pl.when(jnp.logical_not(moved))
        def _():
            stay(l).wait()

    wide = small_all.shape[2]

    def lanes(x):
        x = x.astype(F32)
        if x.shape[1] == wide:
            return x
        return jnp.concatenate([x, jnp.zeros((x.shape[0], wide - x.shape[1]), F32)], axis=1)

    rows = [lanes(cw[l]) for l in range(L)] + [lanes(cb[...]), lanes(ng[...]), lanes(gg[...])]
    count = L * (taps + 3)
    rows.append(jnp.zeros((small_all.shape[1] - count, wide), F32))
    small_all[f] = jnp.concatenate(rows, axis=0).astype(BF)

    block_rows = win_raw.shape[1]
    part_rows = block_rows // S
    high, breadth = shared[0].shape[2:]

    def block(l):
        start = pl.multiple_of(s * il, LANES)
        dst = per[l]["win"]
        dst[f, :, :il] = win_raw[l, :, pl.ds(start, il)]
        dst[f, :, il:] = win_raw[l, :, pl.ds(pl.multiple_of(inner + start, LANES), il)]

    def part(l):
        tail = win_raw[l, :, 2 * inner :].astype(F32)
        tail = jnp.concatenate(
            [tail, jnp.zeros((block_rows, breadth - tail.shape[1]), F32)], axis=1
        )
        for q in range(S):
            rows = tail[q * part_rows : (q + 1) * part_rows]
            if high > part_rows:
                rows = jnp.concatenate([rows, jnp.zeros((high - part_rows, breadth), F32)], axis=0)

            @pl.when(s == q)
            def _():
                shared[l][q, f] = rows.astype(BF)

    def assemble(l):
        for k in range(F):
            for q in range(S):
                row = k * block_rows + q * part_rows
                shared32[row : row + part_rows] = shared[l][q, k].astype(F32)[:part_rows]
        out = per[l]["wsh"]
        out[:, :bc] = shared32[:, :bc].astype(BF)
        tail = pltpu.roll(shared32[:, bc:], lax.rem(LANES - s * hl, LANES), 1)
        lane = lax.broadcasted_iota(jnp.int32, tail.shape, 1)
        out[:, bc:] = jnp.where(lane < hl, tail, 0.0).astype(BF)

    part(0)
    block(0)
    ready()
    for l in range(L):
        perm_start(l)
    g_small.start()
    g_part[0].start()
    g_in[0].start()
    for l in range(1, L):
        part(l)
        g_part[l].start()
        block(l)
    gb_all[s] = cot[...].astype(BF)
    seg = seg_parts(segr_ref)

    g_small.forwards()
    g_part[0].forwards()
    g_small.finish()
    got = [small_all[k].astype(F32) for k in range(F)]

    def joined(lo, hi, part):
        return jnp.concatenate([x[lo:hi, :part] for x in got], axis=1)

    full[: L * (taps + 1)] = joined(0, L * (taps + 1), conv_part)
    lo = L * (taps + 1)
    full[lo + L : lo + 2 * L, :inner] = joined(lo + L, lo + 2 * L, inner_part)
    gains[...] = jnp.zeros_like(gains)
    gains[:L] = joined(lo, lo + L, width_part)
    part_in = pl.ds(pl.multiple_of(s * il, LANES), il)
    hm = head_map(il)
    for l in range(L):
        par_ref[l] = jnp.zeros_like(par_ref[l])
        par_ref[l, :taps, :il] = full[l * taps : (l + 1) * taps, part_in]
        par_ref[l, :taps, il:] = full[l * taps : (l + 1) * taps, inner:convdim]
        r = L * taps + l
        par_ref[l, 4:5, :il] = full[r : r + 1, part_in]
        par_ref[l, 4:5, il:] = full[r : r + 1, inner:convdim]
        r = lo + L + l
        par_ref[l, 5:6, :il] = full[r : r + 1, part_in]
        par_ref[l, 6:7, :il] = hdot(hp_ref[l], hm, NT)[2:3]

    per[0]["nrm"][s] = norm_of(hidden[...], gains[:1]).astype(BF)
    g_nrm[0].start()
    g_part[0].finish()
    g_shared[0].start()
    for l in range(1, L):
        g_part[l].forwards()
    g_in[0].forwards()
    perm_wait(0)
    g_out[0].start()
    for l in range(1, L):
        g_in[l].start()
        perm_wait(l)
        g_out[l].start()
    g_nrm[0].forwards()
    g_shared[0].forwards()
    for l in range(1, L):
        g_part[l].finish()
        g_shared[l].start()
    g_cot.start()
    g_nrm[0].finish()
    g_shared[0].finish()
    assemble(0)
    g_in[0].finish()

    for l in range(L):
        last = l == L - 1

        def hooks(stage, l=l, last=last):
            if stage == "projected" and l == 0:
                g_out[0].forwards()
            if stage == "mixed" and not last:
                g_in[l + 1].forward(1)
                if l == 0:
                    for k in range(1, L):
                        g_shared[k].forwards()
                    g_cot.forwards()
            if stage == "gated":
                g_out[l].finish()

        o = per[l]
        mix_forward(
            seg, o["nrm"], o["win"], o["wsh"], o["wout"], par_ref[l], hp_ref[l],
            (parts[l], sq_all[l].at[s], o["z"], o["v"], o["dt"], o["y"], o["sc"]), hooks,
        )
        sc = Scatter("seq", S, parts[l], scs[l])
        sc.start()
        g_sq[l].start()
        current = hidden if l == 0 else per[l - 1]["new"]
        sc.middle()
        g_sq[l].forwards()
        g_sq[l].finish()
        if not last:
            for da in range(2, factor(F)[0]):
                g_in[l + 1].forward(da)
        tokens = hidden.shape[0]
        o["inv"][...] = lax.rsqrt(jnp.sum(sq_all[l][...], axis=0) * (1.0 / inner) + EPS)
        inv = as_col(o["inv"][pl.ds(pl.multiple_of(8 * s, 8), 8)][:1])
        delta = sc.finish() * inv
        u = current[...] + delta
        o["delta"][...] = delta
        o["new"][...] = u
        if l == 0:
            g_cot.finish()
        if last:
            hidden_out[...] = u
            dots = jnp.sum(gb_all[s].astype(F32) * delta, axis=1, keepdims=True)
            dots_all[s] = as_row(dots)
            g = g_dots
        else:
            per[l + 1]["nrm"][s] = norm_of(u, gains[l + 1 : l + 2]).astype(BF)
            g = g_nrm[l + 1]
        g.start()
        for c in stores[l]:
            c.start()
        if not last:
            g_out[l + 1].forwards()
        g.forwards()
        if not last:
            g_shared[l + 1].finish()
            assemble(l + 1)
        g.finish()
        if not last:
            g_in[l + 1].finish()
    for c in stores[L - 1]:
        c.wait()
    for l in range(L - 1):
        for c in stores[l]:
            c.wait()


KEPT = ("new", "delta", "inv")
STORED = ("win", "wsh", "wout", "nrm", "z", "v", "dt", "y", "sc")
FORWARD_OUTS = KEPT + STORED


def forward(S, F, heads, hidden, cot, segr, win_raw, wout_raw, cw, cb, ng, gg, hp):
    tokens, width = hidden.shape
    length = segr.shape[1]
    L, taps, conv_part = cw.shape
    inner, convdim = gg.shape[1] * F, conv_part * F
    il, bc = inner // S, convdim - inner
    conv = il + bc
    sem = pltpu.SemaphoreType.DMA
    rows = -(-(L * (taps + 3)) // 16) * 16
    wide = -(-max(conv_part, ng.shape[1], gg.shape[1]) // LANES) * LANES
    breadth = bc + LANES
    part_rows = -(-(win_raw.shape[1] // S) // 16) * 16
    outs = [
        sds((tokens, width), F32),
        sds((S, tokens, width), BF),
        sds((8, width), F32),
        sds((L, 8, conv), F32),
        sds((S, 8, tokens), F32),
    ]
    kept = [
        sds((tokens, width), F32),
        sds((tokens, width), F32),
        sds((S * 8, tokens), F32),
    ]
    stored = [
        sds((F, win_raw.shape[1], 2 * il), BF),
        sds((width, breadth), BF),
        sds((F,) + wout_raw.shape[2:], BF),
        sds((S, tokens, width), BF),
        sds((length, il), F32),
        sds((length, conv), BF),
        sds((length, LANES), F32),
        sds((length, il), BF),
        sds((length, il), BF),
    ]
    vmem_outs = len(outs) + L * len(kept)
    outs += kept * L + stored * L
    scratch = [pltpu.VMEM((F, rows, wide), BF), pltpu.VMEM((rows, convdim), F32)]
    scratch += [pltpu.VMEM((S, tokens, width), BF) for _ in range(L)]
    scratch += [pltpu.VMEM((S, S * 8, tokens), F32) for _ in range(L)]
    for _ in range(L):
        scratch += Scatter.scratch(S, (tokens, width))
    scratch += [pltpu.VMEM((S, F, part_rows, breadth), BF) for _ in range(L)]
    scratch += [pltpu.VMEM((width, breadth), F32)]
    for _ in range(L):
        scratch += [pltpu.VMEM(x.shape, x.dtype) for x in stored] + [sem((len(stored),))]
    for n in [F, S, S]:
        scratch += Gather.scratch(n)
    scratch += Line.scratch(F)
    for n in [F] * (2 * L - 1) + [S] * (2 * L) + [F] * L + [S] * L:
        scratch += Gather.scratch(n)
    scratch += [sem((L,)), sem((L,)), sem((L,))]
    got = comm_call(
        partial(forward_kernel, S, F, L, heads), "forward", 0, outs, scratch,
        (hidden, cot, segr, win_raw, wout_raw, cw, cb, ng, gg, hp),
        out_spaces=[pltpu.VMEM] * vmem_outs + [pl.ANY] * (len(outs) - vmem_outs),
    )
    k, n = len(kept), len(stored)
    layers = []
    for l in range(L):
        low, high = 5 + l * k, vmem_outs + l * n
        layers.append(dict(zip(FORWARD_OUTS, got[low : low + k] + got[high : high + n])))
    return got[:5], layers


def mix_backward(total_inner, seg, nrm, win, wsh, wout, par, hp, kept, gb, inv, dots, out, hooks):
    z_ref, v_ref, dt_ref, y_ref, sc_ref = kept
    gz_ref, gx_ref, gout_ref, dpart_ref, dbc_ref, ddt_ref, small_ref, dproj = out
    segc, segr, cm = seg
    inner = z_ref.shape[1]
    length, conv = v_ref.shape
    blocks = length // SPAN
    nstate = (conv - inner) // 2

    scaled_in = lax.dot_general(gb, wout[...], (NT, ((), ())), preferred_element_type=F32) * inv
    z = z_ref[...]
    y = y_ref[...].astype(F32)
    sig = sigmoid(z)
    silu = z * sig
    prod = y * silu
    small_ref[5:6, :inner] = jnp.sum(scaled_in * prod, axis=0, keepdims=True)
    d_prod = scaled_in * par[5:6, :inner] - prod * (inv * inv * dots * (1.0 / total_inner))
    dy = d_prod * silu
    dy = dy.astype(BF).astype(F32)
    dproj[:, :inner] = (d_prod * y * (sig * (1.0 + z * (1.0 - sig)))).astype(BF)
    grad_scaled = (gb.astype(F32) * inv).astype(BF)
    put(
        gout_ref,
        lax.dot_general(sc_ref[...], grad_scaled, (TN, ((), ())), preferred_element_type=F32),
    )
    put(gz_ref, bdot(nrm[...], dproj[:, :inner], TN))
    hooks("gout")

    lim = limits(segc, segr)
    v = v_ref[...].astype(F32)
    moved = shifts(v, cm)
    pre = conv_pre(v, moved, par)
    csig = sigmoid(pre)
    act = pre * csig
    x_act = act[:, :inner]
    b_act = act[:, inner : inner + nstate].astype(BF)
    c_act = act[:, inner + nstate :].astype(BF)
    u, delta, decay = decay_of(dt_ref[...], hp)
    cum = cumulate(lim, decay)
    cum_t = [c.T for c in cum]
    hm = head_map(inner)
    delta_bc = hdot(delta, hm, NT)
    xs = x_act * delta_bc
    cb = {k: bdot(c_act[span(k[0])], b_act[span(k[1])], NT) for k in lim}

    lane = lax.broadcasted_iota(jnp.int32, (SPAN, LANES), 1)
    sub = lax.broadcasted_iota(jnp.int32, (LANES, SPAN), 0)
    dcb = {k: jnp.zeros((SPAN, SPAN), F32) for k in lim}
    drow = [jnp.zeros((SPAN, LANES), F32) for _ in range(blocks)]
    dcol = [jnp.zeros((LANES, SPAN), F32) for _ in range(blocks)]
    dxs = []
    for q in range(inner // LANES):
        ql = slice(q * LANES, (q + 1) * LANES)
        pair = xs[:, ql].astype(BF)
        dyp = halves(dy[:, ql])
        dxq = [jnp.zeros((SPAN, LANES), F32) for _ in range(blocks)]
        for i in range(blocks):
            for j in range(i + 1):
                for e in range(2):
                    h = 2 * q + e
                    w = jnp.exp(jnp.minimum(cum[i][:, h : h + 1] - cum_t[j][h : h + 1], lim[i, j]))
                    p = w * cb[i, j]
                    dp = bdot(dyp[e][span(i)], pair[span(j)], NT)
                    dxq[j] = dxq[j] + bdot(p, dyp[e][span(i)], TN)
                    dcb[i, j] = dcb[i, j] + dp * w
                    g = dp * p
                    drow[i] = drow[i] + jnp.where(lane == h, jnp.sum(g, axis=1, keepdims=True), 0.0)
                    dcol[j] = dcol[j] + jnp.where(sub == h, jnp.sum(g, axis=0, keepdims=True), 0.0)
        dxs.append(jnp.concatenate(dxq, axis=0))
        hooks(f"pair{q}")
    dxs = jnp.concatenate(dxs, axis=1)
    db, dc = [], []
    for k in range(blocks):
        db.append(sum(bdot(dcb[i, k], c_act[span(i)], TN) for i in range(k, blocks)))
        dc.append(sum(bdot(dcb[k, j], b_act[span(j)]) for j in range(k + 1)))
    dcum_t = [drow[k].T - dcol[k] for k in range(blocks)]
    ddecay = []
    for j in range(blocks):
        total = None
        for i in range(j, blocks):
            term = hdot(dcum_t[i], (lim[i, j] == 0.0).astype(F32))
            total = term if total is None else total + term
        ddecay.append(total.T)
    ddecay = jnp.concatenate(ddecay, axis=0)
    ddelta = hdot(dxs * x_act, hm) - jnp.exp(hp[0:1]) * ddecay
    ddt = ddelta * sigmoid(u)
    small_ref[6:7, :LANES] = jnp.sum(ddecay * decay, axis=0, keepdims=True)
    small_ref[6:7, LANES : 2 * LANES] = jnp.sum(ddt, axis=0, keepdims=True)
    skip = jnp.broadcast_to(jnp.sum(dy * x_act, axis=0, keepdims=True), (8, inner))
    small_ref[6:7, 2 * LANES : 3 * LANES] = hdot(skip, hm)[:1]
    dx_act = dxs * delta_bc + dy * par[6:7, :inner]
    dact = jnp.concatenate(
        [dx_act, jnp.concatenate(db, axis=0), jnp.concatenate(dc, axis=0)], axis=1
    )

    dpre = dact * (csig * (1.0 + pre * (1.0 - csig)))
    small_ref[4:5, :conv] = jnp.sum(dpre, axis=0, keepdims=True)
    small_ref[3:4, :conv] = jnp.sum(dpre * v, axis=0, keepdims=True)
    dv = par[3:4] * dpre
    for d in range(1, 4):
        small_ref[3 - d : 4 - d, :conv] = jnp.sum(dpre * moved[d - 1], axis=0, keepdims=True)
        back = dpre * cm[:, d - 1 : d] * par[3 - d : 4 - d]
        dv = dv + pltpu.roll(back, length - d, 0)
    heads = inner // HEADDIM
    real = lax.broadcasted_iota(jnp.int32, (length, LANES), 1) < heads
    ddt = jnp.where(real, ddt, 0.0)
    dproj[:, inner : inner + conv] = dv.astype(BF)
    dproj[:, inner + conv :] = ddt.astype(BF)
    put(dbc_ref, dv[:, inner:].T)
    ddt_ref[...] = ddt.T[: ddt_ref.shape[0]].astype(BF)
    put(
        dpart_ref,
        bdot(dproj[:, : 2 * inner], win[...], NT) + bdot(dproj[:, 2 * inner :], wsh[...], NT),
    )
    hooks("dpart")
    put(gx_ref, bdot(nrm[...], dproj[:, inner : 2 * inner], TN))
    hooks("gin")


BACKWARD_SMALL = ("inv", "prior")
BACKWARD_INS = STORED + BACKWARD_SMALL


def backward_kernel(S, F, L, total_inner, *refs):
    take = Take(refs)
    cot, segr_ref, gb_last, dots_last, gains, par_ref, hp_ref = take(7)
    ins = [dict(zip(BACKWARD_INS, take(len(BACKWARD_INS)))) for _ in range(L)]
    deltas = take(L)
    sources = [x.copy() for x in ins]
    input_grad, small_out = take(2)
    outs = [take(4) for _ in range(L)]
    jobs = [take(4) for _ in range(L)]
    dparts, dbcs, ddts = take(L), take(L), take(L)
    gbs, dotss = take(L - 1), take(L - 1)
    dproj, small, out_mid = take(), take(), take(L)
    scat = [[Scatter("fsdp", F, jobs[l][k], take(N_SCATTER)) for k in range(4)] for l in range(L)]
    sc = [Scatter("seq", S, dparts[l], take(N_SCATTER)) for l in range(L)]
    sb = [Scatter("seq", S, dbcs[l], take(N_SCATTER)) for l in range(L)]
    g_gb = [Gather("seq", S, gbs[l], take(2)) for l in range(L - 1)]
    g_dots = [Gather("seq", S, dotss[l], take(2)) for l in range(L - 1)]
    g_job = [[Gather("seq", S, outs[l][k], take(2)) for k in range(4)] for l in range(L)]
    g_small = Gather("seq", S, small_out, take(2))
    perm_send, perm_recv = take(2)
    sm_row, sm_mid, sm_col, sm_s1, sm_r1, sm_s2, sm_r2 = take(7)
    loads = [[] for _ in range(L)]
    for l in range(L - 1):
        for k, ref in zip(STORED, take(len(STORED))):
            ins[l][k] = ref
        sem = take()
        for i, k in enumerate(STORED):
            loads[l].append(pltpu.make_async_copy(sources[l][k], ins[l][k], sem.at[i]))
    for l in range(L - 1):
        for c in loads[l]:
            c.start()

    s, f = lax.axis_index("seq"), lax.axis_index("fsdp")
    a_n, b_n = factor(F)
    a, b = f // b_n, f % b_n
    flat_id = f * S + s
    own = s * F + f
    target = (own % S, own // S)
    source = (flat_id // F, flat_id % F)
    moved = flat_id != own
    ready = barrier([("fsdp", F), ("seq", S)], (source, moved))

    def perm(l):
        return pltpu.make_async_remote_copy(
            src_ref=out_mid[l],
            dst_ref=outs[l][3].at[own % S],
            send_sem=perm_send.at[l],
            recv_sem=perm_recv.at[l],
            device_id=target,
            device_id_type=MESH,
        )

    def row(db):
        return pltpu.make_async_remote_copy(
            src_ref=small,
            dst_ref=sm_row.at[db],
            send_sem=sm_s1.at[db],
            recv_sem=sm_r1.at[db],
            device_id=(s, a * b_n + lax.rem(b + db, b_n)),
            device_id_type=MESH,
        )

    def col(da, sender=True):
        at = a if sender else lax.rem(a + a_n - da, a_n)
        return pltpu.make_async_remote_copy(
            src_ref=sm_mid,
            dst_ref=sm_col.at[at],
            send_sem=sm_s2.at[da],
            recv_sem=sm_r2.at[da],
            device_id=(s, lax.rem(a + da, a_n) * b_n + b),
            device_id_type=MESH,
        )

    def out_done(l):
        value = scat[l][3].finish().astype(BF)
        out_mid[l][...] = value

        @pl.when(moved)
        def _():
            perm(l).start()

        @pl.when(jnp.logical_not(moved))
        def _():
            outs[l][3][s] = value

    def out_gather(l):
        @pl.when(moved)
        def _():
            perm(l).wait()

        g_job[l][3].start()

    def job_done(l, k):
        outs[l][k][s] = scat[l][k].finish().astype(BF)
        g_job[l][k].start()

    seg = seg_parts(segr_ref)
    small[...] = jnp.zeros_like(small)
    pairs = ins[0]["z"].shape[1] // LANES

    for l in reversed(range(L)):
        x = ins[l]
        base = 16 * l
        if l == L - 1:
            gb_ref, dots_ref = gb_last, dots_last
        else:
            gb_ref, dots_ref = gbs[l], dotss[l]

        def hooks(stage, l=l):
            if stage == "gout":
                if l == L - 1:
                    ready()
                scat[l][3].start()
                scat[l][0].start()
                if l < L - 1:
                    out_done(l + 1)
                    scat[l + 1][1].middle()
                    scat[l + 1][2].middle()
            if stage == f"pair{pairs - 1}":
                scat[l][3].middle()
                if l < L - 1:
                    out_gather(l + 1)
                    job_done(l + 1, 0)
            if stage == "dpart":
                sb[l].start()
                sc[l].start()
            if stage == "gin":
                scat[l][1].start()

        for c in loads[l]:
            c.wait()
        inv = jnp.concatenate([as_col(x["inv"][8 * k : 8 * k + 1]) for k in range(S)], axis=0)
        dots = jnp.concatenate([as_col(dots_ref[k][:1]) for k in range(S)], axis=0)
        mix_backward(
            total_inner, seg, x["nrm"], x["win"], x["wsh"], x["wout"], par_ref[l], hp_ref[l],
            (x["z"], x["v"], x["dt"], x["y"], x["sc"]), flat(gb_ref), inv, dots,
            (jobs[l][0], jobs[l][1], jobs[l][3], dparts[l], dbcs[l], ddts[l], small.at[base : base + 8], dproj),
            hooks,
        )
        sb[l].middle()
        sc[l].middle()
        scat[l][0].middle()
        u = x["prior"][...]
        n = lax.rsqrt(jnp.mean(u * u, axis=-1, keepdims=True) + EPS)
        xhat = u * n
        tail = jnp.concatenate([sb[l].finish().astype(BF), ddts[l][...]], axis=0)
        put(
            jobs[l][2],
            lax.dot_general(
                x["nrm"][...], tail, (((0,), (1,)), ((), ())), preferred_element_type=F32
            ),
        )
        scat[l][2].start()
        dn = sc[l].finish()
        small[base + 8 : base + 9] = jnp.sum(dn * xhat, axis=0, keepdims=True)
        t = dn * gains[l : l + 1]
        g_ref = cot if l == L - 1 else input_grad
        new = g_ref[...] + n * (t - xhat * jnp.mean(t * xhat, axis=-1, keepdims=True))
        input_grad[...] = new
        if l > 0:
            gb = new.astype(BF)
            gbs[l - 1][s] = gb
            dotss[l - 1][s] = as_row(
                jnp.sum(gb.astype(F32) * deltas[l - 1][...], axis=1, keepdims=True)
            )
            for g in (g_gb[l - 1], g_dots[l - 1]):
                g.start()
            for g in (g_gb[l - 1], g_dots[l - 1]):
                g.forwards()
            for g in (g_gb[l - 1], g_dots[l - 1]):
                g.finish()

    for db in range(1, b_n):
        row(db).start()
    for l in range(1, L):
        job_done(l, 1)
        job_done(l, 2)
    out_done(0)
    job_done(0, 0)
    scat[0][1].middle()
    scat[0][2].middle()
    sm_row[0] = small[...]
    for db in range(1, b_n):
        row(db).wait_recv()
    total = None
    for k in range(b_n):
        term = sm_row[lax.rem(b + b_n - k, b_n)]
        total = term if total is None else total + term
    sm_mid[...] = total
    for da in range(1, a_n):
        col(da).start()
    for l in range(1, L):
        for g in g_job[l]:
            g.forwards()
    out_gather(0)
    g_job[0][0].forwards()
    job_done(0, 1)
    job_done(0, 2)
    sm_col[a] = sm_mid[...]
    for da in range(1, a_n):
        col(da, False).wait_recv()
    small_out[s] = jnp.sum(sm_col[...], axis=0)
    g_small.start()
    g_job[0][3].forwards()
    g_job[0][1].forwards()
    g_job[0][2].forwards()
    g_small.forwards()
    for l in range(L):
        for g in g_job[l]:
            g.finish()
    g_small.finish()
    for db in range(1, b_n):
        row(db).wait_send()
    for da in range(1, a_n):
        col(da).wait_send()


def backward(S, F, total_inner, cot, segr, gb_last, dots_last, gains, par, hp, layers, deltas):
    L = len(layers)
    tokens, width = cot.shape
    length, il = layers[0]["z"].shape
    conv = layers[0]["v"].shape[1]
    bc = conv - il
    bl = bc // S
    a_n, b_n = factor(F)
    sem = pltpu.SemaphoreType.DMA
    shapes = [(width // F, il)] * 2 + [(width // F, LANES), (il // F, width)]
    outs = [sds((tokens, width), F32), sds((S, 16 * L, width), F32)]
    for _ in range(L):
        outs += [sds((S,) + shape, BF) for shape in shapes]
    scratch = []
    for _ in range(L):
        scratch += [pltpu.VMEM((F,) + shape, BF) for shape in shapes]
    scratch += [pltpu.VMEM((S, tokens, width), BF) for _ in range(L)]
    scratch += [pltpu.VMEM((S, bl, length), BF) for _ in range(L)]
    scratch += [pltpu.VMEM((LANES - bl, length), BF) for _ in range(L)]
    scratch += [pltpu.VMEM((S, tokens, width), BF) for _ in range(L - 1)]
    scratch += [pltpu.VMEM((S, 8, tokens), F32) for _ in range(L - 1)]
    scratch += [pltpu.VMEM((length, il + conv + LANES), BF), pltpu.VMEM((16 * L, width), F32)]
    scratch += [pltpu.VMEM(shapes[3], BF) for _ in range(L)]
    for _ in range(L):
        for shape in shapes:
            scratch += Scatter.scratch(F, shape)
    for _ in range(L):
        scratch += Scatter.scratch(S, (tokens, width))
    for _ in range(L):
        scratch += Scatter.scratch(S, (bl, length))
    for _ in range(2 * (L - 1) + 4 * L + 1):
        scratch += Gather.scratch(S)
    scratch += [sem((L,)), sem((L,))]
    scratch += [
        pltpu.VMEM((b_n, 16 * L, width), F32),
        pltpu.VMEM((16 * L, width), F32),
        pltpu.VMEM((a_n, 16 * L, width), F32),
        sem((b_n,)), sem((b_n,)), sem((a_n,)), sem((a_n,)),
    ]
    for l in range(L - 1):
        scratch += [pltpu.VMEM(layers[l][k].shape, layers[l][k].dtype) for k in STORED]
        scratch += [sem((len(STORED),))]
    args = [cot, segr, gb_last, dots_last, gains, par, hp]
    spaces = [pltpu.VMEM] * len(args)
    for l, x in enumerate(layers):
        args += [x[k] for k in BACKWARD_INS]
        spaces += [pltpu.VMEM if l == L - 1 else pl.ANY] * len(STORED)
        spaces += [pltpu.VMEM] * len(BACKWARD_SMALL)
    args += deltas
    spaces += [pltpu.VMEM] * L
    return comm_call(
        partial(backward_kernel, S, F, L, total_inner), "backward", 1, outs, scratch, args,
        in_spaces=spaces,
    )


def finish_kernel(S, F, L, heads, *refs):
    take = Take(refs)
    sums = take()
    jobs = [take(4) for _ in range(L)]
    gin, gout, gcw, gcb, gng, ggg, gal, gdb, gds = take(9)
    f = lax.axis_index("fsdp")
    taps, conv_part = gcw.shape[1:]
    width_part, inner_part = gng.shape[1], ggg.shape[1]
    inner, convdim = inner_part * F, conv_part * F
    il, hl = inner // S, heads // S
    bc = convdim - inner
    bl = bc // S

    def own(x, part):
        n = x.shape[1]
        return pltpu.roll(x, lax.rem(n - f * part, n), 1)[:, :part]

    for l in range(L):
        gz, gx, tail, out = jobs[l]
        for s in range(S):
            gin[l, :, s * il : (s + 1) * il] = gz[s].astype(F32)
            gin[l, :, inner + s * il : inner + (s + 1) * il] = gx[s].astype(F32)
        tails = [tail[s].astype(F32) for s in range(S)]
        gin[l, :, 2 * inner : 2 * inner + bc] = jnp.concatenate([t[:, :bl] for t in tails], axis=1)
        gin[l, :, 2 * inner + bc :] = jnp.concatenate([t[:, bl : bl + hl] for t in tails], axis=1)
        rows = out.shape[1]
        for s in range(S):
            gout[l, s * rows : (s + 1) * rows] = out[s].astype(F32)
        base = 16 * l
        low = [sums[s, base : base + 8] for s in range(S)]
        xs = jnp.concatenate([t[:, :il] for t in low], axis=1)
        both = sum(t[:, il : il + bc] for t in low)
        five = own(jnp.concatenate([xs, both], axis=1), conv_part)
        gcw[l] = five[:taps]
        gcb[l : l + 1] = five[taps : taps + 1]
        ggg[l : l + 1] = own(xs, inner_part)[5:6]
        gng[l : l + 1] = own(sum(sums[s, base + 8 : base + 16] for s in range(S)), width_part)[:1]
        for k, ref in enumerate((gal, gdb, gds)):
            ref[l : l + 1] = jnp.concatenate(
                [t[6:7, k * LANES : k * LANES + hl] for t in low], axis=1
            )


def body(
    hidden, cotangent, segments, in_weight, out_weight, conv_weight, conv_bias,
    norm_gain, gate_gain, a_log, dt_bias, d_skip,
):
    seq_idx = lax.axis_index("seq")
    S = lax.axis_size("seq")
    F = lax.axis_size("fsdp")
    tokens, width = hidden.shape[1:]
    L = in_weight.shape[0]
    heads = a_log.shape[1]
    hl = heads // S
    inner = gate_gain.shape[1] * F
    length = segments.shape[1]

    hp = lax.dynamic_slice_in_dim(jnp.stack([a_log, dt_bias, d_skip], axis=1), seq_idx * hl, hl, 2)
    hp = jnp.pad(hp, ((0, 0), (0, 5), (0, LANES - hl)))
    wout_raw = out_weight.reshape(L, S, out_weight.shape[1] // S, width)
    hid, cot = hidden[0], cotangent[0]
    got, layers = forward(
        S, F, heads, hid, cot, segments, in_weight, wout_raw,
        conv_weight, conv_bias, norm_gain, gate_gain, hp,
    )
    hidden_out, gb_all, gains, par, dots_all = got
    deltas = [x["delta"] for x in layers]
    for l, x in enumerate(layers):
        x["prior"] = hid if l == 0 else layers[l - 1]["new"]
        x["nrm"] = x["nrm"].reshape(length, width)
        x["win"] = x["win"].reshape(width, -1)
        x["wout"] = x["wout"].reshape(-1, width)
    got = backward(S, F, inner, cot, segments, gb_all, dots_all, gains, par, hp, layers, deltas)
    outs = [
        sds(in_weight.shape, F32),
        sds(out_weight.shape, F32),
        sds(conv_weight.shape, F32),
        sds(conv_bias.shape, F32),
        sds(norm_gain.shape, F32),
        sds(gate_gain.shape, F32),
    ] + [sds(a_log.shape, F32)] * 3
    final = local_call(partial(finish_kernel, S, F, L, heads), "finish", outs, got[1:])
    return (hidden_out[None], got[0][None], *final)


def solution(mesh):
    token = P("fsdp", "seq", None)
    rows = P(None, "fsdp", None)
    split = P(None, "fsdp")
    taps = P(None, None, "fsdp")
    return jax.shard_map(
        body,
        mesh=mesh,
        in_specs=(
            token, token, P("fsdp", None), rows, rows, taps, split, split, split, P(), P(), P(),
        ),
        out_specs=(token, token, rows, rows, taps, split, split, split, P(), P(), P()),
        check_vma=False,
    )
```
